32 devices in a mesh: dp: 32 (over z, y, x, core).
Axes of the slice: x: 2, y: 2, z: 4, core: 2. Of those that a mesh axis runs over, the one named last changes fastest.
Arguments:
- frames: bfloat16 [32, 1536, 512], P('dp'), may hold values from -6 to 6
- lengths: int32 [32, 2], P('dp'), may hold values from 0 to 1536, as said below
- attn_gain: bfloat16 [512], P('dp'), may hold values from 0.5 to 1.5
- attn_shift: bfloat16 [512], P('dp'), may hold values from -1.1953125 to 1.1953125
- query_weight: bfloat16 [512, 512], P(None, 'dp'), may hold values from -0.25 to 0.25
- query_bias: bfloat16 [512], P('dp'), may hold values from -1.1953125 to 1.1953125
- key_weight: bfloat16 [512, 512], P(None, 'dp'), may hold values from -0.25 to 0.25
- value_weight: bfloat16 [512, 512], P(None, 'dp'), may hold values from -0.25 to 0.25
- value_bias: bfloat16 [512], P('dp'), may hold values from -0.1796875 to 0.1796875
- out_weight: bfloat16 [512, 512], P(None, 'dp'), may hold values from -2.5 to 2.5
- out_bias: bfloat16 [512], P('dp'), may hold values from -1.1953125 to 1.1953125
- mlp_gain: bfloat16 [512], P('dp'), may hold values from 0.5 to 1.5
- mlp_shift: bfloat16 [512], P('dp'), may hold values from -1.1953125 to 1.1953125
- up_weight: bfloat16 [512, 2048], P(None, 'dp'), may hold values from -0.25 to 0.25
- up_bias: bfloat16 [2048], P('dp'), may hold values from -1.1953125 to 1.1953125
- down_weight: bfloat16 [2048, 512], P(None, 'dp'), may hold values from -0.125 to 0.125
- down_bias: bfloat16 [512], P('dp'), may hold values from -1.1953125 to 1.1953125
- grad_out: bfloat16 [32, 1536, 512], P('dp'), may hold values from -6 to 6
Outputs:
- layer_out: bfloat16 [32, 1536, 512], P('dp')
- grad_frames: bfloat16 [32, 1536, 512], P('dp')
- grad_attn_gain: float32 [512], P('dp')
- grad_attn_shift: float32 [512], P('dp')
- grad_query_weight: float32 [512, 512], P(None, 'dp')
- grad_query_bias: float32 [512], P('dp')
- grad_key_weight: float32 [512, 512], P(None, 'dp')
- grad_value_weight: float32 [512, 512], P(None, 'dp')
- grad_value_bias: float32 [512], P('dp')
- grad_out_weight: float32 [512, 512], P(None, 'dp')
- grad_out_bias: float32 [512], P('dp')
- grad_mlp_gain: float32 [512], P('dp')
- grad_mlp_shift: float32 [512], P('dp')
- grad_up_weight: float32 [512, 2048], P(None, 'dp')
- grad_up_bias: float32 [2048], P('dp')
- grad_down_weight: float32 [2048, 512], P(None, 'dp')
- grad_down_bias: float32 [512], P('dp')
The draws below stay inside these ranges and needn't reach their ends.
Inputs may be any that keep to these rules, and one draw needn't show every extreme that they name: lengths[w, 0] is 1 or more and reaches 1536 in some slot; lengths[w, 1] is at most 1536 - lengths[w, 0]; frames past their sum are padding.
All inputs are finite; a program needn't handle non-finite values.
Results may differ from the reference program's by a relative error of at most 0.014.
Values may be sent and summed in bfloat16 or wider, within the bound.
A program may use at most 128 MiB of HBM per device.

```python
import math
import jax
import jax.numpy as jnp
from jax import lax

D = 512
HEADS = 8
HEAD = 64
FF = 2048
FRAMES = 1536
WINDOWS = 32


def draw_lengths(key, part):
    first_key, pick_key, second_key = jax.random.split(key, 3)
    lowest = max(FRAMES // 16, 1)
    samples = jax.random.randint(first_key, (3, WINDOWS), lowest, FRAMES + 1)
    leading = jnp.min(samples, axis=0)
    longest = jax.random.randint(pick_key, (), 0, WINDOWS)
    leading = jnp.where(jnp.arange(WINDOWS) == longest, FRAMES, leading)
    spare_draw = jax.random.randint(second_key, (WINDOWS,), 0, FRAMES + 1)
    second = spare_draw % (FRAMES - leading + 1)
    second = jnp.where(2 * leading <= FRAMES, second, 0)
    return jnp.stack([leading, second], axis=1).astype(jnp.int32)


def spiked(drawn, own_key, source, target, shards_of, factor):
    def block_of(dim):
        return (jnp.arange(drawn.shape[dim]) // (drawn.shape[dim] // shards_of)).reshape((-1,) + (1,) * (drawn.ndim - 1 - dim))

    near = jax.random.permutation(own_key, shards_of)[block_of(target)]
    far = (block_of(target) + shards_of // 2) % shards_of
    return jnp.where((block_of(source) == near) | (block_of(source) == far), factor * drawn, drawn)


def steps_of(stream_key, dims, pieces, low, high):
    factor_of = 1.0
    for dim, parts in pieces:
        steps = jax.random.uniform(jax.random.fold_in(jax.random.fold_in(stream_key, 6), dim), (parts,), jnp.float32, low / len(pieces), high / len(pieces))
        factor_of = factor_of * jnp.repeat(jnp.exp(steps), dims[dim] // parts).reshape((-1,) + (1,) * (len(dims) - 1 - dim))
    return factor_of


def gaussian(own_key, dims, scale, reach, pieces=(), kind=jnp.bfloat16):
    drawn = jax.random.normal(own_key, dims, jnp.float32) * scale
    if len(pieces) > 0:
        drawn = steps_of(own_key, dims, pieces, -0.22, 0.18) * drawn
    return jnp.clip(drawn, min=-reach, max=reach).astype(kind)


def noise_with(stream_key, shape, scale, bound, shards, heavy, kind=jnp.bfloat16):
    entries = scale * jax.random.normal(stream_key, shape, jnp.float32)
    if shards:
        entries = entries * steps_of(stream_key, shape, shards, -0.22, 0.18)
    return jnp.clip(spiked(entries, jax.random.fold_in(stream_key, 3), *heavy), -bound, bound).astype(kind)


def setup_inputs(seed: int = 0) -> dict:
    keys = jax.random.split(jax.random.key(seed), 19)
    frames = gaussian(keys[0], (WINDOWS, FRAMES, D), 1.0, 6.0, ((0, 32),))
    lengths = draw_lengths(jax.random.fold_in(keys[18], 71), 0)
    attn_gain = jnp.clip(1.0 + 0.1 * jax.random.normal(keys[2], (D,), jnp.float32), 0.5, 1.5).astype(jnp.bfloat16)
    attn_shift = gaussian(keys[3], (D,), 0.2, 1.1953125, ((0, 32),))
    query_weight = gaussian(keys[4], (D, D), D ** -0.5, 0.25, ((1, 32),))
    query_bias = gaussian(keys[5], (D,), 0.2, 1.1953125, ((0, 32),))
    key_weight = gaussian(keys[6], (D, D), D ** -0.5, 0.25, ((1, 32),))
    value_weight = gaussian(keys[7], (D, D), D ** -0.5, 0.25, ((1, 32),))
    value_bias = gaussian(keys[8], (D,), 0.03, 0.1796875, ((0, 32),))
    out_weight = gaussian(keys[9], (D, D), (D * 16 // FRAMES) ** -0.5, 2.5, ((1, 32),))
    out_bias = gaussian(keys[10], (D,), 0.2, 1.1953125, ((0, 32),))
    mlp_gain = jnp.clip(1.0 + 0.1 * jax.random.normal(keys[11], (D,), jnp.float32), 0.5, 1.5).astype(jnp.bfloat16)
    mlp_shift = gaussian(keys[12], (D,), 0.2, 1.1953125, ((0, 32),))
    up_weight = gaussian(keys[13], (D, FF), D ** -0.5, 0.25, ((1, 32),))
    up_bias = gaussian(keys[14], (FF,), 0.2, 1.1953125, ((0, 32),))
    down_weight = gaussian(keys[15], (FF, D), FF ** -0.5, 0.125, ((1, 32),))
    down_bias = gaussian(keys[16], (D,), 0.2, 1.1953125, ((0, 32),))
    grad_out = noise_with(keys[17], (WINDOWS, FRAMES, D), 1.0, 6.0, ((0, 32),), (0, 2, 32, 2.75))
    return dict(frames=frames, lengths=lengths, attn_gain=attn_gain, attn_shift=attn_shift, query_weight=query_weight, query_bias=query_bias, key_weight=key_weight, value_weight=value_weight, value_bias=value_bias, out_weight=out_weight, out_bias=out_bias, mlp_gain=mlp_gain, mlp_shift=mlp_shift, up_weight=up_weight, up_bias=up_bias, down_weight=down_weight, down_bias=down_bias, grad_out=grad_out)


@jax.custom_vjp
def low(v):
    return lax.optimization_barrier(v.astype(jnp.bfloat16)).astype(jnp.float32)

@jax.custom_vjp
def low_back(v):
    return v

def low_keep(v):
    return (low(v), None)

def low_pass(kept, grad):
    return (grad,)

def back_keep(v):
    return (v, None)

def back_low(kept, grad):
    return (low(grad),)
low.defvjp(low_keep, low_pass)
low_back.defvjp(back_keep, back_low)
highest = lax.Precision.HIGHEST
epsilon = 1e-05

def matmul_high(left, right):
    return jnp.dot(left, right, precision=highest, preferred_element_type=jnp.float32)

def normalize(inputs, norm_gain, norm_shift):
    row_mean = lax.optimization_barrier(jnp.mean(inputs, axis=-1, keepdims=True))
    centered = inputs - row_mean
    variance = lax.optimization_barrier(jnp.mean(centered * centered, axis=-1, keepdims=True))
    return centered * lax.rsqrt(variance + epsilon) * norm_gain + norm_shift

def segment_of(length_pair):
    position = jnp.arange(FRAMES, dtype=jnp.int32)
    leading = length_pair[0]
    finish = length_pair[0] + length_pair[1]
    segment = jnp.where(position < leading, 0, jnp.where(position < finish, 1, 2)).astype(jnp.int32)
    return (segment, position < finish)

def attend_block(query_block, segment_block, key_heads, value_heads, segment):
    scores = jnp.einsum('bhe,khe->hbk', query_block, key_heads, precision=highest, preferred_element_type=jnp.float32) * (1.0 / math.sqrt(HEAD))
    scores = low_back(scores)
    allowed = segment_block[:, None] == segment[None, :]
    scores = jnp.where(allowed[None, :, :], scores, -1e+30)
    row_max = lax.optimization_barrier(jnp.max(scores, axis=-1, keepdims=True))
    raised = jnp.exp(scores - row_max)
    weights = raised / lax.optimization_barrier(jnp.sum(raised, axis=-1, keepdims=True))
    weights = low(weights)
    return jnp.einsum('hbk,khe->bhe', weights, value_heads, precision=highest, preferred_element_type=jnp.float32)

def window_layer(window, length_pair, params):
    attn_gain, attn_shift, query_weight, query_bias, key_weight, value_weight, value_bias, out_weight, out_bias, mlp_gain, mlp_shift, up_weight, up_bias, down_weight, down_bias = params
    segment, valid = segment_of(length_pair)
    normed_attn = low(normalize(window, attn_gain, attn_shift))
    queries = low(low_back(matmul_high(normed_attn, query_weight) + query_bias))
    key_rows = low(low_back(matmul_high(normed_attn, key_weight)))
    value_rows = low(low_back(matmul_high(normed_attn, value_weight) + value_bias))
    block_rows = min(512, FRAMES)
    block_count = FRAMES // block_rows
    query_blocks = queries.reshape(block_count, block_rows, HEADS, HEAD)
    segment_blocks = segment.reshape(block_count, block_rows)
    key_heads = key_rows.reshape(FRAMES, HEADS, HEAD)
    value_heads = value_rows.reshape(FRAMES, HEADS, HEAD)
    checked = jax.checkpoint(attend_block)
    mixed = lax.map(lambda element: checked(element[0], element[1], key_heads, value_heads, segment), (query_blocks, segment_blocks))
    mixed = low(low_back(mixed.reshape(FRAMES, D)))
    branch = low_back(matmul_high(mixed, out_weight) + out_bias)
    middle = window + branch
    normed_mlp = low(normalize(middle, mlp_gain, mlp_shift))
    up_proj = low_back(matmul_high(normed_mlp, up_weight) + up_bias)
    activation = low(jax.nn.gelu(up_proj, approximate=False))
    down_proj = low_back(matmul_high(activation, down_weight) + down_bias)
    return jnp.where(valid[:, None], middle + down_proj, 0.0)

def reference(frames, lengths, attn_gain, attn_shift, query_weight, query_bias, key_weight, value_weight, value_bias, out_weight, out_bias, mlp_gain, mlp_shift, up_weight, up_bias, down_weight, down_bias, grad_out):
    params = tuple((item.astype(jnp.float32) for item in (attn_gain, attn_shift, query_weight, query_bias, key_weight, value_weight, value_bias, out_weight, out_bias, mlp_gain, mlp_shift, up_weight, up_bias, down_weight, down_bias)))
    inputs = frames.astype(jnp.float32)
    checked_layer = jax.checkpoint(window_layer)

    def forward(inputs, params):

        def scan_step(carry, element):
            return (carry, checked_layer(element[0], element[1], params))
        unused, results = lax.scan(scan_step, jnp.zeros((), jnp.float32), (inputs, lengths))
        return results
    results, pullback = jax.vjp(forward, inputs, params)
    grad_inputs, grad_params = pullback(grad_out.astype(jnp.float32))
    return (results.astype(jnp.bfloat16), grad_inputs.astype(jnp.bfloat16), grad_params[0], grad_params[1], grad_params[2], grad_params[3], grad_params[4], grad_params[5], grad_params[6], grad_params[7], grad_params[8], grad_params[9], grad_params[10], grad_params[11], grad_params[12], grad_params[13], grad_params[14])
```

```python
import functools
import math

import jax
import jax.numpy as jnp
from jax import lax
from jax.experimental import pallas as pl
from jax.experimental.pallas import tpu as pltpu
from jax.sharding import PartitionSpec as P

HEADS = 8
EPS = 1e-05
MESH = pl.DeviceIdType.MESH
F32 = jnp.float32
BF = jnp.bfloat16
VMEM_SPEC = pl.BlockSpec(memory_space=pltpu.VMEM)
SMEM_SPEC = pl.BlockSpec(memory_space=pltpu.SMEM)
HBM_SPEC = pl.BlockSpec(memory_space=pl.ANY)
EXCLUDED = -1e30
VMEM_LIMIT = 62 << 20


def dot_nn(a, b):
    return lax.dot_general(a, b, (((1,), (0,)), ((), ())), preferred_element_type=F32)


def dot_nt(a, b):
    return lax.dot_general(a, b, (((1,), (1,)), ((), ())), preferred_element_type=F32)


def dot_tn(a, b):
    return lax.dot_general(a, b, (((0,), (0,)), ((), ())), preferred_element_type=F32)


def levels_of(n):
    rest = n // 2
    bits = rest.bit_length() - 1
    near = 2 ** ((bits + 1) // 2)
    return rest // near, near


def rows(start, size):
    return pl.ds(pl.multiple_of(start, size), size)


def normal_stats(block):
    mean = jnp.mean(block, axis=-1, keepdims=True)
    centered = block - mean
    inv = lax.rsqrt(jnp.mean(centered * centered, axis=-1, keepdims=True) + EPS)
    return centered * inv, inv


def everyone_barrier(n, me, far, near):
    barrier = pltpu.get_barrier_semaphore()
    core = lax.rem(me, 2)
    mid = lax.rem(me // 2, near)
    top = me // (2 * near)
    peers = [(lax.rem(top + k, far) * near + mid) * 2 + core for k in range(1, far)]
    peers += [(top * near + lax.rem(mid + k, near)) * 2 + core for k in range(1, near)]
    peers += [(top * near + mid) * 2 + 1 - core]
    for peer in peers:
        pl.semaphore_signal(barrier, inc=1, device_id=(peer,), device_id_type=MESH)
    pl.semaphore_wait(barrier, len(peers))
    return top, mid, core


def gather_kernel(n, count, *refs):
    shards, outs = refs[:count], refs[count : 2 * count]
    own_sem, far_s, far_r, near_s, near_r, core_s, core_r = refs[2 * count :]
    far, near = levels_of(n)
    me = lax.axis_index("dp")
    top, mid, core = everyone_barrier(n, me, far, near)

    def index(t, m, c):
        return (t * near + m) * 2 + c

    far_copies, near_copies = {}, {}
    for a in range(count):
        for k in range(1, far):
            copy = pltpu.make_async_remote_copy(
                src_ref=shards[a],
                dst_ref=outs[a].at[top, mid, core],
                send_sem=far_s.at[a, k - 1],
                recv_sem=far_r.at[a, k - 1],
                device_id=(index(lax.rem(top + k, far), mid, core),),
                device_id_type=MESH,
            )
            copy.start()
            far_copies[a, k] = copy
        pltpu.make_async_copy(shards[a], outs[a].at[top, mid, core], own_sem.at[a]).start()
    for a in range(count):
        pltpu.make_async_copy(shards[a], outs[a].at[top, mid, core], own_sem.at[a]).wait()
        for k in range(1, far):
            far_copies[a, k].wait_recv()
        for k in range(1, near):
            copy = pltpu.make_async_remote_copy(
                src_ref=outs[a].at[:, mid, core],
                dst_ref=outs[a].at[:, mid, core],
                send_sem=near_s.at[a, k - 1],
                recv_sem=near_r.at[a, k - 1],
                device_id=(index(top, lax.rem(mid + k, near), core),),
                device_id_type=MESH,
            )
            copy.start()
            near_copies[a, k] = copy
    core_copies = []
    for a in range(count):
        for k in range(1, near):
            near_copies[a, k].wait_recv()
        copy = pltpu.make_async_remote_copy(
            src_ref=outs[a].at[:, :, core],
            dst_ref=outs[a].at[:, :, core],
            send_sem=core_s.at[a],
            recv_sem=core_r.at[a],
            device_id=(index(top, mid, 1 - core),),
            device_id_type=MESH,
        )
        copy.start()
        core_copies.append(copy)
    for a in range(count):
        core_copies[a].wait_recv()
    for a in range(count):
        for k in range(1, far):
            far_copies[a, k].wait_send()
        for k in range(1, near):
            near_copies[a, k].wait_send()
        core_copies[a].wait_send()


def gather_all(n, shards):
    far, near = levels_of(n)
    count = len(shards)
    return pl.pallas_call(
        functools.partial(gather_kernel, n, count),
        out_shape=[jax.ShapeDtypeStruct((far, near, 2) + s.shape, s.dtype) for s in shards],
        in_specs=[VMEM_SPEC] * count,
        out_specs=[HBM_SPEC] * count,
        scratch_shapes=[
            pltpu.SemaphoreType.DMA((count,)),
            pltpu.SemaphoreType.DMA((count, far - 1)),
            pltpu.SemaphoreType.DMA((count, far - 1)),
            pltpu.SemaphoreType.DMA((count, near - 1)),
            pltpu.SemaphoreType.DMA((count, near - 1)),
            pltpu.SemaphoreType.DMA((count,)),
            pltpu.SemaphoreType.DMA((count,)),
        ],
        compiler_params=pltpu.CompilerParams(
            collective_id=0, has_side_effects=True, vmem_limit_bytes=32 << 20
        ),
        name="gather_params",
    )(*shards)


def scatter_kernel(n, count, *refs):
    parts, outs = refs[:count], refs[count : 2 * count]
    pos = 2 * count
    core_in, core_sum = refs[pos : pos + count], refs[pos + count : pos + 2 * count]
    pos += 2 * count
    near_in, near_sum = refs[pos : pos + count], refs[pos + count : pos + 2 * count]
    pos += 2 * count
    far_in = refs[pos : pos + count]
    core_s, core_r, near_s, near_r, far_s, far_r = refs[pos + count :]
    far, near = levels_of(n)
    me = lax.axis_index("dp")
    top, mid, core = everyone_barrier(n, me, far, near)

    def index(t, m, c):
        return (t * near + m) * 2 + c

    core_copies, near_copies, far_copies = [], {}, {}
    for a in range(count):
        copy = pltpu.make_async_remote_copy(
            src_ref=parts[a].at[:, :, 1 - core],
            dst_ref=core_in[a],
            send_sem=core_s.at[a],
            recv_sem=core_r.at[a],
            device_id=(index(top, mid, 1 - core),),
            device_id_type=MESH,
        )
        copy.start()
        core_copies.append(copy)
    for a in range(count):
        core_copies[a].wait_recv()

        def add_core(i, carry, a=a):
            f, m = i // near, lax.rem(i, near)
            core_sum[a][m, f] = (
                parts[a][f, m, core].astype(F32) + core_in[a][f, m].astype(F32)
            ).astype(BF)
            return carry

        lax.fori_loop(0, far * near, add_core, 0)
        for k in range(1, near):
            peer = lax.rem(mid + k, near)
            copy = pltpu.make_async_remote_copy(
                src_ref=core_sum[a].at[peer],
                dst_ref=near_in[a].at[k - 1],
                send_sem=near_s.at[a, k - 1],
                recv_sem=near_r.at[a, k - 1],
                device_id=(index(top, peer, core),),
                device_id_type=MESH,
            )
            copy.start()
            near_copies[a, k] = copy
    for a in range(count):
        for k in range(1, near):
            near_copies[a, k].wait_recv()

        def add_near(f, carry, a=a):
            total = core_sum[a][mid, f].astype(F32)
            for k in range(near - 1):
                total = total + near_in[a][k, f].astype(F32)
            near_sum[a][f] = total.astype(BF)
            return carry

        lax.fori_loop(0, far, add_near, 0)
        for k in range(1, far):
            peer = lax.rem(top + k, far)
            copy = pltpu.make_async_remote_copy(
                src_ref=near_sum[a].at[peer],
                dst_ref=far_in[a].at[k - 1],
                send_sem=far_s.at[a, k - 1],
                recv_sem=far_r.at[a, k - 1],
                device_id=(index(peer, mid, core),),
                device_id_type=MESH,
            )
            copy.start()
            far_copies[a, k] = copy
    for a in range(count):
        for k in range(1, far):
            far_copies[a, k].wait_recv()
        total = near_sum[a][top].astype(F32)
        for k in range(far - 1):
            total = total + far_in[a][k].astype(F32)
        outs[a][...] = total
    for a in range(count):
        core_copies[a].wait_send()
        for k in range(1, near):
            near_copies[a, k].wait_send()
        for k in range(1, far):
            far_copies[a, k].wait_send()


def scatter_all(n, parts):
    far, near = levels_of(n)
    count = len(parts)
    blocks = [p.shape[3:] for p in parts]
    return pl.pallas_call(
        functools.partial(scatter_kernel, n, count),
        out_shape=[jax.ShapeDtypeStruct(b, F32) for b in blocks],
        in_specs=[VMEM_SPEC] * count,
        out_specs=[VMEM_SPEC] * count,
        scratch_shapes=[pltpu.VMEM((far, near) + b, BF) for b in blocks]
        + [pltpu.VMEM((near, far) + b, BF) for b in blocks]
        + [pltpu.VMEM((near - 1, far) + b, BF) for b in blocks]
        + [pltpu.VMEM((far,) + b, BF) for b in blocks]
        + [pltpu.VMEM((far - 1,) + b, BF) for b in blocks]
        + [
            pltpu.SemaphoreType.DMA((count,)),
            pltpu.SemaphoreType.DMA((count,)),
            pltpu.SemaphoreType.DMA((count, near - 1)),
            pltpu.SemaphoreType.DMA((count, near - 1)),
            pltpu.SemaphoreType.DMA((count, far - 1)),
            pltpu.SemaphoreType.DMA((count, far - 1)),
        ],
        compiler_params=pltpu.CompilerParams(
            collective_id=1, has_side_effects=True, vmem_limit_bytes=VMEM_LIMIT
        ),
        name="scatter_grads",
    )(*parts)


def segment_lanes(lengths, position, lane):
    leading = lengths[0, 0]
    finish = leading + lengths[0, 1]
    segment = jnp.where(position < leading, 0, jnp.where(position < finish, 1, 2))
    return lax.rem(lane, 64) == segment


def three_pieces(column):
    high = column.astype(BF)
    rest = column - high.astype(F32)
    middle = rest.astype(BF)
    return high, middle, (rest - middle.astype(F32)).astype(BF)


def own_lanes(lane, half):
    return (lane < 64) if half == 0 else (lane >= 64)


def attend_kernel(
    lengths, x, wq, wk, wv, wo, vec, nb, qaug, kk, vv, mixed, middle, kaug, qbuf, *, tb, lb
):
    frame_count = x.shape[0]
    lane = lax.broadcasted_iota(jnp.int32, (1, 128), 1)
    table = vec[...].astype(F32).T
    gain, shift, bq, bv, bo = (table[i : i + 1] for i in range(5))

    def project(i, carry):
        r = rows(i * lb, lb)
        xhat, _ = normal_stats(x[r, :].astype(F32))
        normed = (xhat * gain + shift).astype(BF)
        nb[r, :] = normed
        qbuf[r, :] = ((dot_nt(normed, wq[...]) + bq).astype(BF).astype(F32) * 0.125).astype(BF)
        kk[r, :] = dot_nt(normed, wk[...]).astype(BF)
        vv[r, :] = (dot_nt(normed, wv[...]) + bv).astype(BF)
        position = lax.broadcasted_iota(jnp.int32, (lb, 128), 0) + i * lb
        lanes = lax.broadcasted_iota(jnp.int32, (lb, 128), 1)
        same = segment_lanes(lengths, position, lanes)
        slot = lax.rem(lanes, 64)
        kaug[r, :] = jnp.where(
            slot < 3, jnp.where(same, 0.0, EXCLUDED), jnp.where(slot < 6, 1.0, 0.0)
        ).astype(BF)
        return carry

    lax.fori_loop(0, frame_count // lb, project, 0)

    def pair_step(p, carry):
        cols = rows(p * 128, 128)
        for half in range(2):
            own = own_lanes(lane, half)
            base = 64 - 64 * half
            key = jnp.where(own, kk[:, cols], kaug[...])
            value = jnp.where(own, vv[:, cols], jnp.ones((1, 128), BF))
            head = pl.multiple_of((2 * p + half) * 128, 128)

            def block(i, inner, half=half, own=own, base=base, key=key, value=value, head=head):
                r = rows(i * tb, tb)
                position = lax.broadcasted_iota(jnp.int32, (tb, 128), 0) + i * tb
                lanes = lax.broadcasted_iota(jnp.int32, (tb, 128), 1)
                mark = jnp.where(segment_lanes(lengths, position, lanes), 1.0, 0.0).astype(BF)
                query = jnp.where(own, qbuf[r, cols], mark)
                scores = dot_nt(query, key)
                top = jnp.max(scores, axis=1, keepdims=True)
                raised = jnp.exp(scores - top).astype(BF)
                got = dot_nn(raised, value)
                total = got[:, base : base + 1]
                got = (got * (1.0 / total)).astype(BF)
                if half == 0:
                    mixed[r, cols] = got
                else:
                    mixed[r, cols] = jnp.where(own, got, mixed[r, cols])
                high, mid, low = three_pieces(-(top + jnp.log(total)))
                query = jnp.where(lane == base + 3, high, query)
                query = jnp.where(lane == base + 4, mid, query)
                qaug[r, pl.ds(head, 128)] = jnp.where(lane == base + 5, low, query)
                return inner

            lax.fori_loop(0, frame_count // tb, block, 0, unroll=True)
        return carry

    lax.fori_loop(0, HEADS // 2, pair_step, 0)

    def finish(i, carry):
        r = rows(i * lb, lb)
        middle[r, :] = x[r, :].astype(F32) + (dot_nt(mixed[r, :], wo[...]) + bo)
        return carry

    lax.fori_loop(0, frame_count // lb, finish, 0)


def attend(lengths, x, wq, wk, wv, wo, vec):
    frame_count, width = x.shape
    low = jax.ShapeDtypeStruct((frame_count, width), BF)
    return pl.pallas_call(
        functools.partial(attend_kernel, tb=512, lb=512),
        out_shape=[
            low,
            jax.ShapeDtypeStruct((frame_count, HEADS * 128), BF),
            low,
            low,
            low,
            jax.ShapeDtypeStruct((frame_count, width), F32),
            jax.ShapeDtypeStruct((frame_count, 128), BF),
        ],
        in_specs=[SMEM_SPEC] + [VMEM_SPEC] * 6,
        out_specs=[VMEM_SPEC] * 7,
        scratch_shapes=[pltpu.VMEM((frame_count, width), BF)],
        compiler_params=pltpu.CompilerParams(vmem_limit_bytes=VMEM_LIMIT),
        name="attend_forward",
    )(lengths, x, wq, wk, wv, wo, vec)


def feed_kernel(
    lengths,
    middle,
    gout,
    mixed,
    wup,
    wdn,
    wo,
    vec,
    bup,
    layer_out,
    gmid,
    dmixed,
    dwo,
    dwup,
    dwdn,
    sums,
    sum_up,
    nb,
    act,
    gup,
    glow,
    gbl,
    *,
    tb,
):
    frame_count = middle.shape[0]
    finish = lengths[0, 0] + lengths[0, 1]
    table = vec[...].astype(F32).T
    gain, shift, bdn = (table[i : i + 1] for i in range(5, 8))
    sums[...] = jnp.zeros_like(sums)
    sum_up[...] = jnp.zeros_like(sum_up)

    def block(i, carry):
        r = rows(i * tb, tb)
        valid = lax.broadcasted_iota(jnp.int32, (tb, 1), 0) + i * tb < finish
        mid = middle[r, :]
        xhat, inv = normal_stats(mid)
        normed = (xhat * gain + shift).astype(BF)
        nb[r, :] = normed
        up = dot_nt(normed, wup[...]) + bup[...].astype(F32)
        cdf = 0.5 * (1.0 + lax.erf(up * (1.0 / math.sqrt(2.0))))
        low = (up * cdf).astype(BF)
        act[r, :] = low
        down = dot_nt(low, wdn[...]) + bdn
        layer_out[r, :] = jnp.where(valid, mid + down, 0.0).astype(BF)
        grow = jnp.where(valid, gout[r, :].astype(F32), 0.0)
        gl = grow.astype(BF)
        glow[r, :] = gl
        slope = cdf + up * jnp.exp(-0.5 * up * up) * (1.0 / math.sqrt(2.0 * math.pi))
        gu = (dot_nn(gl, wdn[...]) * slope).astype(BF)
        gup[r, :] = gu
        gn = dot_nn(gu, wup[...])
        scaled = gn * gain
        gm = grow + inv * (
            scaled
            - jnp.mean(scaled, axis=-1, keepdims=True)
            - xhat * jnp.mean(scaled * xhat, axis=-1, keepdims=True)
        )
        gmid[r, :] = gm
        gb = gm.astype(BF)
        gbl[r, :] = gb
        dmixed[r, :] = dot_nn(gb, wo[...]).astype(BF)
        sums[0:1, :] += jnp.sum(gb.astype(F32), axis=0, keepdims=True)
        sums[1:2, :] += jnp.sum(gn * xhat, axis=0, keepdims=True)
        sums[2:3, :] += jnp.sum(gn, axis=0, keepdims=True)
        sums[3:4, :] += jnp.sum(grow, axis=0, keepdims=True)
        sum_up[0:1, :] += jnp.sum(gu.astype(F32), axis=0, keepdims=True)
        return carry

    lax.fori_loop(0, frame_count // tb, block, 0)
    dwo[...] = dot_tn(gbl[...], mixed[...]).astype(BF)

    def weights(i, carry):
        c = rows(i * 512, 512)
        dwup[c, :] = dot_tn(gup[:, c], nb[...]).astype(BF)
        dwdn[:, c] = dot_tn(glow[...], act[:, c]).astype(BF)
        return carry

    lax.fori_loop(0, wup.shape[0] // 512, weights, 0)


def feed(lengths, middle, gout, mixed, wup, wdn, wo, vec, bup):
    frame_count, width = middle.shape
    hidden = wup.shape[0]
    low = jax.ShapeDtypeStruct((frame_count, width), BF)
    return pl.pallas_call(
        functools.partial(feed_kernel, tb=256),
        out_shape=[
            low,
            jax.ShapeDtypeStruct((frame_count, width), F32),
            low,
            jax.ShapeDtypeStruct((width, width), BF),
            jax.ShapeDtypeStruct((hidden, width), BF),
            jax.ShapeDtypeStruct((width, hidden), BF),
            jax.ShapeDtypeStruct((8, width), F32),
            jax.ShapeDtypeStruct((8, hidden), F32),
        ],
        in_specs=[SMEM_SPEC] + [VMEM_SPEC] * 8,
        out_specs=[VMEM_SPEC] * 8,
        scratch_shapes=[
            pltpu.VMEM((frame_count, width), BF),
            pltpu.VMEM((frame_count, hidden), BF),
            pltpu.VMEM((frame_count, hidden), BF),
            pltpu.VMEM((frame_count, width), BF),
            pltpu.VMEM((frame_count, width), BF),
        ],
        compiler_params=pltpu.CompilerParams(vmem_limit_bytes=VMEM_LIMIT),
        name="feed_forward_both",
    )(lengths, middle, gout, mixed, wup, wdn, wo, vec, bup)


def attend_back_kernel(
    x,
    gmid,
    nb,
    qaug,
    kk,
    vv,
    mixed,
    dmixed,
    kaug,
    wq,
    wk,
    wv,
    vec,
    grad_x,
    dwq,
    dwk,
    dwv,
    sums,
    dq,
    dqb,
    dkt,
    dvt,
    *,
    ub,
    lb,
):
    frame_count = x.shape[0]
    lane = lax.broadcasted_iota(jnp.int32, (1, 128), 1)
    gain = vec[...].astype(F32).T[0:1]

    def pair_step(p, carry):
        cols = rows(p * 128, 128)
        grad_pair = dmixed[:, cols]
        product = grad_pair.astype(F32) * mixed[:, cols].astype(F32)
        for half in range(2):
            own = own_lanes(lane, half)
            base = 64 - 64 * half
            delta = jnp.sum(jnp.where(own, product, 0.0), axis=1, keepdims=True)
            high, mid, low = three_pieces(-delta)
            grad = jnp.where(own, grad_pair, jnp.zeros((1, 128), BF))
            grad = jnp.where(lane == base + 3, high, grad)
            grad = jnp.where(lane == base + 4, mid, grad)
            grad = jnp.where(lane == base + 5, low, grad)
            query = qaug[:, pl.ds(pl.multiple_of((2 * p + half) * 128, 128), 128)]
            here = pl.ds(pl.multiple_of(p * 128 + 64 * half, 64), 64)
            part = slice(64 * half, 64 * half + 64)
            ones = jnp.where(
                (lane >= base + 3) & (lane < base + 6), jnp.ones((1, 128), F32), 0.0
            ).astype(BF)

            def block(i, inner):
                r = rows(i * ub, ub)
                key = jnp.where(own, kk[r, cols], kaug[r, :])
                value = jnp.where(own, vv[r, cols], ones)
                probs = jnp.exp(dot_nt(query, key))
                low_probs = probs.astype(BF)
                gs = (probs * dot_nt(grad, value)).astype(BF)
                dvt[here, r] = dot_tn(grad, low_probs)[part].astype(BF)
                dkt[here, r] = dot_tn(query, gs)[part].astype(BF)
                step = dot_nn(gs, kk[r, cols])
                if i == 0:
                    dq[...] = step
                else:
                    dq[...] += step
                return inner

            for i in range(frame_count // ub):
                block(i, 0)
            done = (dq[...] * 0.125).astype(BF)
            if half == 0:
                dqb[:, cols] = done
            else:
                dqb[:, cols] = jnp.where(own, done, dqb[:, cols])
        return carry

    lax.fori_loop(0, HEADS // 2, pair_step, 0)
    sums[...] = jnp.zeros_like(sums)

    def finish(i, carry):
        r = rows(i * lb, lb)
        gn = dot_nn(dqb[r, :], wq[...]) + dot_tn(dkt[:, r], wk[...]) + dot_tn(dvt[:, r], wv[...])
        xhat, inv = normal_stats(x[r, :].astype(F32))
        scaled = gn * gain
        grad_x[r, :] = (
            gmid[r, :]
            + inv
            * (
                scaled
                - jnp.mean(scaled, axis=-1, keepdims=True)
                - xhat * jnp.mean(scaled * xhat, axis=-1, keepdims=True)
            )
        ).astype(BF)
        sums[0:1, :] += jnp.sum(gn * xhat, axis=0, keepdims=True)
        sums[1:2, :] += jnp.sum(gn, axis=0, keepdims=True)
        sums[2:3, :] += jnp.sum(dqb[r, :].astype(F32), axis=0, keepdims=True)
        return carry

    lax.fori_loop(0, frame_count // lb, finish, 0)
    sums[3:4, :] = dot_nt(jnp.ones((8, frame_count), BF), dvt[...])[0:1]
    dwq[...] = dot_tn(dqb[...], nb[...]).astype(BF)
    dwk[...] = dot_nn(dkt[...], nb[...]).astype(BF)
    dwv[...] = dot_nn(dvt[...], nb[...]).astype(BF)


def attend_back(x, gmid, nb, qaug, kk, vv, mixed, dmixed, kaug, wq, wk, wv, vec):
    frame_count, width = x.shape
    square = jax.ShapeDtypeStruct((width, width), BF)
    return pl.pallas_call(
        functools.partial(attend_back_kernel, ub=512, lb=512),
        out_shape=[
            jax.ShapeDtypeStruct((frame_count, width), BF),
            square,
            square,
            square,
            jax.ShapeDtypeStruct((8, width), F32),
        ],
        in_specs=[VMEM_SPEC] * 13,
        out_specs=[VMEM_SPEC] * 5,
        scratch_shapes=[
            pltpu.VMEM((frame_count, 128), F32),
            pltpu.VMEM((frame_count, width), BF),
            pltpu.VMEM((width, frame_count), BF),
            pltpu.VMEM((width, frame_count), BF),
        ],
        compiler_params=pltpu.CompilerParams(vmem_limit_bytes=VMEM_LIMIT),
        name="attend_backward",
    )(x, gmid, nb, qaug, kk, vv, mixed, dmixed, kaug, wq, wk, wv, vec)


def per_device(
    n,
    frames,
    lengths,
    attn_gain,
    attn_shift,
    query_weight,
    query_bias,
    key_weight,
    value_weight,
    value_bias,
    out_weight,
    out_bias,
    mlp_gain,
    mlp_shift,
    up_weight,
    up_bias,
    down_weight,
    down_bias,
    grad_out,
):
    slots, frame_count, width = frames.shape
    assert slots == 1
    share = width // n
    vectors = (
        attn_gain,
        attn_shift,
        query_bias,
        value_bias,
        out_bias,
        mlp_gain,
        mlp_shift,
        down_bias,
    )
    packed = jnp.concatenate(
        [jnp.stack(vectors, axis=1), up_bias.reshape(share, 4), jnp.zeros((share, 116), BF)], axis=1
    )
    shards = (
        query_weight.T,
        key_weight.T,
        value_weight.T,
        out_weight.T,
        up_weight.T,
        down_weight.T,
        packed,
    )
    full = gather_all(n, shards)
    wq, wk, wv, wo, wup, wdn, vec = (
        f.reshape(n * f.shape[3], f.shape[4]) for f in full
    )
    bup = vec[:, 8:12].reshape(1, 4 * width)
    x = frames[0]
    nb, qaug, kk, vv, mixed, middle, kaug = attend(lengths, x, wq, wk, wv, wo, vec)
    layer_out, gmid, dmixed, dwo, dwup, dwdn, sums_two, sum_up = feed(
        lengths, middle, grad_out[0], mixed, wup, wdn, wo, vec, bup
    )
    grad_x, dwq, dwk, dwv, sums_one = attend_back(
        x, gmid, nb, qaug, kk, vv, mixed, dmixed, kaug, wq, wk, wv, vec
    )
    columns = jnp.concatenate(
        [
            sums_one[:4].T,
            sums_two[:4].T,
            sum_up[0].reshape(width, 4),
            jnp.zeros((width, 116), F32),
        ],
        axis=1,
    ).astype(BF)
    far, near = levels_of(n)

    def split(g):
        return g.reshape(far, near, 2, g.shape[0] // n, g.shape[1])

    gq, gk, gv, go, gu, gd, gc = scatter_all(
        n, tuple(split(g) for g in (dwq, dwk, dwv, dwo, dwup, dwdn, columns))
    )
    return (
        layer_out[None],
        grad_x[None],
        gc[:, 0],
        gc[:, 1],
        gq.T,
        gc[:, 2],
        gk.T,
        gv.T,
        gc[:, 3],
        go.T,
        gc[:, 4],
        gc[:, 5],
        gc[:, 6],
        gu.T,
        gc[:, 8:12].reshape(4 * share),
        gd.T,
        gc[:, 7],
    )


def solution(mesh):
    row, col, vector = P("dp", None, None), P(None, "dp"), P("dp")
    return jax.shard_map(
        functools.partial(per_device, mesh.shape["dp"]),
        mesh=mesh,
        in_specs=(
            row,
            P("dp", None),
            vector,
            vector,
            col,
            vector,
            col,
            col,
            vector,
            col,
            vector,
            vector,
            vector,
            col,
            vector,
            col,
            vector,
            row,
        ),
        out_specs=(
            row,
            row,
            vector,
            vector,
            col,
            vector,
            col,
            col,
            vector,
            col,
            vector,
            vector,
            vector,
            col,
            vector,
            col,
            vector,
        ),
        check_vma=False,
    )
```

```python
import functools
import math

import jax
import jax.numpy as jnp
from jax import lax
from jax.experimental import pallas as pl
from jax.experimental.pallas import tpu as pltpu
from jax.sharding import PartitionSpec as P

HEADS = 8
EPS = 1e-05
MESH = pl.DeviceIdType.MESH
F32 = jnp.float32
BF = jnp.bfloat16
VMEM_SPEC = pl.BlockSpec(memory_space=pltpu.VMEM)
SMEM_SPEC = pl.BlockSpec(memory_space=pltpu.SMEM)
HBM_SPEC = pl.BlockSpec(memory_space=pl.ANY)
EXCLUDED = -1e30
VMEM_LIMIT = 62 << 20


def dot_nn(a, b):
    return lax.dot_general(a, b, (((1,), (0,)), ((), ())), preferred_element_type=F32)


def dot_nt(a, b):
    return lax.dot_general(a, b, (((1,), (1,)), ((), ())), preferred_element_type=F32)


def dot_tn(a, b):
    return lax.dot_general(a, b, (((0,), (0,)), ((), ())), preferred_element_type=F32)


def levels_of(n):
    rest = n // 2
    bits = rest.bit_length() - 1
    near = 2 ** ((bits + 1) // 2)
    return rest // near, near


def rows(start, size):
    return pl.ds(pl.multiple_of(start, size), size)


def normal_stats(block):
    mean = jnp.mean(block, axis=-1, keepdims=True)
    centered = block - mean
    inv = lax.rsqrt(jnp.mean(centered * centered, axis=-1, keepdims=True) + EPS)
    return centered * inv, inv


def everyone_barrier(n, me, far, near):
    barrier = pltpu.get_barrier_semaphore()
    core = lax.rem(me, 2)
    mid = lax.rem(me // 2, near)
    top = me // (2 * near)
    peers = [(lax.rem(top + k, far) * near + mid) * 2 + core for k in range(1, far)]
    peers += [(top * near + lax.rem(mid + k, near)) * 2 + core for k in range(1, near)]
    peers += [(top * near + mid) * 2 + 1 - core]
    for peer in peers:
        pl.semaphore_signal(barrier, inc=1, device_id=(peer,), device_id_type=MESH)
    pl.semaphore_wait(barrier, len(peers))
    return top, mid, core


def gather_kernel(n, count, *refs):
    shards, outs = refs[:count], refs[count : 2 * count]
    own_sem, far_s, far_r, near_s, near_r, core_s, core_r = refs[2 * count :]
    far, near = levels_of(n)
    me = lax.axis_index("dp")
    top, mid, core = everyone_barrier(n, me, far, near)

    def index(t, m, c):
        return (t * near + m) * 2 + c

    far_copies, near_copies = {}, {}
    for a in range(count):
        for k in range(1, far):
            copy = pltpu.make_async_remote_copy(
                src_ref=shards[a],
                dst_ref=outs[a].at[top, mid, core],
                send_sem=far_s.at[a, k - 1],
                recv_sem=far_r.at[a, k - 1],
                device_id=(index(lax.rem(top + k, far), mid, core),),
                device_id_type=MESH,
            )
            copy.start()
            far_copies[a, k] = copy
        pltpu.make_async_copy(shards[a], outs[a].at[top, mid, core], own_sem.at[a]).start()
    for a in range(count):
        pltpu.make_async_copy(shards[a], outs[a].at[top, mid, core], own_sem.at[a]).wait()
        for k in range(1, far):
            far_copies[a, k].wait_recv()
        for k in range(1, near):
            copy = pltpu.make_async_remote_copy(
                src_ref=outs[a].at[:, mid, core],
                dst_ref=outs[a].at[:, mid, core],
                send_sem=near_s.at[a, k - 1],
                recv_sem=near_r.at[a, k - 1],
                device_id=(index(top, lax.rem(mid + k, near), core),),
                device_id_type=MESH,
            )
            copy.start()
            near_copies[a, k] = copy
    core_copies = []
    for a in range(count):
        for k in range(1, near):
            near_copies[a, k].wait_recv()
        copy = pltpu.make_async_remote_copy(
            src_ref=outs[a].at[:, :, core],
            dst_ref=outs[a].at[:, :, core],
            send_sem=core_s.at[a],
            recv_sem=core_r.at[a],
            device_id=(index(top, mid, 1 - core),),
            device_id_type=MESH,
        )
        copy.start()
        core_copies.append(copy)
    for a in range(count):
        core_copies[a].wait_recv()
    for a in range(count):
        for k in range(1, far):
            far_copies[a, k].wait_send()
        for k in range(1, near):
            near_copies[a, k].wait_send()
        core_copies[a].wait_send()


def gather_all(n, shards):
    far, near = levels_of(n)
    count = len(shards)
    return pl.pallas_call(
        functools.partial(gather_kernel, n, count),
        out_shape=[jax.ShapeDtypeStruct((far, near, 2) + s.shape, s.dtype) for s in shards],
        in_specs=[VMEM_SPEC] * count,
        out_specs=[HBM_SPEC] * count,
        scratch_shapes=[
            pltpu.SemaphoreType.DMA((count,)),
            pltpu.SemaphoreType.DMA((count, far - 1)),
            pltpu.SemaphoreType.DMA((count, far - 1)),
            pltpu.SemaphoreType.DMA((count, near - 1)),
            pltpu.SemaphoreType.DMA((count, near - 1)),
            pltpu.SemaphoreType.DMA((count,)),
            pltpu.SemaphoreType.DMA((count,)),
        ],
        compiler_params=pltpu.CompilerParams(
            collective_id=0, has_side_effects=True, vmem_limit_bytes=32 << 20
        ),
        name="gather_params",
    )(*shards)


def scatter_kernel(n, count, *refs):
    parts, outs = refs[:count], refs[count : 2 * count]
    pos = 2 * count
    core_in, core_sum = refs[pos : pos + count], refs[pos + count : pos + 2 * count]
    pos += 2 * count
    near_in, near_sum = refs[pos : pos + count], refs[pos + count : pos + 2 * count]
    pos += 2 * count
    far_in = refs[pos : pos + count]
    core_s, core_r, near_s, near_r, far_s, far_r = refs[pos + count :]
    far, near = levels_of(n)
    me = lax.axis_index("dp")
    top, mid, core = everyone_barrier(n, me, far, near)

    def index(t, m, c):
        return (t * near + m) * 2 + c

    core_copies, near_copies, far_copies = [], {}, {}
    for a in range(count):
        copy = pltpu.make_async_remote_copy(
            src_ref=parts[a].at[:, :, 1 - core],
            dst_ref=core_in[a],
            send_sem=core_s.at[a],
            recv_sem=core_r.at[a],
            device_id=(index(top, mid, 1 - core),),
            device_id_type=MESH,
        )
        copy.start()
        core_copies.append(copy)
    for a in range(count):
        core_copies[a].wait_recv()

        def add_core(i, carry, a=a):
            f, m = i // near, lax.rem(i, near)
            core_sum[a][m, f] = (
                parts[a][f, m, core].astype(F32) + core_in[a][f, m].astype(F32)
            ).astype(BF)
            return carry

        lax.fori_loop(0, far * near, add_core, 0)
        for k in range(1, near):
            peer = lax.rem(mid + k, near)
            copy = pltpu.make_async_remote_copy(
                src_ref=core_sum[a].at[peer],
                dst_ref=near_in[a].at[k - 1],
                send_sem=near_s.at[a, k - 1],
                recv_sem=near_r.at[a, k - 1],
                device_id=(index(top, peer, core),),
                device_id_type=MESH,
            )
            copy.start()
            near_copies[a, k] = copy
    for a in range(count):
        for k in range(1, near):
            near_copies[a, k].wait_recv()

        def add_near(f, carry, a=a):
            total = core_sum[a][mid, f].astype(F32)
            for k in range(near - 1):
                total = total + near_in[a][k, f].astype(F32)
            near_sum[a][f] = total.astype(BF)
            return carry

        lax.fori_loop(0, far, add_near, 0)
        for k in range(1, far):
            peer = lax.rem(top + k, far)
            copy = pltpu.make_async_remote_copy(
                src_ref=near_sum[a].at[peer],
                dst_ref=far_in[a].at[k - 1],
                send_sem=far_s.at[a, k - 1],
                recv_sem=far_r.at[a, k - 1],
                device_id=(index(peer, mid, core),),
                device_id_type=MESH,
            )
            copy.start()
            far_copies[a, k] = copy
    for a in range(count):
        for k in range(1, far):
            far_copies[a, k].wait_recv()
        total = near_sum[a][top].astype(F32)
        for k in range(far - 1):
            total = total + far_in[a][k].astype(F32)
        outs[a][...] = total
    for a in range(count):
        core_copies[a].wait_send()
        for k in range(1, near):
            near_copies[a, k].wait_send()
        for k in range(1, far):
            far_copies[a, k].wait_send()


def scatter_all(n, parts):
    far, near = levels_of(n)
    count = len(parts)
    blocks = [p.shape[3:] for p in parts]
    return pl.pallas_call(
        functools.partial(scatter_kernel, n, count),
        out_shape=[jax.ShapeDtypeStruct(b, F32) for b in blocks],
        in_specs=[VMEM_SPEC] * count,
        out_specs=[VMEM_SPEC] * count,
        scratch_shapes=[pltpu.VMEM((far, near) + b, BF) for b in blocks]
        + [pltpu.VMEM((near, far) + b, BF) for b in blocks]
        + [pltpu.VMEM((near - 1, far) + b, BF) for b in blocks]
        + [pltpu.VMEM((far,) + b, BF) for b in blocks]
        + [pltpu.VMEM((far - 1,) + b, BF) for b in blocks]
        + [
            pltpu.SemaphoreType.DMA((count,)),
            pltpu.SemaphoreType.DMA((count,)),
            pltpu.SemaphoreType.DMA((count, near - 1)),
            pltpu.SemaphoreType.DMA((count, near - 1)),
            pltpu.SemaphoreType.DMA((count, far - 1)),
            pltpu.SemaphoreType.DMA((count, far - 1)),
        ],
        compiler_params=pltpu.CompilerParams(
            collective_id=1, has_side_effects=True, vmem_limit_bytes=VMEM_LIMIT
        ),
        name="scatter_grads",
    )(*parts)


def segment_lanes(lengths, position, lane):
    leading = lengths[0, 0]
    finish = leading + lengths[0, 1]
    segment = jnp.where(position < leading, 0, jnp.where(position < finish, 1, 2))
    return lax.rem(lane, 64) == segment


def three_pieces(column):
    high = column.astype(BF)
    rest = column - high.astype(F32)
    middle = rest.astype(BF)
    return high, middle, (rest - middle.astype(F32)).astype(BF)


def own_lanes(lane, half):
    return (lane < 64) if half == 0 else (lane >= 64)


def attend_kernel(
    lengths, x, wq, wk, wv, wo, vec, nb, qaug, kk, vv, mixed, middle, kaug, qbuf, *, tb, lb
):
    frame_count = x.shape[0]
    lane = lax.broadcasted_iota(jnp.int32, (1, 128), 1)
    table = vec[...].astype(F32).T
    gain, shift, bq, bv, bo = (table[i : i + 1] for i in range(5))

    def project(i, carry):
        r = rows(i * lb, lb)
        xhat, _ = normal_stats(x[r, :].astype(F32))
        normed = (xhat * gain + shift).astype(BF)
        nb[r, :] = normed
        qbuf[r, :] = ((dot_nt(normed, wq[...]) + bq).astype(BF).astype(F32) * 0.125).astype(BF)
        kk[r, :] = dot_nt(normed, wk[...]).astype(BF)
        vv[r, :] = (dot_nt(normed, wv[...]) + bv).astype(BF)
        position = lax.broadcasted_iota(jnp.int32, (lb, 128), 0) + i * lb
        lanes = lax.broadcasted_iota(jnp.int32, (lb, 128), 1)
        same = segment_lanes(lengths, position, lanes)
        slot = lax.rem(lanes, 64)
        kaug[r, :] = jnp.where(
            slot < 3, jnp.where(same, 0.0, EXCLUDED), jnp.where(slot < 6, 1.0, 0.0)
        ).astype(BF)
        return carry

    lax.fori_loop(0, frame_count // lb, project, 0)

    def pair_step(p, carry):
        cols = rows(p * 128, 128)
        for half in range(2):
            own = own_lanes(lane, half)
            base = 64 - 64 * half
            key = jnp.where(own, kk[:, cols], kaug[...])
            value = jnp.where(own, vv[:, cols], jnp.ones((1, 128), BF))
            head = pl.multiple_of((2 * p + half) * 128, 128)

            def block(i, inner, half=half, own=own, base=base, key=key, value=value, head=head):
                r = rows(i * tb, tb)
                position = lax.broadcasted_iota(jnp.int32, (tb, 128), 0) + i * tb
                lanes = lax.broadcasted_iota(jnp.int32, (tb, 128), 1)
                mark = jnp.where(segment_lanes(lengths, position, lanes), 1.0, 0.0).astype(BF)
                query = jnp.where(own, qbuf[r, cols], mark)
                scores = dot_nt(query, key)
                top = jnp.max(scores, axis=1, keepdims=True)
                raised = jnp.exp(scores - top).astype(BF)
                got = dot_nn(raised, value)
                total = got[:, base : base + 1]
                got = (got * (1.0 / total)).astype(BF)
                if half == 0:
                    mixed[r, cols] = got
                else:
                    mixed[r, cols] = jnp.where(own, got, mixed[r, cols])
                high, mid, low = three_pieces(-(top + jnp.log(total)))
                query = jnp.where(lane == base + 3, high, query)
                query = jnp.where(lane == base + 4, mid, query)
                qaug[r, pl.ds(head, 128)] = jnp.where(lane == base + 5, low, query)
                return inner

            lax.fori_loop(0, frame_count // tb, block, 0, unroll=True)
        return carry

    lax.fori_loop(0, HEADS // 2, pair_step, 0)

    def finish(i, carry):
        r = rows(i * lb, lb)
        middle[r, :] = x[r, :].astype(F32) + (dot_nt(mixed[r, :], wo[...]) + bo)
        return carry

    lax.fori_loop(0, frame_count // lb, finish, 0)


def attend(lengths, x, wq, wk, wv, wo, vec):
    frame_count, width = x.shape
    low = jax.ShapeDtypeStruct((frame_count, width), BF)
    return pl.pallas_call(
        functools.partial(attend_kernel, tb=512, lb=512),
        out_shape=[
            low,
            jax.ShapeDtypeStruct((frame_count, HEADS * 128), BF),
            low,
            low,
            low,
            jax.ShapeDtypeStruct((frame_count, width), F32),
            jax.ShapeDtypeStruct((frame_count, 128), BF),
        ],
        in_specs=[SMEM_SPEC] + [VMEM_SPEC] * 6,
        out_specs=[VMEM_SPEC] * 7,
        scratch_shapes=[pltpu.VMEM((frame_count, width), BF)],
        compiler_params=pltpu.CompilerParams(vmem_limit_bytes=VMEM_LIMIT),
        name="attend_forward",
    )(lengths, x, wq, wk, wv, wo, vec)


def feed_kernel(
    lengths,
    middle,
    gout,
    mixed,
    wup,
    wdn,
    wo,
    vec,
    bup,
    layer_out,
    gmid,
    dmixed,
    dwo,
    dwup,
    dwdn,
    sums,
    sum_up,
    nb,
    act,
    gup,
    glow,
    gbl,
    *,
    tb,
):
    frame_count = middle.shape[0]
    finish = lengths[0, 0] + lengths[0, 1]
    table = vec[...].astype(F32).T
    gain, shift, bdn = (table[i : i + 1] for i in range(5, 8))
    sums[...] = jnp.zeros_like(sums)
    sum_up[...] = jnp.zeros_like(sum_up)

    def block(i, carry):
        r = rows(i * tb, tb)
        valid = lax.broadcasted_iota(jnp.int32, (tb, 1), 0) + i * tb < finish
        mid = middle[r, :]
        xhat, inv = normal_stats(mid)
        normed = (xhat * gain + shift).astype(BF)
        nb[r, :] = normed
        up = dot_nt(normed, wup[...]) + bup[...].astype(F32)
        cdf = 0.5 * (1.0 + lax.erf(up * (1.0 / math.sqrt(2.0))))
        low = (up * cdf).astype(BF)
        act[r, :] = low
        down = dot_nt(low, wdn[...]) + bdn
        layer_out[r, :] = jnp.where(valid, mid + down, 0.0).astype(BF)
        grow = jnp.where(valid, gout[r, :].astype(F32), 0.0)
        gl = grow.astype(BF)
        glow[r, :] = gl
        slope = cdf + up * jnp.exp(-0.5 * up * up) * (1.0 / math.sqrt(2.0 * math.pi))
        gu = (dot_nn(gl, wdn[...]) * slope).astype(BF)
        gup[r, :] = gu
        gn = dot_nn(gu, wup[...])
        scaled = gn * gain
        gm = grow + inv * (
            scaled
            - jnp.mean(scaled, axis=-1, keepdims=True)
            - xhat * jnp.mean(scaled * xhat, axis=-1, keepdims=True)
        )
        gmid[r, :] = gm
        gb = gm.astype(BF)
        gbl[r, :] = gb
        dmixed[r, :] = dot_nn(gb, wo[...]).astype(BF)
        sums[0:1, :] += jnp.sum(gb.astype(F32), axis=0, keepdims=True)
        sums[1:2, :] += jnp.sum(gn * xhat, axis=0, keepdims=True)
        sums[2:3, :] += jnp.sum(gn, axis=0, keepdims=True)
        sums[3:4, :] += jnp.sum(grow, axis=0, keepdims=True)
        sum_up[0:1, :] += jnp.sum(gu.astype(F32), axis=0, keepdims=True)
        return carry

    lax.fori_loop(0, frame_count // tb, block, 0)
    dwo[...] = dot_tn(gbl[...], mixed[...]).astype(BF)

    def weights(i, carry):
        c = rows(i * 512, 512)
        dwup[c, :] = dot_tn(gup[:, c], nb[...]).astype(BF)
        dwdn[:, c] = dot_tn(glow[...], act[:, c]).astype(BF)
        return carry

    lax.fori_loop(0, wup.shape[0] // 512, weights, 0)


def feed(lengths, middle, gout, mixed, wup, wdn, wo, vec, bup):
    frame_count, width = middle.shape
    hidden = wup.shape[0]
    low = jax.ShapeDtypeStruct((frame_count, width), BF)
    return pl.pallas_call(
        functools.partial(feed_kernel, tb=256),
        out_shape=[
            low,
            jax.ShapeDtypeStruct((frame_count, width), F32),
            low,
            jax.ShapeDtypeStruct((width, width), BF),
            jax.ShapeDtypeStruct((hidden, width), BF),
            jax.ShapeDtypeStruct((width, hidden), BF),
            jax.ShapeDtypeStruct((8, width), F32),
            jax.ShapeDtypeStruct((8, hidden), F32),
        ],
        in_specs=[SMEM_SPEC] + [VMEM_SPEC] * 8,
        out_specs=[VMEM_SPEC] * 8,
        scratch_shapes=[
            pltpu.VMEM((frame_count, width), BF),
            pltpu.VMEM((frame_count, hidden), BF),
            pltpu.VMEM((frame_count, hidden), BF),
            pltpu.VMEM((frame_count, width), BF),
            pltpu.VMEM((frame_count, width), BF),
        ],
        compiler_params=pltpu.CompilerParams(vmem_limit_bytes=VMEM_LIMIT),
        name="feed_forward_both",
    )(lengths, middle, gout, mixed, wup, wdn, wo, vec, bup)


def attend_back_kernel(
    x,
    gmid,
    nb,
    qaug,
    kk,
    vv,
    mixed,
    dmixed,
    kaug,
    wq,
    wk,
    wv,
    vec,
    grad_x,
    dwq,
    dwk,
    dwv,
    sums,
    dq,
    dqb,
    dkt,
    dvt,
    *,
    ub,
    lb,
):
    frame_count = x.shape[0]
    lane = lax.broadcasted_iota(jnp.int32, (1, 128), 1)
    gain = vec[...].astype(F32).T[0:1]

    def pair_step(p, carry):
        cols = rows(p * 128, 128)
        grad_pair = dmixed[:, cols]
        product = grad_pair.astype(F32) * mixed[:, cols].astype(F32)
        for half in range(2):
            own = own_lanes(lane, half)
            base = 64 - 64 * half
            delta = jnp.sum(jnp.where(own, product, 0.0), axis=1, keepdims=True)
            high, mid, low = three_pieces(-delta)
            grad = jnp.where(own, grad_pair, jnp.zeros((1, 128), BF))
            grad = jnp.where(lane == base + 3, high, grad)
            grad = jnp.where(lane == base + 4, mid, grad)
            grad = jnp.where(lane == base + 5, low, grad)
            query = qaug[:, pl.ds(pl.multiple_of((2 * p + half) * 128, 128), 128)]
            here = pl.ds(pl.multiple_of(p * 128 + 64 * half, 64), 64)
            part = slice(64 * half, 64 * half + 64)
            ones = jnp.where(
                (lane >= base + 3) & (lane < base + 6), jnp.ones((1, 128), F32), 0.0
            ).astype(BF)

            def block(i, inner):
                r = rows(i * ub, ub)
                key = jnp.where(own, kk[r, cols], kaug[r, :])
                value = jnp.where(own, vv[r, cols], ones)
                probs = jnp.exp(dot_nt(query, key))
                low_probs = probs.astype(BF)
                gs = (probs * dot_nt(grad, value)).astype(BF)
                dvt[here, r] = dot_tn(grad, low_probs)[part].astype(BF)
                dkt[here, r] = dot_tn(query, gs)[part].astype(BF)
                step = dot_nn(gs, kk[r, cols])
                if i == 0:
                    dq[...] = step
                else:
                    dq[...] += step
                return inner

            for i in range(frame_count // ub):
                block(i, 0)
            done = (dq[...] * 0.125).astype(BF)
            if half == 0:
                dqb[:, cols] = done
            else:
                dqb[:, cols] = jnp.where(own, done, dqb[:, cols])
        return carry

    lax.fori_loop(0, HEADS // 2, pair_step, 0)
    sums[...] = jnp.zeros_like(sums)

    def finish(i, carry):
        r = rows(i * lb, lb)
        gn = dot_nn(dqb[r, :], wq[...]) + dot_tn(dkt[:, r], wk[...]) + dot_tn(dvt[:, r], wv[...])
        xhat, inv = normal_stats(x[r, :].astype(F32))
        scaled = gn * gain
        grad_x[r, :] = (
            gmid[r, :]
            + inv
            * (
                scaled
                - jnp.mean(scaled, axis=-1, keepdims=True)
                - xhat * jnp.mean(scaled * xhat, axis=-1, keepdims=True)
            )
        ).astype(BF)
        sums[0:1, :] += jnp.sum(gn * xhat, axis=0, keepdims=True)
        sums[1:2, :] += jnp.sum(gn, axis=0, keepdims=True)
        sums[2:3, :] += jnp.sum(dqb[r, :].astype(F32), axis=0, keepdims=True)
        return carry

    lax.fori_loop(0, frame_count // lb, finish, 0)
    sums[3:4, :] = dot_nt(jnp.ones((8, frame_count), BF), dvt[...])[0:1]
    dwq[...] = dot_tn(dqb[...], nb[...]).astype(BF)
    dwk[...] = dot_nn(dkt[...], nb[...]).astype(BF)
    dwv[...] = dot_nn(dvt[...], nb[...]).astype(BF)


def attend_back(x, gmid, nb, qaug, kk, vv, mixed, dmixed, kaug, wq, wk, wv, vec):
    frame_count, width = x.shape
    square = jax.ShapeDtypeStruct((width, width), BF)
    return pl.pallas_call(
        functools.partial(attend_back_kernel, ub=512, lb=512),
        out_shape=[
            jax.ShapeDtypeStruct((frame_count, width), BF),
            square,
            square,
            square,
            jax.ShapeDtypeStruct((8, width), F32),
        ],
        in_specs=[VMEM_SPEC] * 13,
        out_specs=[VMEM_SPEC] * 5,
        scratch_shapes=[
            pltpu.VMEM((frame_count, 128), F32),
            pltpu.VMEM((frame_count, width), BF),
            pltpu.VMEM((width, frame_count), BF),
            pltpu.VMEM((width, frame_count), BF),
        ],
        compiler_params=pltpu.CompilerParams(vmem_limit_bytes=VMEM_LIMIT),
        name="attend_backward",
    )(x, gmid, nb, qaug, kk, vv, mixed, dmixed, kaug, wq, wk, wv, vec)


def bits_differ(a, b, size):
    total, bit = 0, 1
    while bit < size:
        total = total + bit * lax.rem(a // bit + b // bit, 2)
        bit *= 2
    return total


def remote(src, dst, send, recv, device):
    return pltpu.make_async_remote_copy(
        src_ref=src,
        dst_ref=dst,
        send_sem=send,
        recv_sem=recv,
        device_id=(device,),
        device_id_type=MESH,
    )


def vector_rows(vec, first, count, share, width, n):
    lanes = vec.shape[-1]
    flat = vec[...].reshape(n * 8, lanes).astype(BF)
    out = []
    source = lax.broadcasted_iota(jnp.int32, (lanes, width), 0)
    target = lax.broadcasted_iota(jnp.int32, (lanes, width), 1)
    owner = lax.broadcasted_iota(jnp.int32, (n * 8, width), 0)
    place = lax.broadcasted_iota(jnp.int32, (n * 8, width), 1)
    chosen = owner == 8 * (place // share)
    for v in range(count):
        pick = jnp.where(source == first + v * share + lax.rem(target, share), 1.0, 0.0).astype(BF)
        spread = dot_nn(flat, pick)
        out.append(jnp.sum(jnp.where(chosen, spread, 0.0), axis=0, keepdims=True))
    return out


def gather_attend_kernel(n, tb, lb, *refs):
    (lengths, x, sq, sk, sv, so, su, sd, svec) = refs[:9]
    (wq, wk, wv, wo, wup, wdn, table, bup, kk_h, vv_h, qaug_h, nb_h, mixed_h, middle_h) = refs[9:23]
    (xhat, nb, mixed, middle, kaug, qbuf, kbuf, vbuf, qaug, vec) = refs[23:33]
    (own_sem, near_s, near_r, core_s, core_r, far_s, far_r, fwd_s, fwd_r) = refs[33:42]
    (bown_sem, bfar_s, bfar_r, bnear_s, bnear_r, bcore_s, bcore_r, out_sem, end_sem) = refs[42:]
    far, near = levels_of(n)
    share = 512 // n
    frame_count, width = x.shape
    pairs = HEADS // 2
    me = lax.axis_index("dp")
    top, mid, core = everyone_barrier(n, me, far, near)
    lane = lax.broadcasted_iota(jnp.int32, (1, 128), 1)

    def index(t, m, c):
        return (t * near + m) * 2 + c

    sibling = index(top, mid, 1 - core)
    first = list(zip((sq, sk, sv), (wq, wk, wv)))
    second = list(zip((svec, so, su, sd), (vec, wo, wup, wdn)))

    def near_copy(a, k):
        peer = index(top, lax.rem(mid + k, near), core)
        src, dst = first[a]
        return remote(src, dst.at[top, mid, core], near_s.at[a, k - 1], near_r.at[a, k - 1], peer)

    def core_copy(a):
        ref = first[a][1].at[top, :, core]
        return remote(ref, ref, core_s.at[a], core_r.at[a], sibling)

    def far_copy(a, k):
        ref = first[a][1].at[top, :, core]
        peer = index(bits_differ(top, k, far), mid, core)
        return remote(ref, ref, far_s.at[a, k - 1], far_r.at[a, k - 1], peer)

    def fwd_copy(a, k):
        ref = first[a][1].at[bits_differ(top, k, far), :, core]
        return remote(ref, ref, fwd_s.at[a, k - 1], fwd_r.at[a, k - 1], sibling)

    def bfar_copy(a, k):
        src, dst = second[a]
        peer = index(bits_differ(top, k, far), mid, core)
        return remote(src, dst.at[top, mid, core], bfar_s.at[a, k - 1], bfar_r.at[a, k - 1], peer)

    def bnear_copy(a, k):
        ref = second[a][1].at[:, mid, core]
        peer = index(top, lax.rem(mid + k, near), core)
        return remote(ref, ref, bnear_s.at[a, k - 1], bnear_r.at[a, k - 1], peer)

    def bcore_copy(a):
        ref = second[a][1].at[:, :, core]
        return remote(ref, ref, bcore_s.at[a], bcore_r.at[a], sibling)

    def own_copy(a):
        src, dst = first[a]
        return pltpu.make_async_copy(src, dst.at[top, mid, core], own_sem.at[a])

    def bown_copy(a):
        src, dst = second[a]
        return pltpu.make_async_copy(src, dst.at[top, mid, core], bown_sem.at[a])

    for k in range(1, far):
        bfar_copy(0, k).start()
    bown_copy(0).start()
    for a in range(3):
        for k in range(1, near):
            near_copy(a, k).start()
        own_copy(a).start()
    for a in range(1, 4):
        for k in range(1, far):
            bfar_copy(a, k).start()
        bown_copy(a).start()

    def stats(i, carry):
        r = rows(i * lb, lb)
        xhat[r, :] = normal_stats(x[r, :].astype(F32))[0]
        position = lax.broadcasted_iota(jnp.int32, (lb, 128), 0) + i * lb
        lanes = lax.broadcasted_iota(jnp.int32, (lb, 128), 1)
        same = segment_lanes(lengths, position, lanes)
        slot = lax.rem(lanes, 64)
        kaug[r, :] = jnp.where(
            slot < 3, jnp.where(same, 0.0, EXCLUDED), jnp.where(slot < 6, 1.0, 0.0)
        ).astype(BF)
        return carry

    bown_copy(0).wait()
    for k in range(1, far):
        bfar_copy(0, k).wait_recv()
    for k in range(1, near):
        bnear_copy(0, k).start()
    lax.fori_loop(0, frame_count // lb, stats, 0)
    for a in range(3):
        own_copy(a).wait()
        for k in range(1, near):
            near_copy(a, k).wait_recv()
        core_copy(a).start()
    for k in range(1, near):
        bnear_copy(0, k).wait_recv()
    bcore_copy(0).start()
    for k in range(1, far):
        for a in range(3):
            far_copy(a, k).start()
    bcore_copy(0).wait_recv()
    found = vector_rows(vec, 0, 8, share, width, n)
    for v in range(8):
        table[v : v + 1, :] = found[v]
    table[8:16, :] = jnp.zeros((8, width), F32)
    bup[...] = jnp.broadcast_to(vector_rows(vec, 8 * share, 1, 4 * share, 4 * width, n)[0], bup.shape)
    gain, shift = table[0:1, :], table[1:2, :]

    def norm(i, carry):
        r = rows(i * lb, lb)
        nb[r, :] = (xhat[r, :] * gain + shift).astype(BF)
        return carry

    lax.fori_loop(0, frame_count // lb, norm, 0)
    nb_copy = pltpu.make_async_copy(nb, nb_h, end_sem.at[0])
    nb_copy.start()
    for a in range(3):
        core_copy(a).wait_recv()

    def out_copies(p, slot):
        cols = rows(p * 128, 128)
        wide = rows(p * 256, 256)
        return (
            pltpu.make_async_copy(kbuf.at[slot], kk_h.at[:, cols], out_sem.at[slot, 0]),
            pltpu.make_async_copy(vbuf.at[slot], vv_h.at[:, cols], out_sem.at[slot, 1]),
            pltpu.make_async_copy(qaug.at[slot], qaug_h.at[:, wide], out_sem.at[slot, 2]),
        )

    def pair_step(i, carry):
        p = bits_differ(top, i, far)
        slot = lax.rem(i, 2)
        cols = rows(p * 128, 128)

        @pl.when(i > 0)
        def _():
            for a in range(3):
                fwd_copy(a, i).wait_recv()

        @pl.when(i > 1)
        def _():
            for copy in out_copies(bits_differ(top, i - 2, far), slot):
                copy.wait()

        weights = jnp.concatenate(
            [w[p].reshape(128, width) for w in (wq, wk, wv)], axis=0
        )
        bq, bv = table[2:3, cols], table[3:4, cols]

        def project(j, inner):
            r = rows(j * lb, lb)
            got = dot_nt(nb[r, :], weights)
            qbuf[r, :] = ((got[:, :128] + bq).astype(BF).astype(F32) * 0.125).astype(BF)
            kbuf[slot, r, :] = got[:, 128:256].astype(BF)
            vbuf[slot, r, :] = (got[:, 256:] + bv).astype(BF)
            return inner

        lax.fori_loop(0, frame_count // lb, project, 0)
        for half in range(2):
            own = own_lanes(lane, half)
            base = 64 - 64 * half
            key = jnp.where(own, kbuf[slot], kaug[...])
            value = jnp.where(own, vbuf[slot], jnp.ones((1, 128), BF))

            def block(j):
                r = pl.ds(j * tb, tb)
                position = lax.broadcasted_iota(jnp.int32, (tb, 128), 0) + j * tb
                lanes = lax.broadcasted_iota(jnp.int32, (tb, 128), 1)
                mark = jnp.where(segment_lanes(lengths, position, lanes), 1.0, 0.0).astype(BF)
                query = jnp.where(own, qbuf[r, :], mark)
                scores = dot_nt(query, key)
                peak = jnp.max(scores, axis=1, keepdims=True)
                raised = jnp.exp(scores - peak).astype(BF)
                got = dot_nn(raised, value)
                total = got[:, base : base + 1]
                got = (got * (1.0 / total)).astype(BF)
                if half == 0:
                    mixed[r, cols] = got
                else:
                    mixed[r, cols] = jnp.where(own, got, mixed[r, cols])
                high, middle_piece, low = three_pieces(-(peak + jnp.log(total)))
                query = jnp.where(lane == base + 3, high, query)
                query = jnp.where(lane == base + 4, middle_piece, query)
                qaug[slot, r, 128 * half : 128 * half + 128] = jnp.where(
                    lane == base + 5, low, query
                )

            for j in range(frame_count // tb):
                block(j)
            if half == 0:

                @pl.when(i < far - 1)
                def _():
                    for a in range(3):
                        far_copy(a, i + 1).wait_recv()
                        fwd_copy(a, i + 1).start()

            else:

                @pl.when(i == 0)
                def _():
                    for a in range(1, 4):
                        bown_copy(a).wait()
                        for k in range(1, far):
                            bfar_copy(a, k).wait_recv()
                        for k in range(1, near):
                            bnear_copy(a, k).start()

                @pl.when(i == 2)
                def _():
                    for a in range(1, 4):
                        for k in range(1, near):
                            bnear_copy(a, k).wait_recv()
                        bcore_copy(a).start()

        for copy in out_copies(p, slot):
            copy.start()
        return carry

    lax.fori_loop(0, pairs, pair_step, 0)
    mixed_copy = pltpu.make_async_copy(mixed, mixed_h, end_sem.at[1])
    mixed_copy.start()
    bcore_copy(1).wait_recv()
    out_weight = wo[...].reshape(width, width)
    bo = table[4:5, :]

    def finish(i, carry):
        r = rows(i * lb, lb)
        middle[r, :] = x[r, :].astype(F32) + (dot_nt(mixed[r, :], out_weight) + bo)
        return carry

    lax.fori_loop(0, frame_count // lb, finish, 0)
    middle_copy = pltpu.make_async_copy(middle, middle_h, end_sem.at[2])
    middle_copy.start()
    for i in (pairs - 2, pairs - 1):
        for copy in out_copies(bits_differ(top, i, far), i % 2):
            copy.wait()
    nb_copy.wait()
    mixed_copy.wait()
    for a in range(3):
        for k in range(1, near):
            near_copy(a, k).wait_send()
        core_copy(a).wait_send()
        for k in range(1, far):
            far_copy(a, k).wait_send()
            fwd_copy(a, k).wait_send()
    bcore_copy(2).wait_recv()
    bcore_copy(3).wait_recv()
    for a in range(4):
        for k in range(1, far):
            bfar_copy(a, k).wait_send()
        for k in range(1, near):
            bnear_copy(a, k).wait_send()
        bcore_copy(a).wait_send()
    middle_copy.wait()


def gather_attend(n, lengths, x, shards):
    far, near = levels_of(n)
    frame_count, width = x.shape
    lead = (far, near, 2)
    share = width // n
    square = jax.ShapeDtypeStruct(lead + (share, width), BF)
    low = jax.ShapeDtypeStruct((frame_count, width), BF)
    dma = pltpu.SemaphoreType.DMA
    return pl.pallas_call(
        functools.partial(gather_attend_kernel, n, 512, 512),
        out_shape=[
            square,
            square,
            square,
            square,
            jax.ShapeDtypeStruct(lead + (4 * share, width), BF),
            jax.ShapeDtypeStruct(lead + (share, 4 * width), BF),
            jax.ShapeDtypeStruct((16, width), F32),
            jax.ShapeDtypeStruct((8, 4 * width), F32),
            low,
            low,
            jax.ShapeDtypeStruct((frame_count, HEADS * 128), BF),
            low,
            low,
            jax.ShapeDtypeStruct((frame_count, width), F32),
        ],
        in_specs=[SMEM_SPEC, VMEM_SPEC] + [HBM_SPEC] * 7,
        out_specs=[VMEM_SPEC] * 4 + [HBM_SPEC] * 2 + [VMEM_SPEC] * 2 + [HBM_SPEC] * 6,
        scratch_shapes=[
            pltpu.VMEM((frame_count, width), F32),
            pltpu.VMEM((frame_count, width), BF),
            pltpu.VMEM((frame_count, width), BF),
            pltpu.VMEM((frame_count, width), F32),
            pltpu.VMEM((frame_count, 128), BF),
            pltpu.VMEM((frame_count, 128), BF),
            pltpu.VMEM((2, frame_count, 128), BF),
            pltpu.VMEM((2, frame_count, 128), BF),
            pltpu.VMEM((2, frame_count, 256), BF),
            pltpu.VMEM(lead + (8, 256), F32),
            dma((3,)),
            dma((3, near - 1)),
            dma((3, near - 1)),
            dma((3,)),
            dma((3,)),
            dma((3, far - 1)),
            dma((3, far - 1)),
            dma((3, far - 1)),
            dma((3, far - 1)),
            dma((4,)),
            dma((4, far - 1)),
            dma((4, far - 1)),
            dma((4, near - 1)),
            dma((4, near - 1)),
            dma((4,)),
            dma((4,)),
            dma((2, 3)),
            dma((3,)),
        ],
        compiler_params=pltpu.CompilerParams(
            collective_id=2, has_side_effects=True, vmem_limit_bytes=VMEM_LIMIT
        ),
        name="gather_attend",
    )(lengths, x, *shards)


def feed_fused_kernel(
    n,
    lengths,
    middle,
    gout,
    mixed,
    wup,
    wdn,
    wo,
    table,
    bup,
    layer_out,
    gmid,
    dmixed,
    dwo,
    dwup,
    dwdn,
    columns,
    sums,
    sum_up,
    nb,
    act,
    gup,
    glow,
    gbl,
    *,
    tb,
):
    frame_count, width = middle.shape
    share = width // n
    finish = lengths[0, 0] + lengths[0, 1]
    gain, shift, bdn = (table[i : i + 1, :] for i in range(5, 8))
    sums[...] = jnp.zeros_like(sums)
    sum_up[...] = jnp.zeros_like(sum_up)

    def block(i, carry):
        r = rows(i * tb, tb)
        valid = lax.broadcasted_iota(jnp.int32, (tb, 1), 0) + i * tb < finish
        mid = middle[r, :]
        xhat, inv = normal_stats(mid)
        normed = (xhat * gain + shift).astype(BF)
        nb[r, :] = normed
        up = dot_nt(normed, wup[...]) + bup[0:1, :]
        cdf = 0.5 * (1.0 + lax.erf(up * (1.0 / math.sqrt(2.0))))
        low = (up * cdf).astype(BF)
        act[r, :] = low
        down = dot_nt(low, wdn[...]) + bdn
        layer_out[r, :] = jnp.where(valid, mid + down, 0.0).astype(BF)
        grow = jnp.where(valid, gout[r, :].astype(F32), 0.0)
        gl = grow.astype(BF)
        glow[r, :] = gl
        slope = cdf + up * jnp.exp(-0.5 * up * up) * (1.0 / math.sqrt(2.0 * math.pi))
        gu = (dot_nn(gl, wdn[...]) * slope).astype(BF)
        gup[r, :] = gu
        gn = dot_nn(gu, wup[...])
        scaled = gn * gain
        gm = grow + inv * (
            scaled
            - jnp.mean(scaled, axis=-1, keepdims=True)
            - xhat * jnp.mean(scaled * xhat, axis=-1, keepdims=True)
        )
        gmid[r, :] = gm
        gb = gm.astype(BF)
        gbl[r, :] = gb
        dmixed[r, :] = dot_nn(gb, wo[...]).astype(BF)
        sums[4:5, :] += jnp.sum(gb.astype(F32), axis=0, keepdims=True)
        sums[5:6, :] += jnp.sum(gn * xhat, axis=0, keepdims=True)
        sums[6:7, :] += jnp.sum(gn, axis=0, keepdims=True)
        sums[7:8, :] += jnp.sum(grow, axis=0, keepdims=True)
        sum_up[0:1, :] += jnp.sum(gu.astype(F32), axis=0, keepdims=True)
        return carry

    lax.fori_loop(0, frame_count // tb, block, 0)
    dwo[...] = dot_tn(gbl[...], mixed[...]).astype(BF)

    def weights(i, carry):
        c = rows(i * 512, 512)
        dwup[c, :] = dot_tn(gup[:, c], nb[...]).astype(BF)
        dwdn[:, c] = dot_tn(glow[...], act[:, c]).astype(BF)
        return carry

    lax.fori_loop(0, wup.shape[0] // 512, weights, 0)
    lane = lax.broadcasted_iota(jnp.int32, (1, 128), 1)
    plain = sums[...].T
    hidden = sum_up[...].T.reshape(n, 4, share, 8)
    found = jnp.zeros((width, 128), F32)
    for v in range(4, 8):
        found = jnp.where(lane == v, plain[:, v : v + 1], found)
    for k in range(4):
        piece = hidden[:, k].reshape(width, 8)
        found = jnp.where(lane == 8 + k, piece[:, 0:1], found)
    columns[...] = found


def feed_fused(n, lengths, middle, gout, mixed, wup, wdn, wo, table, bup):
    frame_count, width = middle.shape
    hidden = wup.shape[0]
    low = jax.ShapeDtypeStruct((frame_count, width), BF)
    return pl.pallas_call(
        functools.partial(feed_fused_kernel, n, tb=256),
        out_shape=[
            low,
            jax.ShapeDtypeStruct((frame_count, width), F32),
            low,
            jax.ShapeDtypeStruct((width, width), BF),
            jax.ShapeDtypeStruct((hidden, width), BF),
            jax.ShapeDtypeStruct((width, hidden), BF),
            jax.ShapeDtypeStruct((width, 128), F32),
        ],
        in_specs=[SMEM_SPEC] + [VMEM_SPEC] * 8,
        out_specs=[VMEM_SPEC] * 7,
        scratch_shapes=[
            pltpu.VMEM((8, width), F32),
            pltpu.VMEM((8, hidden), F32),
            pltpu.VMEM((frame_count, width), BF),
            pltpu.VMEM((frame_count, hidden), BF),
            pltpu.VMEM((frame_count, hidden), BF),
            pltpu.VMEM((frame_count, width), BF),
            pltpu.VMEM((frame_count, width), BF),
        ],
        compiler_params=pltpu.CompilerParams(vmem_limit_bytes=VMEM_LIMIT),
        name="feed_forward_both",
    )(lengths, middle, gout, mixed, wup, wdn, wo, table, bup)


def back_scatter_kernel(n, ub, lb, *refs):
    (lengths, x_h, gmid_h, nb_h, qaug_h, kk_h, vv_h, mixed_h, dmixed_h) = refs[:9]
    (wq, wk, wv, table, columns, po, pu, pd) = refs[9:17]
    (grad_h, gq, gk, gv, go, gu, gd, gc) = refs[17:25]
    (x, gmid, nb, qaug, kbuf, vbuf, mixed, dmixed, kaug, dq, dqb, dkt, dvt, sums, grad) = refs[25:40]
    (parts, core_in, core_sum, near_in, near_sum, far_in) = refs[40:46]
    (own2, core_in2, near_in2, near_sum2, far_in2) = (refs[46 + 3 * j : 49 + 3 * j] for j in range(5))
    (cparts, ccore_in, ccore_sum, cnear_in, cnear_sum, cfar_in) = refs[61:67]
    (in_sem, end_sem, core_s, core_r, near_s, near_r, far_s, far_r) = refs[67:75]
    (own2_sem, core2_s, core2_r, near2_s, near2_r, far2_s, far2_r) = refs[75:82]
    (ccore_s, ccore_r, cnear_s, cnear_r, cfar_s, cfar_r) = refs[82:]
    far, near = levels_of(n)
    frame_count, width = x.shape
    share = width // n
    pairs = HEADS // 2
    last = pairs - 1
    me = lax.axis_index("dp")
    top, mid, core = everyone_barrier(n, me, far, near)
    lane = lax.broadcasted_iota(jnp.int32, (1, 128), 1)

    def index(t, m, c):
        return (t * near + m) * 2 + c

    sibling = index(top, mid, 1 - core)
    big = (po, pu, pd)

    def own2_copy(a):
        return pltpu.make_async_copy(big[a].at[:, :, core], own2[a], own2_sem.at[a])

    def core2_copy(a):
        return remote(
            big[a].at[:, :, 1 - core], core_in2[a], core2_s.at[a], core2_r.at[a], sibling
        )

    def near2_copy(a, k):
        peer = lax.rem(mid + k, near)
        return remote(
            own2[a].at[:, peer],
            near_in2[a].at[k - 1],
            near2_s.at[a, k - 1],
            near2_r.at[a, k - 1],
            index(top, peer, core),
        )

    def far2_copy(a, k):
        peer = bits_differ(top, k, far)
        return remote(
            near_sum2[a].at[peer],
            far_in2[a].at[k - 1],
            far2_s.at[a, k - 1],
            far2_r.at[a, k - 1],
            index(peer, mid, core),
        )

    def core_copy(j):
        return remote(
            parts.at[j, :, :, 1 - core], core_in.at[j], core_s.at[j], core_r.at[j], sibling
        )

    def near_copy(j, k):
        peer = lax.rem(mid + k, near)
        return remote(
            core_sum.at[j, peer],
            near_in.at[j, k - 1],
            near_s.at[j, k - 1],
            near_r.at[j, k - 1],
            index(top, peer, core),
        )

    def far_copy(j):
        peer = index(bits_differ(top, last - j, far), mid, core)
        return remote(near_sum.at[j], far_in.at[j], far_s.at[j], far_r.at[j], peer)

    def add_core(j):
        for m in range(near):
            core_sum[j, m] = (
                parts[j, :, m, core].astype(F32) + core_in[j, :, m].astype(F32)
            ).astype(BF)

    def add_near(j):
        total = core_sum[j, mid].astype(F32)
        for k in range(near - 1):
            total = total + near_in[j, k].astype(F32)
        return total

    def in_copies(p, slot):
        cols = rows(p * 128, 128)
        wide = rows(p * 256, 256)
        return [
            pltpu.make_async_copy(qaug_h.at[:, wide], qaug.at[slot], in_sem.at[slot, 0]),
            pltpu.make_async_copy(kk_h.at[:, cols], kbuf.at[slot], in_sem.at[slot, 1]),
            pltpu.make_async_copy(vv_h.at[:, cols], vbuf.at[slot], in_sem.at[slot, 2]),
            pltpu.make_async_copy(mixed_h.at[:, cols], mixed.at[slot], in_sem.at[slot, 3]),
            pltpu.make_async_copy(dmixed_h.at[:, cols], dmixed.at[slot], in_sem.at[slot, 4]),
        ]

    end_copies = [
        pltpu.make_async_copy(nb_h, nb, end_sem.at[0]),
        pltpu.make_async_copy(x_h, x, end_sem.at[1]),
        pltpu.make_async_copy(gmid_h, gmid, end_sem.at[2]),
    ]
    for copy in in_copies(bits_differ(top, last, far), 0):
        copy.start()
    for a in range(3):
        core2_copy(a).start()
        own2_copy(a).start()
    for copy in end_copies:
        copy.start()

    def marks(i, carry):
        r = rows(i * lb, lb)
        position = lax.broadcasted_iota(jnp.int32, (lb, 128), 0) + i * lb
        lanes = lax.broadcasted_iota(jnp.int32, (lb, 128), 1)
        same = segment_lanes(lengths, position, lanes)
        slot = lax.rem(lanes, 64)
        kaug[r, :] = jnp.where(
            slot < 3, jnp.where(same, 0.0, EXCLUDED), jnp.where(slot < 6, 1.0, 0.0)
        ).astype(BF)
        return carry

    lax.fori_loop(0, frame_count // lb, marks, 0)
    end_copies[0].wait()

    def pair_step(i, carry):
        p = bits_differ(top, last - i, far)
        slot = lax.rem(i, 2)
        cols = rows(p * 128, 128)
        for copy in in_copies(p, slot):
            copy.wait()

        @pl.when(i < last)
        def _():
            for copy in in_copies(bits_differ(top, last - i - 1, far), 1 - slot):
                copy.start()

        grad_pair = dmixed[slot]
        product = grad_pair.astype(F32) * mixed[slot].astype(F32)
        for half in range(2):
            own = own_lanes(lane, half)
            base = 64 - 64 * half
            delta = jnp.sum(jnp.where(own, product, 0.0), axis=1, keepdims=True)
            high, middle_piece, low = three_pieces(-delta)
            grad_head = jnp.where(own, grad_pair, jnp.zeros((1, 128), BF))
            grad_head = jnp.where(lane == base + 3, high, grad_head)
            grad_head = jnp.where(lane == base + 4, middle_piece, grad_head)
            grad_head = jnp.where(lane == base + 5, low, grad_head)
            query = qaug[slot, :, 128 * half : 128 * half + 128]
            here = pl.ds(pl.multiple_of(p * 128 + 64 * half, 64), 64)
            part = slice(64 * half, 64 * half + 64)
            ones = jnp.where(
                (lane >= base + 3) & (lane < base + 6), jnp.ones((1, 128), F32), 0.0
            ).astype(BF)
            for j in range(frame_count // ub):
                r = pl.ds(j * ub, ub)
                pair_key = kbuf[slot, r, :]
                key = jnp.where(own, pair_key, kaug[r, :])
                value = jnp.where(own, vbuf[slot, r, :], ones)
                probs = jnp.exp(dot_nt(query, key))
                low_probs = probs.astype(BF)
                gs = (probs * dot_nt(grad_head, value)).astype(BF)
                dvt[here, r] = dot_tn(grad_head, low_probs)[part].astype(BF)
                dkt[here, r] = dot_tn(query, gs)[part].astype(BF)
                step = dot_nn(gs, pair_key)
                if j == 0:
                    dq[...] = step
                else:
                    dq[...] += step
            done = (dq[...] * 0.125).astype(BF)
            if half == 0:
                dqb[:, cols] = done

                @pl.when(i == 0)
                def _():
                    for a in range(3):
                        core2_copy(a).wait_recv()
                        own2_copy(a).wait()

                        def add(f, inner, a=a):
                            own2[a][f] = (
                                own2[a][f].astype(F32) + core_in2[a][f].astype(F32)
                            ).astype(BF)
                            return inner

                        lax.fori_loop(0, far, add, 0)
                        for k in range(1, near):
                            near2_copy(a, k).start()

                @pl.when(i > 0)
                def _():
                    core_copy(i - 1).wait_recv()
                    add_core(i - 1)
                    for k in range(1, near):
                        near_copy(i - 1, k).start()

            else:
                dqb[:, cols] = jnp.where(own, done, dqb[:, cols])

                @pl.when(i > 0)
                def _():
                    for k in range(1, near):
                        near_copy(i - 1, k).wait_recv()
                    near_sum[i - 1] = add_near(i - 1).astype(BF)
                    far_copy(i - 1).start()

                @pl.when(i == last - 1)
                def _():
                    for a in range(3):
                        for k in range(1, near):
                            near2_copy(a, k).wait_recv()

                        def add(f, inner, a=a):
                            total = own2[a][f, mid].astype(F32)
                            for k in range(near - 1):
                                total = total + near_in2[a][k, f].astype(F32)
                            near_sum2[a][f] = total.astype(BF)
                            return inner

                        lax.fori_loop(0, far, add, 0)
                        for k in range(1, far):
                            far2_copy(a, k).start()

        pair_rows = rows(p * 128, 128)
        shape = (near, 2, share, width)
        parts[i, 0] = dot_tn(dqb[:, cols], nb[...]).astype(BF).reshape(shape)
        parts[i, 1] = dot_nn(dkt[pair_rows, :], nb[...]).astype(BF).reshape(shape)
        parts[i, 2] = dot_nn(dvt[pair_rows, :], nb[...]).astype(BF).reshape(shape)
        core_copy(i).start()
        return carry

    lax.fori_loop(0, pairs, pair_step, 0)
    end_copies[1].wait()
    end_copies[2].wait()
    sums[...] = jnp.zeros_like(sums)
    gain = table[0:1, :]

    def finish(i, carry):
        r = rows(i * lb, lb)
        gn = dot_nn(dqb[r, :], wq[...]) + dot_tn(dkt[:, r], wk[...]) + dot_tn(dvt[:, r], wv[...])
        xhat, inv = normal_stats(x[r, :].astype(F32))
        scaled = gn * gain
        grad[r, :] = (
            gmid[r, :]
            + inv
            * (
                scaled
                - jnp.mean(scaled, axis=-1, keepdims=True)
                - xhat * jnp.mean(scaled * xhat, axis=-1, keepdims=True)
            )
        ).astype(BF)
        sums[0:1, :] += jnp.sum(gn * xhat, axis=0, keepdims=True)
        sums[1:2, :] += jnp.sum(gn, axis=0, keepdims=True)
        sums[2:3, :] += jnp.sum(dqb[r, :].astype(F32), axis=0, keepdims=True)

        @pl.when(i == 0)
        def _():
            core_copy(last).wait_recv()
            add_core(last)
            for k in range(1, near):
                near_copy(last, k).start()

        return carry

    lax.fori_loop(0, frame_count // lb, finish, 0)
    grad_copy = pltpu.make_async_copy(grad, grad_h, end_sem.at[3])
    grad_copy.start()
    sums[3:4, :] = dot_nt(jnp.ones((8, frame_count), BF), dvt[...])[0:1]

    plain = sums[...].T
    found = columns[...]
    for v in range(4):
        found = jnp.where(lane == v, plain[:, v : v + 1], found)
    cparts[...] = found.astype(BF).reshape(far, near, 2, share, 128)
    ccore = remote(cparts.at[:, :, 1 - core], ccore_in, ccore_s, ccore_r, sibling)
    ccore.start()
    for k in range(1, near):
        near_copy(last, k).wait_recv()
    total = add_near(last)
    for j in range(last):
        far_copy(j).wait_recv()
        total = total + far_in[j].astype(F32)
    gq[...] = total[0]
    gk[...] = total[1]
    gv[...] = total[2]
    ccore.wait_recv()
    for m in range(near):
        ccore_sum[m] = (cparts[:, m, core].astype(F32) + ccore_in[:, m].astype(F32)).astype(BF)
    cnear = []
    for k in range(1, near):
        peer = lax.rem(mid + k, near)
        cnear.append(
            remote(
                ccore_sum.at[peer],
                cnear_in.at[k - 1],
                cnear_s.at[k - 1],
                cnear_r.at[k - 1],
                index(top, peer, core),
            )
        )
        cnear[-1].start()
    for a, out in enumerate((go, gu, gd)):
        for k in range(1, far):
            far2_copy(a, k).wait_recv()
        total = near_sum2[a][top].astype(F32)
        for k in range(far - 1):
            total = total + far_in2[a][k].astype(F32)
        out[...] = total
    for copy in cnear:
        copy.wait_recv()
    total = ccore_sum[mid].astype(F32)
    for k in range(near - 1):
        total = total + cnear_in[k].astype(F32)
    cnear_sum[...] = total.astype(BF)
    cfar = []
    for k in range(1, far):
        peer = bits_differ(top, k, far)
        cfar.append(
            remote(
                cnear_sum.at[peer],
                cfar_in.at[k - 1],
                cfar_s.at[k - 1],
                cfar_r.at[k - 1],
                index(peer, mid, core),
            )
        )
        cfar[-1].start()
    for copy in cfar:
        copy.wait_recv()
    total = cnear_sum[top].astype(F32)
    for k in range(far - 1):
        total = total + cfar_in[k].astype(F32)
    gc[...] = total
    for a in range(3):
        core2_copy(a).wait_send()
        for k in range(1, near):
            near2_copy(a, k).wait_send()
        for k in range(1, far):
            far2_copy(a, k).wait_send()
    for j in range(pairs):
        core_copy(j).wait_send()
        for k in range(1, near):
            near_copy(j, k).wait_send()
        if j < last:
            far_copy(j).wait_send()
    ccore.wait_send()
    for copy in cnear + cfar:
        copy.wait_send()
    grad_copy.wait()


def back_scatter(n, lengths, x, gmid, nb, qaug, kk, vv, mixed, dmixed, weights, table, columns, big):
    far, near = levels_of(n)
    frame_count, width = x.shape
    share = width // n
    pairs = HEADS // 2
    blocks = [p.shape[3:] for p in big]
    row_block = jax.ShapeDtypeStruct((share, width), F32)
    dma = pltpu.SemaphoreType.DMA
    return pl.pallas_call(
        functools.partial(back_scatter_kernel, n, 512, 512),
        out_shape=[
            jax.ShapeDtypeStruct((frame_count, width), BF),
            row_block,
            row_block,
            row_block,
        ]
        + [jax.ShapeDtypeStruct(b, F32) for b in blocks]
        + [jax.ShapeDtypeStruct((share, 128), F32)],
        in_specs=[SMEM_SPEC] + [HBM_SPEC] * 8 + [VMEM_SPEC] * 5 + [HBM_SPEC] * 3,
        out_specs=[HBM_SPEC] + [VMEM_SPEC] * 7,
        scratch_shapes=[
            pltpu.VMEM((frame_count, width), BF),
            pltpu.VMEM((frame_count, width), F32),
            pltpu.VMEM((frame_count, width), BF),
            pltpu.VMEM((2, frame_count, 256), BF),
            pltpu.VMEM((2, frame_count, 128), BF),
            pltpu.VMEM((2, frame_count, 128), BF),
            pltpu.VMEM((2, frame_count, 128), BF),
            pltpu.VMEM((2, frame_count, 128), BF),
            pltpu.VMEM((frame_count, 128), BF),
            pltpu.VMEM((frame_count, 128), F32),
            pltpu.VMEM((frame_count, width), BF),
            pltpu.VMEM((width, frame_count), BF),
            pltpu.VMEM((width, frame_count), BF),
            pltpu.VMEM((8, width), F32),
            pltpu.VMEM((frame_count, width), BF),
            pltpu.VMEM((pairs, 3, near, 2, share, width), BF),
            pltpu.VMEM((pairs, 3, near, share, width), BF),
            pltpu.VMEM((pairs, near, 3, share, width), BF),
            pltpu.VMEM((pairs, near - 1, 3, share, width), BF),
            pltpu.VMEM((pairs, 3, share, width), BF),
            pltpu.VMEM((pairs - 1, 3, share, width), BF),
        ]
        + [pltpu.VMEM((far, near) + b, BF) for b in blocks]
        + [pltpu.VMEM((far, near) + b, BF) for b in blocks]
        + [pltpu.VMEM((near - 1, far) + b, BF) for b in blocks]
        + [pltpu.VMEM((far,) + b, BF) for b in blocks]
        + [pltpu.VMEM((far - 1,) + b, BF) for b in blocks]
        + [
            pltpu.VMEM((far, near, 2, share, 128), BF),
            pltpu.VMEM((far, near, share, 128), BF),
            pltpu.VMEM((near, far, share, 128), BF),
            pltpu.VMEM((near - 1, far, share, 128), BF),
            pltpu.VMEM((far, share, 128), BF),
            pltpu.VMEM((far - 1, share, 128), BF),
            dma((2, 5)),
            dma((4,)),
            dma((pairs,)),
            dma((pairs,)),
            dma((pairs, near - 1)),
            dma((pairs, near - 1)),
            dma((pairs,)),
            dma((pairs,)),
            dma((3,)),
            dma((3,)),
            dma((3,)),
            dma((3, near - 1)),
            dma((3, near - 1)),
            dma((3, far - 1)),
            dma((3, far - 1)),
            dma,
            dma,
            dma((near - 1,)),
            dma((near - 1,)),
            dma((far - 1,)),
            dma((far - 1,)),
        ],
        compiler_params=pltpu.CompilerParams(
            collective_id=3, has_side_effects=True, vmem_limit_bytes=VMEM_LIMIT
        ),
        name="back_scatter",
    )(lengths, x, gmid, nb, qaug, kk, vv, mixed, dmixed, *weights, table, columns, *big)


def hand_out_kernel(*refs):
    ins, outs = refs[:7], refs[7:]
    for a in range(6):
        outs[a][...] = ins[a][...]
    turned = ins[6][...].T
    for v in range(8):
        outs[6 + v][...] = turned[v : v + 1, :]
    outs[14][...] = turned[8:12, :]


def hand_out(totals):
    share = totals[0].shape[0]
    line = jax.ShapeDtypeStruct((1, share), F32)
    return pl.pallas_call(
        hand_out_kernel,
        out_shape=[jax.ShapeDtypeStruct(t.shape, F32) for t in totals[:6]]
        + [line] * 8
        + [jax.ShapeDtypeStruct((4, share), F32)],
        in_specs=[VMEM_SPEC] * 7,
        out_specs=[VMEM_SPEC] * 15,
        compiler_params=pltpu.CompilerParams(vmem_limit_bytes=8 << 20),
        name="hand_out",
    )(*totals)


def per_device_fused(n, frames, lengths, vectors, up_bias, weights, grad_out):
    width = frames.shape[2]
    packed = jnp.concatenate(vectors + (up_bias,)).astype(F32)
    packed = jnp.broadcast_to(jnp.pad(packed, (0, 256 - packed.shape[0]))[None], (8, 256))
    x = frames[0]
    got = gather_attend(n, lengths, x, tuple(w.T for w in weights) + (packed,))
    wq, wk, wv, wo, wup, wdn = (w.reshape(n * w.shape[3], w.shape[4]) for w in got[:6])
    table, bup, kk, vv, qaug, nb, mixed, middle = got[6:]
    layer_out, gmid, dmixed, dwo, dwup, dwdn, columns = feed_fused(
        n, lengths, middle, grad_out[0], mixed, wup, wdn, wo, table, bup
    )
    far, near = levels_of(n)

    def split(g):
        return g.reshape(far, near, 2, g.shape[0] // n, g.shape[1])

    sums = back_scatter(
        n,
        lengths,
        x,
        gmid,
        nb,
        qaug,
        kk,
        vv,
        mixed,
        dmixed,
        (wq, wk, wv),
        table,
        columns,
        (split(dwo), split(dwup), split(dwdn)),
    )
    outs = hand_out(sums[1:])
    gq, gk, gv, go, gu, gd = (g.T for g in outs[:6])
    line = [v.reshape(-1) for v in outs[6:14]]
    return (
        layer_out[None],
        sums[0][None],
        line[0],
        line[1],
        gq,
        line[2],
        gk,
        gv,
        line[3],
        go,
        line[4],
        line[5],
        line[6],
        gu,
        outs[14].reshape(-1),
        gd,
        line[7],
    )


def per_device(
    n,
    frames,
    lengths,
    attn_gain,
    attn_shift,
    query_weight,
    query_bias,
    key_weight,
    value_weight,
    value_bias,
    out_weight,
    out_bias,
    mlp_gain,
    mlp_shift,
    up_weight,
    up_bias,
    down_weight,
    down_bias,
    grad_out,
):
    slots, frame_count, width = frames.shape
    assert slots == 1
    share = width // n
    vectors = (
        attn_gain,
        attn_shift,
        query_bias,
        value_bias,
        out_bias,
        mlp_gain,
        mlp_shift,
        down_bias,
    )
    far, near = levels_of(n)
    if share % 16 == 0 and far == HEADS // 2:
        return per_device_fused(
            n,
            frames,
            lengths,
            vectors,
            up_bias,
            (query_weight, key_weight, value_weight, out_weight, up_weight, down_weight),
            grad_out,
        )
    packed = jnp.concatenate(
        [jnp.stack(vectors, axis=1), up_bias.reshape(share, 4), jnp.zeros((share, 116), BF)], axis=1
    )
    shards = (
        query_weight.T,
        key_weight.T,
        value_weight.T,
        out_weight.T,
        up_weight.T,
        down_weight.T,
        packed,
    )
    full = gather_all(n, shards)
    wq, wk, wv, wo, wup, wdn, vec = (
        f.reshape(n * f.shape[3], f.shape[4]) for f in full
    )
    bup = vec[:, 8:12].reshape(1, 4 * width)
    x = frames[0]
    nb, qaug, kk, vv, mixed, middle, kaug = attend(lengths, x, wq, wk, wv, wo, vec)
    layer_out, gmid, dmixed, dwo, dwup, dwdn, sums_two, sum_up = feed(
        lengths, middle, grad_out[0], mixed, wup, wdn, wo, vec, bup
    )
    grad_x, dwq, dwk, dwv, sums_one = attend_back(
        x, gmid, nb, qaug, kk, vv, mixed, dmixed, kaug, wq, wk, wv, vec
    )
    columns = jnp.concatenate(
        [
            sums_one[:4].T,
            sums_two[:4].T,
            sum_up[0].reshape(width, 4),
            jnp.zeros((width, 116), F32),
        ],
        axis=1,
    ).astype(BF)

    def split(g):
        return g.reshape(far, near, 2, g.shape[0] // n, g.shape[1])

    gq, gk, gv, go, gu, gd, gc = scatter_all(
        n, tuple(split(g) for g in (dwq, dwk, dwv, dwo, dwup, dwdn, columns))
    )
    return (
        layer_out[None],
        grad_x[None],
        gc[:, 0],
        gc[:, 1],
        gq.T,
        gc[:, 2],
        gk.T,
        gv.T,
        gc[:, 3],
        go.T,
        gc[:, 4],
        gc[:, 5],
        gc[:, 6],
        gu.T,
        gc[:, 8:12].reshape(4 * share),
        gd.T,
        gc[:, 7],
    )


def solution(mesh):
    row, col, vector = P("dp", None, None), P(None, "dp"), P("dp")
    return jax.shard_map(
        functools.partial(per_device, mesh.shape["dp"]),
        mesh=mesh,
        in_specs=(
            row,
            P("dp", None),
            vector,
            vector,
            col,
            vector,
            col,
            col,
            vector,
            col,
            vector,
            vector,
            vector,
            col,
            vector,
            col,
            vector,
            row,
        ),
        out_specs=(
            row,
            row,
            vector,
            vector,
            col,
            vector,
            col,
            col,
            vector,
            col,
            vector,
            vector,
            vector,
            col,
            vector,
            col,
            vector,
        ),
        check_vma=False,
    )
```

```python
import functools
import math

import jax
import jax.numpy as jnp
from jax import lax
from jax.experimental import pallas as pl
from jax.experimental.pallas import tpu as pltpu
from jax.sharding import PartitionSpec as P

HEADS = 8
EPS = 1e-05
MESH = pl.DeviceIdType.MESH
F32 = jnp.float32
BF = jnp.bfloat16
VMEM_SPEC = pl.BlockSpec(memory_space=pltpu.VMEM)
SMEM_SPEC = pl.BlockSpec(memory_space=pltpu.SMEM)
HBM_SPEC = pl.BlockSpec(memory_space=pl.ANY)
EXCLUDED = -1e30
VMEM_LIMIT = 62 << 20


def dot_nn(a, b):
    return lax.dot_general(a, b, (((1,), (0,)), ((), ())), preferred_element_type=F32)


def dot_nt(a, b):
    return lax.dot_general(a, b, (((1,), (1,)), ((), ())), preferred_element_type=F32)


def dot_tn(a, b):
    return lax.dot_general(a, b, (((0,), (0,)), ((), ())), preferred_element_type=F32)


def levels_of(n):
    rest = n // 2
    bits = rest.bit_length() - 1
    near = 2 ** ((bits + 1) // 2)
    return rest // near, near


def rows(start, size):
    return pl.ds(pl.multiple_of(start, size), size)


def normal_stats(block):
    mean = jnp.mean(block, axis=-1, keepdims=True)
    centered = block - mean
    inv = lax.rsqrt(jnp.mean(centered * centered, axis=-1, keepdims=True) + EPS)
    return centered * inv, inv


def announce(n, me, far, near):
    barrier = pltpu.get_barrier_semaphore()
    core = lax.rem(me, 2)
    mid = lax.rem(me // 2, near)
    top = me // (2 * near)
    peers = [(lax.rem(top + k, far) * near + mid) * 2 + core for k in range(1, far)]
    peers += [(top * near + lax.rem(mid + k, near)) * 2 + core for k in range(1, near)]
    peers += [(top * near + mid) * 2 + 1 - core]
    for peer in peers:
        pl.semaphore_signal(barrier, inc=1, device_id=(peer,), device_id_type=MESH)
    return top, mid, core


def await_peers(far, near):
    pl.semaphore_wait(pltpu.get_barrier_semaphore(), far + near - 1)


def everyone_barrier(n, me, far, near):
    place = announce(n, me, far, near)
    await_peers(far, near)
    return place


def gather_kernel(n, count, *refs):
    shards, outs = refs[:count], refs[count : 2 * count]
    own_sem, far_s, far_r, near_s, near_r, core_s, core_r = refs[2 * count :]
    far, near = levels_of(n)
    me = lax.axis_index("dp")
    top, mid, core = everyone_barrier(n, me, far, near)

    def index(t, m, c):
        return (t * near + m) * 2 + c

    far_copies, near_copies = {}, {}
    for a in range(count):
        for k in range(1, far):
            copy = pltpu.make_async_remote_copy(
                src_ref=shards[a],
                dst_ref=outs[a].at[top, mid, core],
                send_sem=far_s.at[a, k - 1],
                recv_sem=far_r.at[a, k - 1],
                device_id=(index(lax.rem(top + k, far), mid, core),),
                device_id_type=MESH,
            )
            copy.start()
            far_copies[a, k] = copy
        pltpu.make_async_copy(shards[a], outs[a].at[top, mid, core], own_sem.at[a]).start()
    for a in range(count):
        pltpu.make_async_copy(shards[a], outs[a].at[top, mid, core], own_sem.at[a]).wait()
        for k in range(1, far):
            far_copies[a, k].wait_recv()
        for k in range(1, near):
            copy = pltpu.make_async_remote_copy(
                src_ref=outs[a].at[:, mid, core],
                dst_ref=outs[a].at[:, mid, core],
                send_sem=near_s.at[a, k - 1],
                recv_sem=near_r.at[a, k - 1],
                device_id=(index(top, lax.rem(mid + k, near), core),),
                device_id_type=MESH,
            )
            copy.start()
            near_copies[a, k] = copy
    core_copies = []
    for a in range(count):
        for k in range(1, near):
            near_copies[a, k].wait_recv()
        copy = pltpu.make_async_remote_copy(
            src_ref=outs[a].at[:, :, core],
            dst_ref=outs[a].at[:, :, core],
            send_sem=core_s.at[a],
            recv_sem=core_r.at[a],
            device_id=(index(top, mid, 1 - core),),
            device_id_type=MESH,
        )
        copy.start()
        core_copies.append(copy)
    for a in range(count):
        core_copies[a].wait_recv()
    for a in range(count):
        for k in range(1, far):
            far_copies[a, k].wait_send()
        for k in range(1, near):
            near_copies[a, k].wait_send()
        core_copies[a].wait_send()


def gather_all(n, shards):
    far, near = levels_of(n)
    count = len(shards)
    return pl.pallas_call(
        functools.partial(gather_kernel, n, count),
        out_shape=[jax.ShapeDtypeStruct((far, near, 2) + s.shape, s.dtype) for s in shards],
        in_specs=[VMEM_SPEC] * count,
        out_specs=[HBM_SPEC] * count,
        scratch_shapes=[
            pltpu.SemaphoreType.DMA((count,)),
            pltpu.SemaphoreType.DMA((count, far - 1)),
            pltpu.SemaphoreType.DMA((count, far - 1)),
            pltpu.SemaphoreType.DMA((count, near - 1)),
            pltpu.SemaphoreType.DMA((count, near - 1)),
            pltpu.SemaphoreType.DMA((count,)),
            pltpu.SemaphoreType.DMA((count,)),
        ],
        compiler_params=pltpu.CompilerParams(
            collective_id=0, has_side_effects=True, vmem_limit_bytes=32 << 20
        ),
        name="gather_params",
    )(*shards)


def scatter_kernel(n, count, *refs):
    parts, outs = refs[:count], refs[count : 2 * count]
    pos = 2 * count
    core_in, core_sum = refs[pos : pos + count], refs[pos + count : pos + 2 * count]
    pos += 2 * count
    near_in, near_sum = refs[pos : pos + count], refs[pos + count : pos + 2 * count]
    pos += 2 * count
    far_in = refs[pos : pos + count]
    core_s, core_r, near_s, near_r, far_s, far_r = refs[pos + count :]
    far, near = levels_of(n)
    me = lax.axis_index("dp")
    top, mid, core = everyone_barrier(n, me, far, near)

    def index(t, m, c):
        return (t * near + m) * 2 + c

    core_copies, near_copies, far_copies = [], {}, {}
    for a in range(count):
        copy = pltpu.make_async_remote_copy(
            src_ref=parts[a].at[:, :, 1 - core],
            dst_ref=core_in[a],
            send_sem=core_s.at[a],
            recv_sem=core_r.at[a],
            device_id=(index(top, mid, 1 - core),),
            device_id_type=MESH,
        )
        copy.start()
        core_copies.append(copy)
    for a in range(count):
        core_copies[a].wait_recv()

        def add_core(i, carry, a=a):
            f, m = i // near, lax.rem(i, near)
            core_sum[a][m, f] = (
                parts[a][f, m, core].astype(F32) + core_in[a][f, m].astype(F32)
            ).astype(BF)
            return carry

        lax.fori_loop(0, far * near, add_core, 0)
        for k in range(1, near):
            peer = lax.rem(mid + k, near)
            copy = pltpu.make_async_remote_copy(
                src_ref=core_sum[a].at[peer],
                dst_ref=near_in[a].at[k - 1],
                send_sem=near_s.at[a, k - 1],
                recv_sem=near_r.at[a, k - 1],
                device_id=(index(top, peer, core),),
                device_id_type=MESH,
            )
            copy.start()
            near_copies[a, k] = copy
    for a in range(count):
        for k in range(1, near):
            near_copies[a, k].wait_recv()

        def add_near(f, carry, a=a):
            total = core_sum[a][mid, f].astype(F32)
            for k in range(near - 1):
                total = total + near_in[a][k, f].astype(F32)
            near_sum[a][f] = total.astype(BF)
            return carry

        lax.fori_loop(0, far, add_near, 0)
        for k in range(1, far):
            peer = lax.rem(top + k, far)
            copy = pltpu.make_async_remote_copy(
                src_ref=near_sum[a].at[peer],
                dst_ref=far_in[a].at[k - 1],
                send_sem=far_s.at[a, k - 1],
                recv_sem=far_r.at[a, k - 1],
                device_id=(index(peer, mid, core),),
                device_id_type=MESH,
            )
            copy.start()
            far_copies[a, k] = copy
    for a in range(count):
        for k in range(1, far):
            far_copies[a, k].wait_recv()
        total = near_sum[a][top].astype(F32)
        for k in range(far - 1):
            total = total + far_in[a][k].astype(F32)
        outs[a][...] = total
    for a in range(count):
        core_copies[a].wait_send()
        for k in range(1, near):
            near_copies[a, k].wait_send()
        for k in range(1, far):
            far_copies[a, k].wait_send()


def scatter_all(n, parts):
    far, near = levels_of(n)
    count = len(parts)
    blocks = [p.shape[3:] for p in parts]
    return pl.pallas_call(
        functools.partial(scatter_kernel, n, count),
        out_shape=[jax.ShapeDtypeStruct(b, F32) for b in blocks],
        in_specs=[VMEM_SPEC] * count,
        out_specs=[VMEM_SPEC] * count,
        scratch_shapes=[pltpu.VMEM((far, near) + b, BF) for b in blocks]
        + [pltpu.VMEM((near, far) + b, BF) for b in blocks]
        + [pltpu.VMEM((near - 1, far) + b, BF) for b in blocks]
        + [pltpu.VMEM((far,) + b, BF) for b in blocks]
        + [pltpu.VMEM((far - 1,) + b, BF) for b in blocks]
        + [
            pltpu.SemaphoreType.DMA((count,)),
            pltpu.SemaphoreType.DMA((count,)),
            pltpu.SemaphoreType.DMA((count, near - 1)),
            pltpu.SemaphoreType.DMA((count, near - 1)),
            pltpu.SemaphoreType.DMA((count, far - 1)),
            pltpu.SemaphoreType.DMA((count, far - 1)),
        ],
        compiler_params=pltpu.CompilerParams(
            collective_id=1, has_side_effects=True, vmem_limit_bytes=VMEM_LIMIT
        ),
        name="scatter_grads",
    )(*parts)


def segment_lanes(lengths, position, lane):
    leading = lengths[0, 0]
    finish = leading + lengths[0, 1]
    segment = jnp.where(position < leading, 0, jnp.where(position < finish, 1, 2))
    return lax.rem(lane, 64) == segment


def three_pieces(column):
    high = column.astype(BF)
    rest = column - high.astype(F32)
    middle = rest.astype(BF)
    return high, middle, (rest - middle.astype(F32)).astype(BF)


def own_lanes(lane, half):
    return (lane < 64) if half == 0 else (lane >= 64)


def attend_kernel(
    lengths, x, wq, wk, wv, wo, vec, nb, qaug, kk, vv, mixed, middle, kaug, qbuf, *, tb, lb
):
    frame_count = x.shape[0]
    lane = lax.broadcasted_iota(jnp.int32, (1, 128), 1)
    table = vec[...].astype(F32).T
    gain, shift, bq, bv, bo = (table[i : i + 1] for i in range(5))

    def project(i, carry):
        r = rows(i * lb, lb)
        xhat, _ = normal_stats(x[r, :].astype(F32))
        normed = (xhat * gain + shift).astype(BF)
        nb[r, :] = normed
        qbuf[r, :] = ((dot_nt(normed, wq[...]) + bq).astype(BF).astype(F32) * 0.125).astype(BF)
        kk[r, :] = dot_nt(normed, wk[...]).astype(BF)
        vv[r, :] = (dot_nt(normed, wv[...]) + bv).astype(BF)
        position = lax.broadcasted_iota(jnp.int32, (lb, 128), 0) + i * lb
        lanes = lax.broadcasted_iota(jnp.int32, (lb, 128), 1)
        same = segment_lanes(lengths, position, lanes)
        slot = lax.rem(lanes, 64)
        kaug[r, :] = jnp.where(
            slot < 3, jnp.where(same, 0.0, EXCLUDED), jnp.where(slot < 6, 1.0, 0.0)
        ).astype(BF)
        return carry

    lax.fori_loop(0, frame_count // lb, project, 0)

    def pair_step(p, carry):
        cols = rows(p * 128, 128)
        for half in range(2):
            own = own_lanes(lane, half)
            base = 64 - 64 * half
            key = jnp.where(own, kk[:, cols], kaug[...])
            value = jnp.where(own, vv[:, cols], jnp.ones((1, 128), BF))
            head = pl.multiple_of((2 * p + half) * 128, 128)

            def block(i, inner, half=half, own=own, base=base, key=key, value=value, head=head):
                r = rows(i * tb, tb)
                position = lax.broadcasted_iota(jnp.int32, (tb, 128), 0) + i * tb
                lanes = lax.broadcasted_iota(jnp.int32, (tb, 128), 1)
                mark = jnp.where(segment_lanes(lengths, position, lanes), 1.0, 0.0).astype(BF)
                query = jnp.where(own, qbuf[r, cols], mark)
                scores = dot_nt(query, key)
                top = jnp.max(scores, axis=1, keepdims=True)
                raised = jnp.exp(scores - top).astype(BF)
                got = dot_nn(raised, value)
                total = got[:, base : base + 1]
                got = (got * (1.0 / total)).astype(BF)
                if half == 0:
                    mixed[r, cols] = got
                else:
                    mixed[r, cols] = jnp.where(own, got, mixed[r, cols])
                high, mid, low = three_pieces(-(top + jnp.log(total)))
                query = jnp.where(lane == base + 3, high, query)
                query = jnp.where(lane == base + 4, mid, query)
                qaug[r, pl.ds(head, 128)] = jnp.where(lane == base + 5, low, query)
                return inner

            lax.fori_loop(0, frame_count // tb, block, 0, unroll=True)
        return carry

    lax.fori_loop(0, HEADS // 2, pair_step, 0)

    def finish(i, carry):
        r = rows(i * lb, lb)
        middle[r, :] = x[r, :].astype(F32) + (dot_nt(mixed[r, :], wo[...]) + bo)
        return carry

    lax.fori_loop(0, frame_count // lb, finish, 0)


def attend(lengths, x, wq, wk, wv, wo, vec):
    frame_count, width = x.shape
    low = jax.ShapeDtypeStruct((frame_count, width), BF)
    return pl.pallas_call(
        functools.partial(attend_kernel, tb=512, lb=512),
        out_shape=[
            low,
            jax.ShapeDtypeStruct((frame_count, HEADS * 128), BF),
            low,
            low,
            low,
            jax.ShapeDtypeStruct((frame_count, width), F32),
            jax.ShapeDtypeStruct((frame_count, 128), BF),
        ],
        in_specs=[SMEM_SPEC] + [VMEM_SPEC] * 6,
        out_specs=[VMEM_SPEC] * 7,
        scratch_shapes=[pltpu.VMEM((frame_count, width), BF)],
        compiler_params=pltpu.CompilerParams(vmem_limit_bytes=VMEM_LIMIT),
        name="attend_forward",
    )(lengths, x, wq, wk, wv, wo, vec)


def feed_kernel(
    lengths,
    middle,
    gout,
    mixed,
    wup,
    wdn,
    wo,
    vec,
    bup,
    layer_out,
    gmid,
    dmixed,
    dwo,
    dwup,
    dwdn,
    sums,
    sum_up,
    nb,
    act,
    gup,
    glow,
    gbl,
    *,
    tb,
):
    frame_count = middle.shape[0]
    finish = lengths[0, 0] + lengths[0, 1]
    table = vec[...].astype(F32).T
    gain, shift, bdn = (table[i : i + 1] for i in range(5, 8))
    sums[...] = jnp.zeros_like(sums)
    sum_up[...] = jnp.zeros_like(sum_up)

    def block(i, carry):
        r = rows(i * tb, tb)
        valid = lax.broadcasted_iota(jnp.int32, (tb, 1), 0) + i * tb < finish
        mid = middle[r, :]
        xhat, inv = normal_stats(mid)
        normed = (xhat * gain + shift).astype(BF)
        nb[r, :] = normed
        up = dot_nt(normed, wup[...]) + bup[...].astype(F32)
        cdf = 0.5 * (1.0 + lax.erf(up * (1.0 / math.sqrt(2.0))))
        low = (up * cdf).astype(BF)
        act[r, :] = low
        down = dot_nt(low, wdn[...]) + bdn
        layer_out[r, :] = jnp.where(valid, mid + down, 0.0).astype(BF)
        grow = jnp.where(valid, gout[r, :].astype(F32), 0.0)
        gl = grow.astype(BF)
        glow[r, :] = gl
        slope = cdf + up * jnp.exp(-0.5 * up * up) * (1.0 / math.sqrt(2.0 * math.pi))
        gu = (dot_nn(gl, wdn[...]) * slope).astype(BF)
        gup[r, :] = gu
        gn = dot_nn(gu, wup[...])
        scaled = gn * gain
        gm = grow + inv * (
            scaled
            - jnp.mean(scaled, axis=-1, keepdims=True)
            - xhat * jnp.mean(scaled * xhat, axis=-1, keepdims=True)
        )
        gmid[r, :] = gm
        gb = gm.astype(BF)
        gbl[r, :] = gb
        dmixed[r, :] = dot_nn(gb, wo[...]).astype(BF)
        sums[0:1, :] += jnp.sum(gb.astype(F32), axis=0, keepdims=True)
        sums[1:2, :] += jnp.sum(gn * xhat, axis=0, keepdims=True)
        sums[2:3, :] += jnp.sum(gn, axis=0, keepdims=True)
        sums[3:4, :] += jnp.sum(grow, axis=0, keepdims=True)
        sum_up[0:1, :] += jnp.sum(gu.astype(F32), axis=0, keepdims=True)
        return carry

    lax.fori_loop(0, frame_count // tb, block, 0)
    dwo[...] = dot_tn(gbl[...], mixed[...]).astype(BF)

    def weights(i, carry):
        c = rows(i * 512, 512)
        dwup[c, :] = dot_tn(gup[:, c], nb[...]).astype(BF)
        dwdn[:, c] = dot_tn(glow[...], act[:, c]).astype(BF)
        return carry

    lax.fori_loop(0, wup.shape[0] // 512, weights, 0)


def feed(lengths, middle, gout, mixed, wup, wdn, wo, vec, bup):
    frame_count, width = middle.shape
    hidden = wup.shape[0]
    low = jax.ShapeDtypeStruct((frame_count, width), BF)
    return pl.pallas_call(
        functools.partial(feed_kernel, tb=256),
        out_shape=[
            low,
            jax.ShapeDtypeStruct((frame_count, width), F32),
            low,
            jax.ShapeDtypeStruct((width, width), BF),
            jax.ShapeDtypeStruct((hidden, width), BF),
            jax.ShapeDtypeStruct((width, hidden), BF),
            jax.ShapeDtypeStruct((8, width), F32),
            jax.ShapeDtypeStruct((8, hidden), F32),
        ],
        in_specs=[SMEM_SPEC] + [VMEM_SPEC] * 8,
        out_specs=[VMEM_SPEC] * 8,
        scratch_shapes=[
            pltpu.VMEM((frame_count, width), BF),
            pltpu.VMEM((frame_count, hidden), BF),
            pltpu.VMEM((frame_count, hidden), BF),
            pltpu.VMEM((frame_count, width), BF),
            pltpu.VMEM((frame_count, width), BF),
        ],
        compiler_params=pltpu.CompilerParams(vmem_limit_bytes=VMEM_LIMIT),
        name="feed_forward_both",
    )(lengths, middle, gout, mixed, wup, wdn, wo, vec, bup)


def attend_back_kernel(
    x,
    gmid,
    nb,
    qaug,
    kk,
    vv,
    mixed,
    dmixed,
    kaug,
    wq,
    wk,
    wv,
    vec,
    grad_x,
    dwq,
    dwk,
    dwv,
    sums,
    dq,
    dqb,
    dkt,
    dvt,
    *,
    ub,
    lb,
):
    frame_count = x.shape[0]
    lane = lax.broadcasted_iota(jnp.int32, (1, 128), 1)
    gain = vec[...].astype(F32).T[0:1]

    def pair_step(p, carry):
        cols = rows(p * 128, 128)
        grad_pair = dmixed[:, cols]
        product = grad_pair.astype(F32) * mixed[:, cols].astype(F32)
        for half in range(2):
            own = own_lanes(lane, half)
            base = 64 - 64 * half
            delta = jnp.sum(jnp.where(own, product, 0.0), axis=1, keepdims=True)
            high, mid, low = three_pieces(-delta)
            grad = jnp.where(own, grad_pair, jnp.zeros((1, 128), BF))
            grad = jnp.where(lane == base + 3, high, grad)
            grad = jnp.where(lane == base + 4, mid, grad)
            grad = jnp.where(lane == base + 5, low, grad)
            query = qaug[:, pl.ds(pl.multiple_of((2 * p + half) * 128, 128), 128)]
            here = pl.ds(pl.multiple_of(p * 128 + 64 * half, 64), 64)
            part = slice(64 * half, 64 * half + 64)
            ones = jnp.where(
                (lane >= base + 3) & (lane < base + 6), jnp.ones((1, 128), F32), 0.0
            ).astype(BF)

            def block(i, inner):
                r = rows(i * ub, ub)
                key = jnp.where(own, kk[r, cols], kaug[r, :])
                value = jnp.where(own, vv[r, cols], ones)
                probs = jnp.exp(dot_nt(query, key))
                low_probs = probs.astype(BF)
                gs = (probs * dot_nt(grad, value)).astype(BF)
                dvt[here, r] = dot_tn(grad, low_probs)[part].astype(BF)
                dkt[here, r] = dot_tn(query, gs)[part].astype(BF)
                step = dot_nn(gs, kk[r, cols])
                if i == 0:
                    dq[...] = step
                else:
                    dq[...] += step
                return inner

            for i in range(frame_count // ub):
                block(i, 0)
            done = (dq[...] * 0.125).astype(BF)
            if half == 0:
                dqb[:, cols] = done
            else:
                dqb[:, cols] = jnp.where(own, done, dqb[:, cols])
        return carry

    lax.fori_loop(0, HEADS // 2, pair_step, 0)
    sums[...] = jnp.zeros_like(sums)

    def finish(i, carry):
        r = rows(i * lb, lb)
        gn = dot_nn(dqb[r, :], wq[...]) + dot_tn(dkt[:, r], wk[...]) + dot_tn(dvt[:, r], wv[...])
        xhat, inv = normal_stats(x[r, :].astype(F32))
        scaled = gn * gain
        grad_x[r, :] = (
            gmid[r, :]
            + inv
            * (
                scaled
                - jnp.mean(scaled, axis=-1, keepdims=True)
                - xhat * jnp.mean(scaled * xhat, axis=-1, keepdims=True)
            )
        ).astype(BF)
        sums[0:1, :] += jnp.sum(gn * xhat, axis=0, keepdims=True)
        sums[1:2, :] += jnp.sum(gn, axis=0, keepdims=True)
        sums[2:3, :] += jnp.sum(dqb[r, :].astype(F32), axis=0, keepdims=True)
        return carry

    lax.fori_loop(0, frame_count // lb, finish, 0)
    sums[3:4, :] = dot_nt(jnp.ones((8, frame_count), BF), dvt[...])[0:1]
    dwq[...] = dot_tn(dqb[...], nb[...]).astype(BF)
    dwk[...] = dot_nn(dkt[...], nb[...]).astype(BF)
    dwv[...] = dot_nn(dvt[...], nb[...]).astype(BF)


def attend_back(x, gmid, nb, qaug, kk, vv, mixed, dmixed, kaug, wq, wk, wv, vec):
    frame_count, width = x.shape
    square = jax.ShapeDtypeStruct((width, width), BF)
    return pl.pallas_call(
        functools.partial(attend_back_kernel, ub=512, lb=512),
        out_shape=[
            jax.ShapeDtypeStruct((frame_count, width), BF),
            square,
            square,
            square,
            jax.ShapeDtypeStruct((8, width), F32),
        ],
        in_specs=[VMEM_SPEC] * 13,
        out_specs=[VMEM_SPEC] * 5,
        scratch_shapes=[
            pltpu.VMEM((frame_count, 128), F32),
            pltpu.VMEM((frame_count, width), BF),
            pltpu.VMEM((width, frame_count), BF),
            pltpu.VMEM((width, frame_count), BF),
        ],
        compiler_params=pltpu.CompilerParams(vmem_limit_bytes=VMEM_LIMIT),
        name="attend_backward",
    )(x, gmid, nb, qaug, kk, vv, mixed, dmixed, kaug, wq, wk, wv, vec)


def bits_differ(a, b, size):
    total, bit = 0, 1
    while bit < size:
        total = total + bit * lax.rem(a // bit + b // bit, 2)
        bit *= 2
    return total


def remote(src, dst, send, recv, device):
    return pltpu.make_async_remote_copy(
        src_ref=src,
        dst_ref=dst,
        send_sem=send,
        recv_sem=recv,
        device_id=(device,),
        device_id_type=MESH,
    )


def spread_rows(blocks, share, width):
    count, height, lanes = blocks.shape
    source = lax.broadcasted_iota(jnp.int32, (lanes, width), 0)
    target = lax.broadcasted_iota(jnp.int32, (lanes, width), 1)
    pick = jnp.where(source == lax.rem(target, share), 1.0, 0.0).astype(BF)
    spread = dot_nn(blocks.reshape(count * height, lanes).astype(BF), pick)
    owner = lax.broadcasted_iota(jnp.int32, (count, height, width), 0)
    place = lax.broadcasted_iota(jnp.int32, (count, height, width), 2)
    spread = spread.reshape(count, height, width)
    return jnp.sum(jnp.where(owner == place // share, spread, 0.0), axis=0)


SECOND_DUTIES = ((0, 0, 2), (1, 0, 3), (2, 1, 1), (4, 1, 2), (6, 1, 3))


def gather_attend_kernel(n, tb, lb, *refs):
    (lengths, x, sq, sk, sv, so, su, sd) = refs[:8]
    vectors, refs = refs[8:17], refs[17:]
    (wq, wk, wv, wo, wup, wdn, table, bup, kk_h, vv_h, qaug_h, nb_h, mixed_h, middle_h) = refs[:14]
    (xhat, nb, mixed, middle, kaug, qbuf, kbuf, vbuf, qaug, svec, vec) = refs[14:25]
    (own_sem, near_s, near_r, core_s, core_r, far_s, far_r, fwd_s, fwd_r) = refs[25:34]
    (bown_sem, bfar_s, bfar_r, bnear_s, bnear_r, bcore_s, bcore_r, out_sem, end_sem) = refs[34:]
    far, near = levels_of(n)
    share = 512 // n
    frame_count, width = x.shape
    pairs = HEADS // 2
    me = lax.axis_index("dp")
    top, mid, core = announce(n, me, far, near)
    lane = lax.broadcasted_iota(jnp.int32, (1, 128), 1)
    svec[...] = jnp.zeros_like(svec)
    for v, vector in enumerate(vectors):
        length = vector.shape[0]
        svec[v : v + 1, :length] = vector[...].astype(F32).reshape(1, length)

    def index(t, m, c):
        return (t * near + m) * 2 + c

    sibling = index(top, mid, 1 - core)
    first = list(zip((sq, sk, sv), (wq, wk, wv)))
    second = list(zip((svec, so, su, sd), (vec, wo, wup, wdn)))

    def near_copy(a, k):
        peer = index(top, lax.rem(mid + k, near), core)
        src, dst = first[a]
        return remote(src, dst.at[top, mid, core], near_s.at[a, k - 1], near_r.at[a, k - 1], peer)

    def core_copy(a):
        ref = first[a][1].at[top, :, core]
        return remote(ref, ref, core_s.at[a], core_r.at[a], sibling)

    def far_copy(a, k):
        ref = first[a][1].at[top, :, core]
        peer = index(bits_differ(top, k, far), mid, core)
        return remote(ref, ref, far_s.at[a, k - 1], far_r.at[a, k - 1], peer)

    def fwd_copy(a, k):
        ref = first[a][1].at[bits_differ(top, k, far), :, core]
        return remote(ref, ref, fwd_s.at[a, k - 1], fwd_r.at[a, k - 1], sibling)

    def bfar_copy(a, k):
        src, dst = second[a]
        peer = index(bits_differ(top, k, far), mid, core)
        return remote(src, dst.at[top, mid, core], bfar_s.at[a, k - 1], bfar_r.at[a, k - 1], peer)

    def bnear_copy(a, k):
        ref = second[a][1].at[:, mid, core]
        peer = index(top, lax.rem(mid + k, near), core)
        return remote(ref, ref, bnear_s.at[a, k - 1], bnear_r.at[a, k - 1], peer)

    def bcore_copy(a):
        ref = second[a][1].at[:, :, core]
        return remote(ref, ref, bcore_s.at[a], bcore_r.at[a], sibling)

    def own_copy(a):
        src, dst = first[a]
        return pltpu.make_async_copy(src, dst.at[top, mid, core], own_sem.at[a])

    def bown_copy(a):
        src, dst = second[a]
        return pltpu.make_async_copy(src, dst.at[top, mid, core], bown_sem.at[a])

    def stats(i, carry):
        r = rows(i * lb, lb)
        xhat[r, :] = normal_stats(x[r, :].astype(F32))[0]
        position = lax.broadcasted_iota(jnp.int32, (lb, 128), 0) + i * lb
        lanes = lax.broadcasted_iota(jnp.int32, (lb, 128), 1)
        same = segment_lanes(lengths, position, lanes)
        slot = lax.rem(lanes, 64)
        kaug[r, :] = jnp.where(
            slot < 3, jnp.where(same, 0.0, EXCLUDED), jnp.where(slot < 6, 1.0, 0.0)
        ).astype(BF)
        return carry

    lax.fori_loop(0, frame_count // lb, stats, 0)
    await_peers(far, near)
    for k in range(1, far):
        bfar_copy(0, k).start()
    bown_copy(0).start()
    for a in range(3):
        for k in range(1, near):
            near_copy(a, k).start()
        own_copy(a).start()
    for a in range(1, 4):
        for k in range(1, far):
            bfar_copy(a, k).start()
        bown_copy(a).start()

    bown_copy(0).wait()
    for k in range(1, far):
        bfar_copy(0, k).wait_recv()
    for k in range(1, near):
        bnear_copy(0, k).start()
    for a in range(3):
        own_copy(a).wait()
        for k in range(1, near):
            near_copy(a, k).wait_recv()
        core_copy(a).start()
    for k in range(1, near):
        bnear_copy(0, k).wait_recv()
    bcore_copy(0).start()
    for k in range(1, far):
        for a in range(3):
            far_copy(a, k).start()
    bcore_copy(0).wait_recv()
    blocks = vec[...].reshape(n, 16, 128)
    table[...] = spread_rows(blocks, share, width)
    gain, shift = table[0:1, :], table[1:2, :]

    def norm(i, carry):
        r = rows(i * lb, lb)
        nb[r, :] = (xhat[r, :] * gain + shift).astype(BF)
        return carry

    lax.fori_loop(0, frame_count // lb, norm, 0)
    nb_copy = pltpu.make_async_copy(nb, nb_h, end_sem.at[0])
    nb_copy.start()
    for a in range(3):
        core_copy(a).wait_recv()

    def second_near(a):
        bown_copy(a).wait()
        for k in range(1, far):
            bfar_copy(a, k).wait_recv()
        for k in range(1, near):
            bnear_copy(a, k).start()

    def second_core(a):
        for k in range(1, near):
            bnear_copy(a, k).wait_recv()
        bcore_copy(a).start()

    second_near(1)

    def out_copies(p, slot):
        cols = rows(p * 128, 128)
        wide = rows(p * 256, 256)
        return (
            pltpu.make_async_copy(kbuf.at[slot], kk_h.at[:, cols], out_sem.at[slot, 0]),
            pltpu.make_async_copy(vbuf.at[slot], vv_h.at[:, cols], out_sem.at[slot, 1]),
            pltpu.make_async_copy(qaug.at[slot], qaug_h.at[:, wide], out_sem.at[slot, 2]),
        )

    def pair_step(i, carry):
        p = bits_differ(top, i, far)
        slot = lax.rem(i, 2)
        cols = rows(p * 128, 128)

        @pl.when(i > 0)
        def _():
            for a in range(3):
                fwd_copy(a, i).wait_recv()

        @pl.when(i > 1)
        def _():
            for copy in out_copies(bits_differ(top, i - 2, far), slot):
                copy.wait()

        weights = jnp.concatenate(
            [w[p].reshape(128, width) for w in (wq, wk, wv)], axis=0
        )
        bq, bv = table[2:3, cols], table[3:4, cols]

        def project(j, inner):
            r = rows(j * lb, lb)
            got = dot_nt(nb[r, :], weights)
            qbuf[r, :] = ((got[:, :128] + bq).astype(BF).astype(F32) * 0.125).astype(BF)
            kbuf[slot, r, :] = got[:, 128:256].astype(BF)
            vbuf[slot, r, :] = (got[:, 256:] + bv).astype(BF)
            return inner

        lax.fori_loop(0, frame_count // lb, project, 0)
        for half in range(2):
            own = own_lanes(lane, half)
            base = 64 - 64 * half
            key = jnp.where(own, kbuf[slot], kaug[...])
            value = jnp.where(own, vbuf[slot], jnp.ones((1, 128), BF))

            def block(j):
                r = pl.ds(j * tb, tb)
                position = lax.broadcasted_iota(jnp.int32, (tb, 128), 0) + j * tb
                lanes = lax.broadcasted_iota(jnp.int32, (tb, 128), 1)
                mark = jnp.where(segment_lanes(lengths, position, lanes), 1.0, 0.0).astype(BF)
                query = jnp.where(own, qbuf[r, :], mark)
                scores = dot_nt(query, key)
                peak = jnp.max(scores, axis=1, keepdims=True)
                raised = jnp.exp(scores - peak).astype(BF)
                got = dot_nn(raised, value)
                total = got[:, base : base + 1]
                got = (got * (1.0 / total)).astype(BF)
                if half == 0:
                    mixed[r, cols] = got
                else:
                    mixed[r, cols] = jnp.where(own, got, mixed[r, cols])
                high, middle_piece, low = three_pieces(-(peak + jnp.log(total)))
                query = jnp.where(lane == base + 3, high, query)
                query = jnp.where(lane == base + 4, middle_piece, query)
                qaug[slot, r, 128 * half : 128 * half + 128] = jnp.where(
                    lane == base + 5, low, query
                )

            for j in range(frame_count // tb):
                block(j)
            if half == 0:

                @pl.when(i < far - 1)
                def _():
                    for a in range(3):
                        far_copy(a, i + 1).wait_recv()
                        fwd_copy(a, i + 1).start()

            for step, duty, a in SECOND_DUTIES:
                if step % 2 == half:
                    act = second_near if duty == 0 else second_core
                    pl.when(i == step // 2)(functools.partial(act, a))

        for copy in out_copies(p, slot):
            copy.start()
        return carry

    lax.fori_loop(0, pairs, pair_step, 0)
    mixed_copy = pltpu.make_async_copy(mixed, mixed_h, end_sem.at[1])
    mixed_copy.start()
    bcore_copy(1).wait_recv()
    out_weight = wo[...].reshape(width, width)
    bo = table[4:5, :]
    bup[...] = spread_rows(vec[...].reshape(n, 16, 128)[:, 8:16], 4 * share, 4 * width)

    def finish(i, carry):
        r = rows(i * lb, lb)
        middle[r, :] = x[r, :].astype(F32) + (dot_nt(mixed[r, :], out_weight) + bo)
        return carry

    lax.fori_loop(0, frame_count // lb, finish, 0)
    middle_copy = pltpu.make_async_copy(middle, middle_h, end_sem.at[2])
    middle_copy.start()
    for i in (pairs - 2, pairs - 1):
        for copy in out_copies(bits_differ(top, i, far), i % 2):
            copy.wait()
    nb_copy.wait()
    mixed_copy.wait()
    for a in range(3):
        for k in range(1, near):
            near_copy(a, k).wait_send()
        core_copy(a).wait_send()
        for k in range(1, far):
            far_copy(a, k).wait_send()
            fwd_copy(a, k).wait_send()
    bcore_copy(2).wait_recv()
    bcore_copy(3).wait_recv()
    for a in range(4):
        for k in range(1, far):
            bfar_copy(a, k).wait_send()
        for k in range(1, near):
            bnear_copy(a, k).wait_send()
        bcore_copy(a).wait_send()
    middle_copy.wait()


def gather_attend(n, lengths, x, shards, vectors):
    far, near = levels_of(n)
    frame_count, width = x.shape
    lead = (far, near, 2)
    share = width // n
    square = jax.ShapeDtypeStruct(lead + (share, width), BF)
    low = jax.ShapeDtypeStruct((frame_count, width), BF)
    dma = pltpu.SemaphoreType.DMA
    return pl.pallas_call(
        functools.partial(gather_attend_kernel, n, 512, 512),
        out_shape=[
            square,
            square,
            square,
            square,
            jax.ShapeDtypeStruct(lead + (4 * share, width), BF),
            jax.ShapeDtypeStruct(lead + (share, 4 * width), BF),
            jax.ShapeDtypeStruct((16, width), F32),
            jax.ShapeDtypeStruct((8, 4 * width), F32),
            low,
            low,
            jax.ShapeDtypeStruct((frame_count, HEADS * 128), BF),
            low,
            low,
            jax.ShapeDtypeStruct((frame_count, width), F32),
        ],
        in_specs=[SMEM_SPEC, VMEM_SPEC] + [HBM_SPEC] * 6 + [VMEM_SPEC] * 9,
        out_specs=[VMEM_SPEC] * 4 + [HBM_SPEC] * 2 + [VMEM_SPEC] * 2 + [HBM_SPEC] * 6,
        scratch_shapes=[
            pltpu.VMEM((frame_count, width), F32),
            pltpu.VMEM((frame_count, width), BF),
            pltpu.VMEM((frame_count, width), BF),
            pltpu.VMEM((frame_count, width), F32),
            pltpu.VMEM((frame_count, 128), BF),
            pltpu.VMEM((frame_count, 128), BF),
            pltpu.VMEM((2, frame_count, 128), BF),
            pltpu.VMEM((2, frame_count, 128), BF),
            pltpu.VMEM((2, frame_count, 256), BF),
            pltpu.VMEM((16, 128), F32),
            pltpu.VMEM(lead + (16, 128), F32),
            dma((3,)),
            dma((3, near - 1)),
            dma((3, near - 1)),
            dma((3,)),
            dma((3,)),
            dma((3, far - 1)),
            dma((3, far - 1)),
            dma((3, far - 1)),
            dma((3, far - 1)),
            dma((4,)),
            dma((4, far - 1)),
            dma((4, far - 1)),
            dma((4, near - 1)),
            dma((4, near - 1)),
            dma((4,)),
            dma((4,)),
            dma((2, 3)),
            dma((3,)),
        ],
        compiler_params=pltpu.CompilerParams(
            collective_id=2, has_side_effects=True, vmem_limit_bytes=VMEM_LIMIT
        ),
        name="gather_attend",
    )(lengths, x, *shards, *vectors)


def feed_fused_kernel(
    n,
    lengths,
    middle,
    gout,
    mixed,
    wup,
    wdn,
    wo,
    table,
    bup,
    layer_out,
    gmid,
    dmixed,
    dwo,
    dwup,
    dwdn,
    columns,
    sums,
    sum_up,
    nb,
    act,
    gup,
    glow,
    gbl,
    *,
    tb,
):
    frame_count, width = middle.shape
    share = width // n
    finish = lengths[0, 0] + lengths[0, 1]
    gain, shift, bdn = (table[i : i + 1, :] for i in range(5, 8))
    sums[...] = jnp.zeros_like(sums)
    sum_up[...] = jnp.zeros_like(sum_up)

    def block(i, carry):
        r = rows(i * tb, tb)
        valid = lax.broadcasted_iota(jnp.int32, (tb, 1), 0) + i * tb < finish
        mid = middle[r, :]
        xhat, inv = normal_stats(mid)
        normed = (xhat * gain + shift).astype(BF)
        nb[r, :] = normed
        up = dot_nt(normed, wup[...]) + bup[0:1, :]
        cdf = 0.5 * (1.0 + lax.erf(up * (1.0 / math.sqrt(2.0))))
        low = (up * cdf).astype(BF)
        act[r, :] = low
        down = dot_nt(low, wdn[...]) + bdn
        layer_out[r, :] = jnp.where(valid, mid + down, 0.0).astype(BF)
        grow = jnp.where(valid, gout[r, :].astype(F32), 0.0)
        gl = grow.astype(BF)
        glow[r, :] = gl
        slope = cdf + up * jnp.exp(-0.5 * up * up) * (1.0 / math.sqrt(2.0 * math.pi))
        gu = (dot_nn(gl, wdn[...]) * slope).astype(BF)
        gup[r, :] = gu
        gn = dot_nn(gu, wup[...])
        scaled = gn * gain
        gm = grow + inv * (
            scaled
            - jnp.mean(scaled, axis=-1, keepdims=True)
            - xhat * jnp.mean(scaled * xhat, axis=-1, keepdims=True)
        )
        gmid[r, :] = gm
        gb = gm.astype(BF)
        gbl[r, :] = gb
        dmixed[r, :] = dot_nn(gb, wo[...]).astype(BF)
        sums[4:5, :] += jnp.sum(gb.astype(F32), axis=0, keepdims=True)
        sums[5:6, :] += jnp.sum(gn * xhat, axis=0, keepdims=True)
        sums[6:7, :] += jnp.sum(gn, axis=0, keepdims=True)
        sums[7:8, :] += jnp.sum(grow, axis=0, keepdims=True)
        sum_up[0:1, :] += jnp.sum(gu.astype(F32), axis=0, keepdims=True)
        return carry

    lax.fori_loop(0, frame_count // tb, block, 0)
    dwo[...] = dot_tn(gbl[...], mixed[...]).astype(BF)

    def weights(i, carry):
        c = rows(i * 512, 512)
        dwup[c, :] = dot_tn(gup[:, c], nb[...]).astype(BF)
        dwdn[:, c] = dot_tn(glow[...], act[:, c]).astype(BF)
        return carry

    lax.fori_loop(0, wup.shape[0] // 512, weights, 0)
    lane = lax.broadcasted_iota(jnp.int32, (1, 128), 1)
    plain = sums[...].T
    hidden = sum_up[...].T.reshape(n, 4, share, 8)
    found = jnp.zeros((width, 128), F32)
    for v in range(4, 8):
        found = jnp.where(lane == v, plain[:, v : v + 1], found)
    for k in range(4):
        piece = hidden[:, k].reshape(width, 8)
        found = jnp.where(lane == 8 + k, piece[:, 0:1], found)
    columns[...] = found


def feed_fused(n, lengths, middle, gout, mixed, wup, wdn, wo, table, bup):
    frame_count, width = middle.shape
    hidden = wup.shape[0]
    low = jax.ShapeDtypeStruct((frame_count, width), BF)
    return pl.pallas_call(
        functools.partial(feed_fused_kernel, n, tb=256),
        out_shape=[
            low,
            jax.ShapeDtypeStruct((frame_count, width), F32),
            low,
            jax.ShapeDtypeStruct((width, width), BF),
            jax.ShapeDtypeStruct((hidden, width), BF),
            jax.ShapeDtypeStruct((width, hidden), BF),
            jax.ShapeDtypeStruct((width, 128), F32),
        ],
        in_specs=[SMEM_SPEC] + [VMEM_SPEC] * 8,
        out_specs=[VMEM_SPEC] * 7,
        scratch_shapes=[
            pltpu.VMEM((8, width), F32),
            pltpu.VMEM((8, hidden), F32),
            pltpu.VMEM((frame_count, width), BF),
            pltpu.VMEM((frame_count, hidden), BF),
            pltpu.VMEM((frame_count, hidden), BF),
            pltpu.VMEM((frame_count, width), BF),
            pltpu.VMEM((frame_count, width), BF),
        ],
        compiler_params=pltpu.CompilerParams(vmem_limit_bytes=VMEM_LIMIT),
        name="feed_forward_both",
    )(lengths, middle, gout, mixed, wup, wdn, wo, table, bup)


def back_scatter_kernel(n, ub, lb, *refs):
    (lengths, x_h, gmid_h, nb_h, qaug_h, kk_h, vv_h, mixed_h, dmixed_h) = refs[:9]
    (wq, wk, wv, table, columns, po, pu, pd) = refs[9:17]
    (grad_h, gq, gk, gv, go, gu, gd, gc) = refs[17:25]
    (x, gmid, nb, qaug, kbuf, vbuf, mixed, dmixed, kaug, dq, dqb, dkt, dvt, sums, grad) = refs[25:40]
    biases, refs = refs[40], refs[:40] + refs[41:]
    (parts, core_in, core_sum, near_in, near_sum, far_in) = refs[40:46]
    (own2, core_in2, near_in2, near_sum2, far_in2) = (refs[46 + 3 * j : 49 + 3 * j] for j in range(5))
    (cparts, ccore_in, ccore_sum, cnear_in, cnear_sum, cfar_in) = refs[61:67]
    (in_sem, end_sem, core_s, core_r, near_s, near_r, far_s, far_r) = refs[67:75]
    (own2_sem, core2_s, core2_r, near2_s, near2_r, far2_s, far2_r) = refs[75:82]
    (ccore_s, ccore_r, cnear_s, cnear_r, cfar_s, cfar_r) = refs[82:]
    far, near = levels_of(n)
    frame_count, width = x.shape
    share = width // n
    pairs = HEADS // 2
    last = pairs - 1
    me = lax.axis_index("dp")
    top, mid, core = announce(n, me, far, near)
    lane = lax.broadcasted_iota(jnp.int32, (1, 128), 1)

    def index(t, m, c):
        return (t * near + m) * 2 + c

    sibling = index(top, mid, 1 - core)
    big = (po, pu, pd)

    def own2_copy(a):
        return pltpu.make_async_copy(big[a].at[:, :, core], own2[a], own2_sem.at[a])

    def core2_copy(a):
        return remote(
            big[a].at[:, :, 1 - core], core_in2[a], core2_s.at[a], core2_r.at[a], sibling
        )

    def near2_copy(a, k):
        peer = lax.rem(mid + k, near)
        return remote(
            own2[a].at[:, peer],
            near_in2[a].at[k - 1],
            near2_s.at[a, k - 1],
            near2_r.at[a, k - 1],
            index(top, peer, core),
        )

    def far2_copy(a, k):
        peer = bits_differ(top, k, far)
        return remote(
            near_sum2[a].at[peer],
            far_in2[a].at[k - 1],
            far2_s.at[a, k - 1],
            far2_r.at[a, k - 1],
            index(peer, mid, core),
        )

    def core_copy(j):
        return remote(
            parts.at[j, :, :, 1 - core], core_in.at[j], core_s.at[j], core_r.at[j], sibling
        )

    def near_copy(j, k):
        peer = lax.rem(mid + k, near)
        return remote(
            core_sum.at[j, peer],
            near_in.at[j, k - 1],
            near_s.at[j, k - 1],
            near_r.at[j, k - 1],
            index(top, peer, core),
        )

    def far_copy(j):
        peer = index(bits_differ(top, last - j, far), mid, core)
        return remote(near_sum.at[j], far_in.at[j], far_s.at[j], far_r.at[j], peer)

    def add_core(j):
        for m in range(near):
            core_sum[j, m] = (
                parts[j, :, m, core].astype(F32) + core_in[j, :, m].astype(F32)
            ).astype(BF)

    def add_near(j):
        total = core_sum[j, mid].astype(F32)
        for k in range(near - 1):
            total = total + near_in[j, k].astype(F32)
        return total

    def second_far(a):
        for k in range(1, near):
            near2_copy(a, k).wait_recv()

        def add(f, inner):
            total = own2[a][f, mid].astype(F32)
            for k in range(near - 1):
                total = total + near_in2[a][k, f].astype(F32)
            near_sum2[a][f] = total.astype(BF)
            return inner

        lax.fori_loop(0, far, add, 0)
        for k in range(1, far):
            far2_copy(a, k).start()

    def pair_near(j):
        core_copy(j).wait_recv()
        add_core(j)
        for k in range(1, near):
            near_copy(j, k).start()

    def pair_far(j):
        for k in range(1, near):
            near_copy(j, k).wait_recv()
        near_sum[j] = add_near(j).astype(BF)
        far_copy(j).start()

    def in_copies(p, slot):
        cols = rows(p * 128, 128)
        wide = rows(p * 256, 256)
        return [
            pltpu.make_async_copy(qaug_h.at[:, wide], qaug.at[slot], in_sem.at[slot, 0]),
            pltpu.make_async_copy(kk_h.at[:, cols], kbuf.at[slot], in_sem.at[slot, 1]),
            pltpu.make_async_copy(vv_h.at[:, cols], vbuf.at[slot], in_sem.at[slot, 2]),
            pltpu.make_async_copy(mixed_h.at[:, cols], mixed.at[slot], in_sem.at[slot, 3]),
            pltpu.make_async_copy(dmixed_h.at[:, cols], dmixed.at[slot], in_sem.at[slot, 4]),
        ]

    end_copies = [
        pltpu.make_async_copy(nb_h, nb, end_sem.at[0]),
        pltpu.make_async_copy(x_h, x, end_sem.at[1]),
        pltpu.make_async_copy(gmid_h, gmid, end_sem.at[2]),
    ]
    for copy in in_copies(bits_differ(top, last, far), 0):
        copy.start()
    for a in range(3):
        own2_copy(a).start()

    def marks(i, carry):
        r = rows(i * lb, lb)
        position = lax.broadcasted_iota(jnp.int32, (lb, 128), 0) + i * lb
        lanes = lax.broadcasted_iota(jnp.int32, (lb, 128), 1)
        same = segment_lanes(lengths, position, lanes)
        slot = lax.rem(lanes, 64)
        kaug[r, :] = jnp.where(
            slot < 3, jnp.where(same, 0.0, EXCLUDED), jnp.where(slot < 6, 1.0, 0.0)
        ).astype(BF)
        return carry

    lax.fori_loop(0, frame_count // lb, marks, 0)
    await_peers(far, near)
    for a in range(3):
        core2_copy(a).start()
    for copy in end_copies:
        copy.start()
    end_copies[0].wait()

    def pair_step(i, carry):
        p = bits_differ(top, last - i, far)
        slot = lax.rem(i, 2)
        cols = rows(p * 128, 128)
        for copy in in_copies(p, slot):
            copy.wait()

        @pl.when(i < last)
        def _():
            for copy in in_copies(bits_differ(top, last - i - 1, far), 1 - slot):
                copy.start()

        grad_pair = dmixed[slot]
        product = grad_pair.astype(F32) * mixed[slot].astype(F32)
        for half in range(2):
            own = own_lanes(lane, half)
            base = 64 - 64 * half
            delta = jnp.sum(jnp.where(own, product, 0.0), axis=1, keepdims=True)
            high, middle_piece, low = three_pieces(-delta)
            grad_head = jnp.where(own, grad_pair, jnp.zeros((1, 128), BF))
            grad_head = jnp.where(lane == base + 3, high, grad_head)
            grad_head = jnp.where(lane == base + 4, middle_piece, grad_head)
            grad_head = jnp.where(lane == base + 5, low, grad_head)
            query = qaug[slot, :, 128 * half : 128 * half + 128]
            here = pl.ds(pl.multiple_of(p * 128 + 64 * half, 64), 64)
            part = slice(64 * half, 64 * half + 64)
            ones = jnp.where(
                (lane >= base + 3) & (lane < base + 6), jnp.ones((1, 128), F32), 0.0
            ).astype(BF)
            for j in range(frame_count // ub):
                r = pl.ds(j * ub, ub)
                pair_key = kbuf[slot, r, :]
                key = jnp.where(own, pair_key, kaug[r, :])
                value = jnp.where(own, vbuf[slot, r, :], ones)
                probs = jnp.exp(dot_nt(query, key))
                low_probs = probs.astype(BF)
                gs = (probs * dot_nt(grad_head, value)).astype(BF)
                dvt[here, r] = dot_tn(grad_head, low_probs)[part].astype(BF)
                dkt[here, r] = dot_tn(query, gs)[part].astype(BF)
                step = dot_nn(gs, pair_key)
                if j == 0:
                    dq[...] = step
                else:
                    dq[...] += step
            done = (dq[...] * 0.125).astype(BF)
            if half == 0:
                dqb[:, cols] = done

                @pl.when(i == 0)
                def _():
                    for a in range(3):
                        core2_copy(a).wait_recv()
                        own2_copy(a).wait()

                        def add(f, inner, a=a):
                            own2[a][f] = (
                                own2[a][f].astype(F32) + core_in2[a][f].astype(F32)
                            ).astype(BF)
                            return inner

                        lax.fori_loop(0, far, add, 0)
                        for k in range(1, near):
                            near2_copy(a, k).start()

                pl.when(i > 0)(functools.partial(pair_near, i - 1))
                pl.when(i == last)(functools.partial(pair_far, 0))

            else:
                dqb[:, cols] = jnp.where(own, done, dqb[:, cols])

                for a in range(3):
                    pl.when(i == a)(functools.partial(second_far, a))
                pl.when(i == last)(functools.partial(pair_far, 1))

        pair_rows = rows(p * 128, 128)
        shape = (near, 2, share, width)
        found = (
            dot_tn(dqb[:, cols], nb[...]),
            dot_nn(dkt[pair_rows, :], nb[...]),
            dot_nn(dvt[pair_rows, :], nb[...]),
        )
        for a in range(3):
            parts[i, a] = found[a].astype(BF).reshape(shape)
        core_copy(i).start()
        by_query = dot_tn(dqb[:, cols], jnp.ones((frame_count, 128), BF))
        column = (
            by_query[:, 0:1],
            jnp.sum(dkt[pair_rows, :].astype(F32), axis=1, keepdims=True),
            jnp.sum(dvt[pair_rows, :].astype(F32), axis=1, keepdims=True),
        )
        held = [w[pair_rows, :].astype(F32) for w in (wq, wk, wv)]
        with_rows = sum(g * w for g, w in zip(found, held))
        alone = sum(c * w for c, w in zip(column, held))
        sums[0:1, :] += jnp.sum(with_rows, axis=0, keepdims=True)
        sums[1:2, :] += jnp.sum(alone, axis=0, keepdims=True)
        biases[pair_rows, :] = jnp.where(
            lane == 2, column[0], jnp.where(lane == 3, column[2], columns[pair_rows, :])
        )
        return carry

    sums[...] = jnp.zeros_like(sums)
    lax.fori_loop(0, pairs, pair_step, 0)

    gain, shift = table[0:1, :], table[1:2, :]
    sums[0:1, :] = (sums[0:1, :] - shift * sums[1:2, :]) / gain
    plain = sums[...].T
    found = jnp.where(lane == 0, plain[:, 0:1], biases[...])
    found = jnp.where(lane == 1, plain[:, 1:2], found)
    cparts[...] = found.astype(BF).reshape(far, near, 2, share, 128)
    ccore = remote(cparts.at[:, :, 1 - core], ccore_in, ccore_s, ccore_r, sibling)
    ccore.start()
    pair_near(last)
    pair_far(last - 1)
    cnear, cfar = [], []
    for k in range(1, near):
        peer = lax.rem(mid + k, near)
        cnear.append(
            remote(
                ccore_sum.at[peer],
                cnear_in.at[k - 1],
                cnear_s.at[k - 1],
                cnear_r.at[k - 1],
                index(top, peer, core),
            )
        )
    for k in range(1, far):
        peer = bits_differ(top, k, far)
        cfar.append(
            remote(
                cnear_sum.at[peer],
                cfar_in.at[k - 1],
                cfar_s.at[k - 1],
                cfar_r.at[k - 1],
                index(peer, mid, core),
            )
        )
    end_copies[1].wait()
    end_copies[2].wait()

    def finish(i, carry):
        r = rows(i * lb, lb)
        gn = dot_nn(dqb[r, :], wq[...]) + dot_tn(dkt[:, r], wk[...]) + dot_tn(dvt[:, r], wv[...])
        xhat, inv = normal_stats(x[r, :].astype(F32))
        scaled = gn * gain
        grad[r, :] = (
            gmid[r, :]
            + inv
            * (
                scaled
                - jnp.mean(scaled, axis=-1, keepdims=True)
                - xhat * jnp.mean(scaled * xhat, axis=-1, keepdims=True)
            )
        ).astype(BF)

        @pl.when(i == 0)
        def _():
            ccore.wait_recv()
            for m in range(near):
                ccore_sum[m] = (
                    cparts[:, m, core].astype(F32) + ccore_in[:, m].astype(F32)
                ).astype(BF)
            for copy in cnear:
                copy.start()

        @pl.when(i == 1)
        def _():
            for copy in cnear:
                copy.wait_recv()
            total = ccore_sum[mid].astype(F32)
            for k in range(near - 1):
                total = total + cnear_in[k].astype(F32)
            cnear_sum[...] = total.astype(BF)
            for copy in cfar:
                copy.start()

        return carry

    lax.fori_loop(0, frame_count // lb, finish, 0)
    grad_copy = pltpu.make_async_copy(grad, grad_h, end_sem.at[3])
    grad_copy.start()
    for k in range(1, near):
        near_copy(last, k).wait_recv()
    total = add_near(last)
    for j in range(last):
        far_copy(j).wait_recv()
        total = total + far_in[j].astype(F32)
    gq[...] = total[0]
    gk[...] = total[1]
    gv[...] = total[2]
    for a, out in enumerate((go, gu, gd)):
        for k in range(1, far):
            far2_copy(a, k).wait_recv()
        total = near_sum2[a][top].astype(F32)
        for k in range(far - 1):
            total = total + far_in2[a][k].astype(F32)
        out[...] = total
    for copy in cfar:
        copy.wait_recv()
    total = cnear_sum[top].astype(F32)
    for k in range(far - 1):
        total = total + cfar_in[k].astype(F32)
    gc[...] = total
    for a in range(3):
        core2_copy(a).wait_send()
        for k in range(1, near):
            near2_copy(a, k).wait_send()
        for k in range(1, far):
            far2_copy(a, k).wait_send()
    for j in range(pairs):
        core_copy(j).wait_send()
        for k in range(1, near):
            near_copy(j, k).wait_send()
        if j < last:
            far_copy(j).wait_send()
    ccore.wait_send()
    for copy in cnear + cfar:
        copy.wait_send()
    grad_copy.wait()


def back_scatter(n, lengths, x, gmid, nb, qaug, kk, vv, mixed, dmixed, weights, table, columns, big):
    far, near = levels_of(n)
    frame_count, width = x.shape
    share = width // n
    pairs = HEADS // 2
    blocks = [p.shape[3:] for p in big]
    row_block = jax.ShapeDtypeStruct((share, width), F32)
    dma = pltpu.SemaphoreType.DMA
    return pl.pallas_call(
        functools.partial(back_scatter_kernel, n, 512, 512),
        out_shape=[
            jax.ShapeDtypeStruct((frame_count, width), BF),
            row_block,
            row_block,
            row_block,
        ]
        + [jax.ShapeDtypeStruct(b, F32) for b in blocks]
        + [jax.ShapeDtypeStruct((share, 128), F32)],
        in_specs=[SMEM_SPEC] + [HBM_SPEC] * 8 + [VMEM_SPEC] * 5 + [HBM_SPEC] * 3,
        out_specs=[HBM_SPEC] + [VMEM_SPEC] * 7,
        scratch_shapes=[
            pltpu.VMEM((frame_count, width), BF),
            pltpu.VMEM((frame_count, width), F32),
            pltpu.VMEM((frame_count, width), BF),
            pltpu.VMEM((2, frame_count, 256), BF),
            pltpu.VMEM((2, frame_count, 128), BF),
            pltpu.VMEM((2, frame_count, 128), BF),
            pltpu.VMEM((2, frame_count, 128), BF),
            pltpu.VMEM((2, frame_count, 128), BF),
            pltpu.VMEM((frame_count, 128), BF),
            pltpu.VMEM((frame_count, 128), F32),
            pltpu.VMEM((frame_count, width), BF),
            pltpu.VMEM((width, frame_count), BF),
            pltpu.VMEM((width, frame_count), BF),
            pltpu.VMEM((8, width), F32),
            pltpu.VMEM((frame_count, width), BF),
            pltpu.VMEM((width, 128), F32),
            pltpu.VMEM((pairs, 3, near, 2, share, width), BF),
            pltpu.VMEM((pairs, 3, near, share, width), BF),
            pltpu.VMEM((pairs, near, 3, share, width), BF),
            pltpu.VMEM((pairs, near - 1, 3, share, width), BF),
            pltpu.VMEM((pairs, 3, share, width), BF),
            pltpu.VMEM((pairs - 1, 3, share, width), BF),
        ]
        + [pltpu.VMEM((far, near) + b, BF) for b in blocks]
        + [pltpu.VMEM((far, near) + b, BF) for b in blocks]
        + [pltpu.VMEM((near - 1, far) + b, BF) for b in blocks]
        + [pltpu.VMEM((far,) + b, BF) for b in blocks]
        + [pltpu.VMEM((far - 1,) + b, BF) for b in blocks]
        + [
            pltpu.VMEM((far, near, 2, share, 128), BF),
            pltpu.VMEM((far, near, share, 128), BF),
            pltpu.VMEM((near, far, share, 128), BF),
            pltpu.VMEM((near - 1, far, share, 128), BF),
            pltpu.VMEM((far, share, 128), BF),
            pltpu.VMEM((far - 1, share, 128), BF),
            dma((2, 5)),
            dma((4,)),
            dma((pairs,)),
            dma((pairs,)),
            dma((pairs, near - 1)),
            dma((pairs, near - 1)),
            dma((pairs,)),
            dma((pairs,)),
            dma((3,)),
            dma((3,)),
            dma((3,)),
            dma((3, near - 1)),
            dma((3, near - 1)),
            dma((3, far - 1)),
            dma((3, far - 1)),
            dma,
            dma,
            dma((near - 1,)),
            dma((near - 1,)),
            dma((far - 1,)),
            dma((far - 1,)),
        ],
        compiler_params=pltpu.CompilerParams(
            collective_id=3, has_side_effects=True, vmem_limit_bytes=VMEM_LIMIT
        ),
        name="back_scatter",
    )(lengths, x, gmid, nb, qaug, kk, vv, mixed, dmixed, *weights, table, columns, *big)


def hand_out_kernel(pieces, *refs):
    grad_in, ins, grad_out, outs = refs[0], refs[1:8], refs[8], refs[9:24]
    grad, lanes, grad_r, grad_w, in_sem, out_sem = refs[24], refs[31], *refs[32:]
    held = refs[25:31]
    size = grad.shape[0] // pieces
    reads = [
        pltpu.make_async_copy(
            grad_in.at[pl.ds(j * size, size)], grad.at[pl.ds(j * size, size)], grad_r.at[j]
        )
        for j in range(pieces)
    ]
    writes = [
        pltpu.make_async_copy(
            grad.at[pl.ds(j * size, size)], grad_out.at[pl.ds(j * size, size)], grad_w.at[j]
        )
        for j in range(pieces)
    ]
    small_in = [pltpu.make_async_copy(ins[a], held[a], in_sem.at[a]) for a in range(6)]
    small_in.append(pltpu.make_async_copy(ins[6], lanes, in_sem.at[6]))
    small_out = [pltpu.make_async_copy(held[a], outs[a], out_sem.at[a]) for a in range(6)]
    for copy in small_in + reads:
        copy.start()
    for j in range(pieces):
        reads[j].wait()
        writes[j].start()
    for a in range(6):
        small_in[a].wait()
        small_out[a].start()
    small_in[6].wait()
    turned = lanes[...].T
    for v in range(8):
        outs[6 + v][...] = turned[v : v + 1, :]
    outs[14][...] = turned[8:12, :]
    for copy in writes + small_out:
        copy.wait()


def hand_out(grad, totals):
    share = totals[0].shape[0]
    line = jax.ShapeDtypeStruct((1, share), F32)
    dma = pltpu.SemaphoreType.DMA
    pieces = 4
    return pl.pallas_call(
        functools.partial(hand_out_kernel, pieces),
        out_shape=[jax.ShapeDtypeStruct(grad.shape, grad.dtype)]
        + [jax.ShapeDtypeStruct(t.shape, F32) for t in totals[:6]]
        + [line] * 8
        + [jax.ShapeDtypeStruct((4, share), F32)],
        in_specs=[HBM_SPEC] * 8,
        out_specs=[HBM_SPEC] * 7 + [VMEM_SPEC] * 9,
        scratch_shapes=[pltpu.VMEM(grad.shape, grad.dtype)]
        + [pltpu.VMEM(t.shape, F32) for t in totals]
        + [dma((pieces,)), dma((pieces,)), dma((7,)), dma((6,))],
        compiler_params=pltpu.CompilerParams(vmem_limit_bytes=60 << 20),
        name="hand_out",
    )(grad, *totals)


def per_device_fused(n, frames, lengths, vectors, up_bias, weights, grad_out):
    width = frames.shape[2]
    x = frames[0]
    got = gather_attend(n, lengths, x, tuple(w.T for w in weights), vectors + (up_bias,))
    wq, wk, wv, wo, wup, wdn = (w.reshape(n * w.shape[3], w.shape[4]) for w in got[:6])
    table, bup, kk, vv, qaug, nb, mixed, middle = got[6:]
    layer_out, gmid, dmixed, dwo, dwup, dwdn, columns = feed_fused(
        n, lengths, middle, grad_out[0], mixed, wup, wdn, wo, table, bup
    )
    far, near = levels_of(n)

    def split(g):
        return g.reshape(far, near, 2, g.shape[0] // n, g.shape[1])

    sums = back_scatter(
        n,
        lengths,
        x,
        gmid,
        nb,
        qaug,
        kk,
        vv,
        mixed,
        dmixed,
        (wq, wk, wv),
        table,
        columns,
        (split(dwo), split(dwup), split(dwdn)),
    )
    grad_x, *outs = hand_out(sums[0], sums[1:])
    gq, gk, gv, go, gu, gd = (g.T for g in outs[:6])
    line = [v.reshape(-1) for v in outs[6:14]]
    return (
        layer_out[None],
        grad_x[None],
        line[0],
        line[1],
        gq,
        line[2],
        gk,
        gv,
        line[3],
        go,
        line[4],
        line[5],
        line[6],
        gu,
        outs[14].reshape(-1),
        gd,
        line[7],
    )


def per_device(
    n,
    frames,
    lengths,
    attn_gain,
    attn_shift,
    query_weight,
    query_bias,
    key_weight,
    value_weight,
    value_bias,
    out_weight,
    out_bias,
    mlp_gain,
    mlp_shift,
    up_weight,
    up_bias,
    down_weight,
    down_bias,
    grad_out,
):
    slots, frame_count, width = frames.shape
    assert slots == 1
    share = width // n
    vectors = (
        attn_gain,
        attn_shift,
        query_bias,
        value_bias,
        out_bias,
        mlp_gain,
        mlp_shift,
        down_bias,
    )
    far, near = levels_of(n)
    if share % 16 == 0 and far == HEADS // 2:
        return per_device_fused(
            n,
            frames,
            lengths,
            vectors,
            up_bias,
            (query_weight, key_weight, value_weight, out_weight, up_weight, down_weight),
            grad_out,
        )
    packed = jnp.concatenate(
        [jnp.stack(vectors, axis=1), up_bias.reshape(share, 4), jnp.zeros((share, 116), BF)], axis=1
    )
    shards = (
        query_weight.T,
        key_weight.T,
        value_weight.T,
        out_weight.T,
        up_weight.T,
        down_weight.T,
        packed,
    )
    full = gather_all(n, shards)
    wq, wk, wv, wo, wup, wdn, vec = (
        f.reshape(n * f.shape[3], f.shape[4]) for f in full
    )
    bup = vec[:, 8:12].reshape(1, 4 * width)
    x = frames[0]
    nb, qaug, kk, vv, mixed, middle, kaug = attend(lengths, x, wq, wk, wv, wo, vec)
    layer_out, gmid, dmixed, dwo, dwup, dwdn, sums_two, sum_up = feed(
        lengths, middle, grad_out[0], mixed, wup, wdn, wo, vec, bup
    )
    grad_x, dwq, dwk, dwv, sums_one = attend_back(
        x, gmid, nb, qaug, kk, vv, mixed, dmixed, kaug, wq, wk, wv, vec
    )
    columns = jnp.concatenate(
        [
            sums_one[:4].T,
            sums_two[:4].T,
            sum_up[0].reshape(width, 4),
            jnp.zeros((width, 116), F32),
        ],
        axis=1,
    ).astype(BF)

    def split(g):
        return g.reshape(far, near, 2, g.shape[0] // n, g.shape[1])

    gq, gk, gv, go, gu, gd, gc = scatter_all(
        n, tuple(split(g) for g in (dwq, dwk, dwv, dwo, dwup, dwdn, columns))
    )
    return (
        layer_out[None],
        grad_x[None],
        gc[:, 0],
        gc[:, 1],
        gq.T,
        gc[:, 2],
        gk.T,
        gv.T,
        gc[:, 3],
        go.T,
        gc[:, 4],
        gc[:, 5],
        gc[:, 6],
        gu.T,
        gc[:, 8:12].reshape(4 * share),
        gd.T,
        gc[:, 7],
    )


def solution(mesh):
    row, col, vector = P("dp", None, None), P(None, "dp"), P("dp")
    return jax.shard_map(
        functools.partial(per_device, mesh.shape["dp"]),
        mesh=mesh,
        in_specs=(
            row,
            P("dp", None),
            vector,
            vector,
            col,
            vector,
            col,
            col,
            vector,
            col,
            vector,
            vector,
            vector,
            col,
            vector,
            col,
            vector,
            row,
        ),
        out_specs=(
            row,
            row,
            vector,
            vector,
            col,
            vector,
            col,
            col,
            vector,
            col,
            vector,
            vector,
            vector,
            col,
            vector,
            col,
            vector,
        ),
        check_vma=False,
    )
```

```python
import functools
import math

import jax
import jax.numpy as jnp
from jax import lax
from jax.experimental import pallas as pl
from jax.experimental.pallas import tpu as pltpu
from jax.sharding import PartitionSpec as P

HEADS = 8
EPS = 1e-05
MESH = pl.DeviceIdType.MESH
F32 = jnp.float32
BF = jnp.bfloat16
VMEM_SPEC = pl.BlockSpec(memory_space=pltpu.VMEM)
SMEM_SPEC = pl.BlockSpec(memory_space=pltpu.SMEM)
HBM_SPEC = pl.BlockSpec(memory_space=pl.ANY)
EXCLUDED = -1e30
VMEM_LIMIT = 62 << 20


def dot_nn(a, b):
    return lax.dot_general(a, b, (((1,), (0,)), ((), ())), preferred_element_type=F32)


def dot_nt(a, b):
    return lax.dot_general(a, b, (((1,), (1,)), ((), ())), preferred_element_type=F32)


def dot_tn(a, b):
    return lax.dot_general(a, b, (((0,), (0,)), ((), ())), preferred_element_type=F32)


def levels_of(n):
    rest = n // 2
    bits = rest.bit_length() - 1
    near = 2 ** ((bits + 1) // 2)
    return rest // near, near


def rows(start, size):
    return pl.ds(pl.multiple_of(start, size), size)


def normal_stats(block):
    mean = jnp.mean(block, axis=-1, keepdims=True)
    centered = block - mean
    inv = lax.rsqrt(jnp.mean(centered * centered, axis=-1, keepdims=True) + EPS)
    return centered * inv, inv


def announce(n, me, far, near):
    barrier = pltpu.get_barrier_semaphore()
    core = lax.rem(me, 2)
    mid = lax.rem(me // 2, near)
    top = me // (2 * near)
    peers = [(lax.rem(top + k, far) * near + mid) * 2 + core for k in range(1, far)]
    peers += [(top * near + lax.rem(mid + k, near)) * 2 + core for k in range(1, near)]
    peers += [(top * near + mid) * 2 + 1 - core]
    for peer in peers:
        pl.semaphore_signal(barrier, inc=1, device_id=(peer,), device_id_type=MESH)
    return top, mid, core


def await_peers(far, near):
    pl.semaphore_wait(pltpu.get_barrier_semaphore(), far + near - 1)


def everyone_barrier(n, me, far, near):
    place = announce(n, me, far, near)
    await_peers(far, near)
    return place


def gather_kernel(n, count, *refs):
    shards, outs = refs[:count], refs[count : 2 * count]
    own_sem, far_s, far_r, near_s, near_r, core_s, core_r = refs[2 * count :]
    far, near = levels_of(n)
    me = lax.axis_index("dp")
    top, mid, core = everyone_barrier(n, me, far, near)

    def index(t, m, c):
        return (t * near + m) * 2 + c

    far_copies, near_copies = {}, {}
    for a in range(count):
        for k in range(1, far):
            copy = pltpu.make_async_remote_copy(
                src_ref=shards[a],
                dst_ref=outs[a].at[top, mid, core],
                send_sem=far_s.at[a, k - 1],
                recv_sem=far_r.at[a, k - 1],
                device_id=(index(lax.rem(top + k, far), mid, core),),
                device_id_type=MESH,
            )
            copy.start()
            far_copies[a, k] = copy
        pltpu.make_async_copy(shards[a], outs[a].at[top, mid, core], own_sem.at[a]).start()
    for a in range(count):
        pltpu.make_async_copy(shards[a], outs[a].at[top, mid, core], own_sem.at[a]).wait()
        for k in range(1, far):
            far_copies[a, k].wait_recv()
        for k in range(1, near):
            copy = pltpu.make_async_remote_copy(
                src_ref=outs[a].at[:, mid, core],
                dst_ref=outs[a].at[:, mid, core],
                send_sem=near_s.at[a, k - 1],
                recv_sem=near_r.at[a, k - 1],
                device_id=(index(top, lax.rem(mid + k, near), core),),
                device_id_type=MESH,
            )
            copy.start()
            near_copies[a, k] = copy
    core_copies = []
    for a in range(count):
        for k in range(1, near):
            near_copies[a, k].wait_recv()
        copy = pltpu.make_async_remote_copy(
            src_ref=outs[a].at[:, :, core],
            dst_ref=outs[a].at[:, :, core],
            send_sem=core_s.at[a],
            recv_sem=core_r.at[a],
            device_id=(index(top, mid, 1 - core),),
            device_id_type=MESH,
        )
        copy.start()
        core_copies.append(copy)
    for a in range(count):
        core_copies[a].wait_recv()
    for a in range(count):
        for k in range(1, far):
            far_copies[a, k].wait_send()
        for k in range(1, near):
            near_copies[a, k].wait_send()
        core_copies[a].wait_send()


def gather_all(n, shards):
    far, near = levels_of(n)
    count = len(shards)
    return pl.pallas_call(
        functools.partial(gather_kernel, n, count),
        out_shape=[jax.ShapeDtypeStruct((far, near, 2) + s.shape, s.dtype) for s in shards],
        in_specs=[VMEM_SPEC] * count,
        out_specs=[HBM_SPEC] * count,
        scratch_shapes=[
            pltpu.SemaphoreType.DMA((count,)),
            pltpu.SemaphoreType.DMA((count, far - 1)),
            pltpu.SemaphoreType.DMA((count, far - 1)),
            pltpu.SemaphoreType.DMA((count, near - 1)),
            pltpu.SemaphoreType.DMA((count, near - 1)),
            pltpu.SemaphoreType.DMA((count,)),
            pltpu.SemaphoreType.DMA((count,)),
        ],
        compiler_params=pltpu.CompilerParams(
            collective_id=0, has_side_effects=True, vmem_limit_bytes=32 << 20
        ),
        name="gather_params",
    )(*shards)


def scatter_kernel(n, count, *refs):
    parts, outs = refs[:count], refs[count : 2 * count]
    pos = 2 * count
    core_in, core_sum = refs[pos : pos + count], refs[pos + count : pos + 2 * count]
    pos += 2 * count
    near_in, near_sum = refs[pos : pos + count], refs[pos + count : pos + 2 * count]
    pos += 2 * count
    far_in = refs[pos : pos + count]
    core_s, core_r, near_s, near_r, far_s, far_r = refs[pos + count :]
    far, near = levels_of(n)
    me = lax.axis_index("dp")
    top, mid, core = everyone_barrier(n, me, far, near)

    def index(t, m, c):
        return (t * near + m) * 2 + c

    core_copies, near_copies, far_copies = [], {}, {}
    for a in range(count):
        copy = pltpu.make_async_remote_copy(
            src_ref=parts[a].at[:, :, 1 - core],
            dst_ref=core_in[a],
            send_sem=core_s.at[a],
            recv_sem=core_r.at[a],
            device_id=(index(top, mid, 1 - core),),
            device_id_type=MESH,
        )
        copy.start()
        core_copies.append(copy)
    for a in range(count):
        core_copies[a].wait_recv()

        def add_core(i, carry, a=a):
            f, m = i // near, lax.rem(i, near)
            core_sum[a][m, f] = (
                parts[a][f, m, core].astype(F32) + core_in[a][f, m].astype(F32)
            ).astype(BF)
            return carry

        lax.fori_loop(0, far * near, add_core, 0)
        for k in range(1, near):
            peer = lax.rem(mid + k, near)
            copy = pltpu.make_async_remote_copy(
                src_ref=core_sum[a].at[peer],
                dst_ref=near_in[a].at[k - 1],
                send_sem=near_s.at[a, k - 1],
                recv_sem=near_r.at[a, k - 1],
                device_id=(index(top, peer, core),),
                device_id_type=MESH,
            )
            copy.start()
            near_copies[a, k] = copy
    for a in range(count):
        for k in range(1, near):
            near_copies[a, k].wait_recv()

        def add_near(f, carry, a=a):
            total = core_sum[a][mid, f].astype(F32)
            for k in range(near - 1):
                total = total + near_in[a][k, f].astype(F32)
            near_sum[a][f] = total.astype(BF)
            return carry

        lax.fori_loop(0, far, add_near, 0)
        for k in range(1, far):
            peer = lax.rem(top + k, far)
            copy = pltpu.make_async_remote_copy(
                src_ref=near_sum[a].at[peer],
                dst_ref=far_in[a].at[k - 1],
                send_sem=far_s.at[a, k - 1],
                recv_sem=far_r.at[a, k - 1],
                device_id=(index(peer, mid, core),),
                device_id_type=MESH,
            )
            copy.start()
            far_copies[a, k] = copy
    for a in range(count):
        for k in range(1, far):
            far_copies[a, k].wait_recv()
        total = near_sum[a][top].astype(F32)
        for k in range(far - 1):
            total = total + far_in[a][k].astype(F32)
        outs[a][...] = total
    for a in range(count):
        core_copies[a].wait_send()
        for k in range(1, near):
            near_copies[a, k].wait_send()
        for k in range(1, far):
            far_copies[a, k].wait_send()


def scatter_all(n, parts):
    far, near = levels_of(n)
    count = len(parts)
    blocks = [p.shape[3:] for p in parts]
    return pl.pallas_call(
        functools.partial(scatter_kernel, n, count),
        out_shape=[jax.ShapeDtypeStruct(b, F32) for b in blocks],
        in_specs=[VMEM_SPEC] * count,
        out_specs=[VMEM_SPEC] * count,
        scratch_shapes=[pltpu.VMEM((far, near) + b, BF) for b in blocks]
        + [pltpu.VMEM((near, far) + b, BF) for b in blocks]
        + [pltpu.VMEM((near - 1, far) + b, BF) for b in blocks]
        + [pltpu.VMEM((far,) + b, BF) for b in blocks]
        + [pltpu.VMEM((far - 1,) + b, BF) for b in blocks]
        + [
            pltpu.SemaphoreType.DMA((count,)),
            pltpu.SemaphoreType.DMA((count,)),
            pltpu.SemaphoreType.DMA((count, near - 1)),
            pltpu.SemaphoreType.DMA((count, near - 1)),
            pltpu.SemaphoreType.DMA((count, far - 1)),
            pltpu.SemaphoreType.DMA((count, far - 1)),
        ],
        compiler_params=pltpu.CompilerParams(
            collective_id=1, has_side_effects=True, vmem_limit_bytes=VMEM_LIMIT
        ),
        name="scatter_grads",
    )(*parts)


def segment_lanes(lengths, position, lane):
    leading = lengths[0, 0]
    finish = leading + lengths[0, 1]
    segment = jnp.where(position < leading, 0, jnp.where(position < finish, 1, 2))
    return lax.rem(lane, 64) == segment


def three_pieces(column):
    high = column.astype(BF)
    rest = column - high.astype(F32)
    middle = rest.astype(BF)
    return high, middle, (rest - middle.astype(F32)).astype(BF)


def own_lanes(lane, half):
    return (lane < 64) if half == 0 else (lane >= 64)


def attend_kernel(
    lengths, x, wq, wk, wv, wo, vec, nb, qaug, kk, vv, mixed, middle, kaug, qbuf, *, tb, lb
):
    frame_count = x.shape[0]
    lane = lax.broadcasted_iota(jnp.int32, (1, 128), 1)
    table = vec[...].astype(F32).T
    gain, shift, bq, bv, bo = (table[i : i + 1] for i in range(5))

    def project(i, carry):
        r = rows(i * lb, lb)
        xhat, _ = normal_stats(x[r, :].astype(F32))
        normed = (xhat * gain + shift).astype(BF)
        nb[r, :] = normed
        qbuf[r, :] = ((dot_nt(normed, wq[...]) + bq).astype(BF).astype(F32) * 0.125).astype(BF)
        kk[r, :] = dot_nt(normed, wk[...]).astype(BF)
        vv[r, :] = (dot_nt(normed, wv[...]) + bv).astype(BF)
        position = lax.broadcasted_iota(jnp.int32, (lb, 128), 0) + i * lb
        lanes = lax.broadcasted_iota(jnp.int32, (lb, 128), 1)
        same = segment_lanes(lengths, position, lanes)
        slot = lax.rem(lanes, 64)
        kaug[r, :] = jnp.where(
            slot < 3, jnp.where(same, 0.0, EXCLUDED), jnp.where(slot < 6, 1.0, 0.0)
        ).astype(BF)
        return carry

    lax.fori_loop(0, frame_count // lb, project, 0)

    def pair_step(p, carry):
        cols = rows(p * 128, 128)
        for half in range(2):
            own = own_lanes(lane, half)
            base = 64 - 64 * half
            key = jnp.where(own, kk[:, cols], kaug[...])
            value = jnp.where(own, vv[:, cols], jnp.ones((1, 128), BF))
            head = pl.multiple_of((2 * p + half) * 128, 128)

            def block(i, inner, half=half, own=own, base=base, key=key, value=value, head=head):
                r = rows(i * tb, tb)
                position = lax.broadcasted_iota(jnp.int32, (tb, 128), 0) + i * tb
                lanes = lax.broadcasted_iota(jnp.int32, (tb, 128), 1)
                mark = jnp.where(segment_lanes(lengths, position, lanes), 1.0, 0.0).astype(BF)
                query = jnp.where(own, qbuf[r, cols], mark)
                scores = dot_nt(query, key)
                top = jnp.max(scores, axis=1, keepdims=True)
                raised = jnp.exp(scores - top).astype(BF)
                got = dot_nn(raised, value)
                total = got[:, base : base + 1]
                got = (got * (1.0 / total)).astype(BF)
                if half == 0:
                    mixed[r, cols] = got
                else:
                    mixed[r, cols] = jnp.where(own, got, mixed[r, cols])
                high, mid, low = three_pieces(-(top + jnp.log(total)))
                query = jnp.where(lane == base + 3, high, query)
                query = jnp.where(lane == base + 4, mid, query)
                qaug[r, pl.ds(head, 128)] = jnp.where(lane == base + 5, low, query)
                return inner

            lax.fori_loop(0, frame_count // tb, block, 0, unroll=True)
        return carry

    lax.fori_loop(0, HEADS // 2, pair_step, 0)

    def finish(i, carry):
        r = rows(i * lb, lb)
        middle[r, :] = x[r, :].astype(F32) + (dot_nt(mixed[r, :], wo[...]) + bo)
        return carry

    lax.fori_loop(0, frame_count // lb, finish, 0)


def attend(lengths, x, wq, wk, wv, wo, vec):
    frame_count, width = x.shape
    low = jax.ShapeDtypeStruct((frame_count, width), BF)
    return pl.pallas_call(
        functools.partial(attend_kernel, tb=512, lb=512),
        out_shape=[
            low,
            jax.ShapeDtypeStruct((frame_count, HEADS * 128), BF),
            low,
            low,
            low,
            jax.ShapeDtypeStruct((frame_count, width), F32),
            jax.ShapeDtypeStruct((frame_count, 128), BF),
        ],
        in_specs=[SMEM_SPEC] + [VMEM_SPEC] * 6,
        out_specs=[VMEM_SPEC] * 7,
        scratch_shapes=[pltpu.VMEM((frame_count, width), BF)],
        compiler_params=pltpu.CompilerParams(vmem_limit_bytes=VMEM_LIMIT),
        name="attend_forward",
    )(lengths, x, wq, wk, wv, wo, vec)


def feed_kernel(
    lengths,
    middle,
    gout,
    mixed,
    wup,
    wdn,
    wo,
    vec,
    bup,
    layer_out,
    gmid,
    dmixed,
    dwo,
    dwup,
    dwdn,
    sums,
    sum_up,
    nb,
    act,
    gup,
    glow,
    gbl,
    *,
    tb,
):
    frame_count = middle.shape[0]
    finish = lengths[0, 0] + lengths[0, 1]
    table = vec[...].astype(F32).T
    gain, shift, bdn = (table[i : i + 1] for i in range(5, 8))
    sums[...] = jnp.zeros_like(sums)
    sum_up[...] = jnp.zeros_like(sum_up)

    def block(i, carry):
        r = rows(i * tb, tb)
        valid = lax.broadcasted_iota(jnp.int32, (tb, 1), 0) + i * tb < finish
        mid = middle[r, :]
        xhat, inv = normal_stats(mid)
        normed = (xhat * gain + shift).astype(BF)
        nb[r, :] = normed
        up = dot_nt(normed, wup[...]) + bup[...].astype(F32)
        cdf = 0.5 * (1.0 + lax.erf(up * (1.0 / math.sqrt(2.0))))
        low = (up * cdf).astype(BF)
        act[r, :] = low
        down = dot_nt(low, wdn[...]) + bdn
        layer_out[r, :] = jnp.where(valid, mid + down, 0.0).astype(BF)
        grow = jnp.where(valid, gout[r, :].astype(F32), 0.0)
        gl = grow.astype(BF)
        glow[r, :] = gl
        slope = cdf + up * jnp.exp(-0.5 * up * up) * (1.0 / math.sqrt(2.0 * math.pi))
        gu = (dot_nn(gl, wdn[...]) * slope).astype(BF)
        gup[r, :] = gu
        gn = dot_nn(gu, wup[...])
        scaled = gn * gain
        gm = grow + inv * (
            scaled
            - jnp.mean(scaled, axis=-1, keepdims=True)
            - xhat * jnp.mean(scaled * xhat, axis=-1, keepdims=True)
        )
        gmid[r, :] = gm
        gb = gm.astype(BF)
        gbl[r, :] = gb
        dmixed[r, :] = dot_nn(gb, wo[...]).astype(BF)
        sums[0:1, :] += jnp.sum(gb.astype(F32), axis=0, keepdims=True)
        sums[1:2, :] += jnp.sum(gn * xhat, axis=0, keepdims=True)
        sums[2:3, :] += jnp.sum(gn, axis=0, keepdims=True)
        sums[3:4, :] += jnp.sum(grow, axis=0, keepdims=True)
        sum_up[0:1, :] += jnp.sum(gu.astype(F32), axis=0, keepdims=True)
        return carry

    lax.fori_loop(0, frame_count // tb, block, 0)
    dwo[...] = dot_tn(gbl[...], mixed[...]).astype(BF)

    def weights(i, carry):
        c = rows(i * 512, 512)
        dwup[c, :] = dot_tn(gup[:, c], nb[...]).astype(BF)
        dwdn[:, c] = dot_tn(glow[...], act[:, c]).astype(BF)
        return carry

    lax.fori_loop(0, wup.shape[0] // 512, weights, 0)


def feed(lengths, middle, gout, mixed, wup, wdn, wo, vec, bup):
    frame_count, width = middle.shape
    hidden = wup.shape[0]
    low = jax.ShapeDtypeStruct((frame_count, width), BF)
    return pl.pallas_call(
        functools.partial(feed_kernel, tb=256),
        out_shape=[
            low,
            jax.ShapeDtypeStruct((frame_count, width), F32),
            low,
            jax.ShapeDtypeStruct((width, width), BF),
            jax.ShapeDtypeStruct((hidden, width), BF),
            jax.ShapeDtypeStruct((width, hidden), BF),
            jax.ShapeDtypeStruct((8, width), F32),
            jax.ShapeDtypeStruct((8, hidden), F32),
        ],
        in_specs=[SMEM_SPEC] + [VMEM_SPEC] * 8,
        out_specs=[VMEM_SPEC] * 8,
        scratch_shapes=[
            pltpu.VMEM((frame_count, width), BF),
            pltpu.VMEM((frame_count, hidden), BF),
            pltpu.VMEM((frame_count, hidden), BF),
            pltpu.VMEM((frame_count, width), BF),
            pltpu.VMEM((frame_count, width), BF),
        ],
        compiler_params=pltpu.CompilerParams(vmem_limit_bytes=VMEM_LIMIT),
        name="feed_forward_both",
    )(lengths, middle, gout, mixed, wup, wdn, wo, vec, bup)


def attend_back_kernel(
    x,
    gmid,
    nb,
    qaug,
    kk,
    vv,
    mixed,
    dmixed,
    kaug,
    wq,
    wk,
    wv,
    vec,
    grad_x,
    dwq,
    dwk,
    dwv,
    sums,
    dq,
    dqb,
    dkt,
    dvt,
    *,
    ub,
    lb,
):
    frame_count = x.shape[0]
    lane = lax.broadcasted_iota(jnp.int32, (1, 128), 1)
    gain = vec[...].astype(F32).T[0:1]

    def pair_step(p, carry):
        cols = rows(p * 128, 128)
        grad_pair = dmixed[:, cols]
        product = grad_pair.astype(F32) * mixed[:, cols].astype(F32)
        for half in range(2):
            own = own_lanes(lane, half)
            base = 64 - 64 * half
            delta = jnp.sum(jnp.where(own, product, 0.0), axis=1, keepdims=True)
            high, mid, low = three_pieces(-delta)
            grad = jnp.where(own, grad_pair, jnp.zeros((1, 128), BF))
            grad = jnp.where(lane == base + 3, high, grad)
            grad = jnp.where(lane == base + 4, mid, grad)
            grad = jnp.where(lane == base + 5, low, grad)
            query = qaug[:, pl.ds(pl.multiple_of((2 * p + half) * 128, 128), 128)]
            here = pl.ds(pl.multiple_of(p * 128 + 64 * half, 64), 64)
            part = slice(64 * half, 64 * half + 64)
            ones = jnp.where(
                (lane >= base + 3) & (lane < base + 6), jnp.ones((1, 128), F32), 0.0
            ).astype(BF)

            def block(i, inner):
                r = rows(i * ub, ub)
                key = jnp.where(own, kk[r, cols], kaug[r, :])
                value = jnp.where(own, vv[r, cols], ones)
                probs = jnp.exp(dot_nt(query, key))
                low_probs = probs.astype(BF)
                gs = (probs * dot_nt(grad, value)).astype(BF)
                dvt[here, r] = dot_tn(grad, low_probs)[part].astype(BF)
                dkt[here, r] = dot_tn(query, gs)[part].astype(BF)
                step = dot_nn(gs, kk[r, cols])
                if i == 0:
                    dq[...] = step
                else:
                    dq[...] += step
                return inner

            for i in range(frame_count // ub):
                block(i, 0)
            done = (dq[...] * 0.125).astype(BF)
            if half == 0:
                dqb[:, cols] = done
            else:
                dqb[:, cols] = jnp.where(own, done, dqb[:, cols])
        return carry

    lax.fori_loop(0, HEADS // 2, pair_step, 0)
    sums[...] = jnp.zeros_like(sums)

    def finish(i, carry):
        r = rows(i * lb, lb)
        gn = dot_nn(dqb[r, :], wq[...]) + dot_tn(dkt[:, r], wk[...]) + dot_tn(dvt[:, r], wv[...])
        xhat, inv = normal_stats(x[r, :].astype(F32))
        scaled = gn * gain
        grad_x[r, :] = (
            gmid[r, :]
            + inv
            * (
                scaled
                - jnp.mean(scaled, axis=-1, keepdims=True)
                - xhat * jnp.mean(scaled * xhat, axis=-1, keepdims=True)
            )
        ).astype(BF)
        sums[0:1, :] += jnp.sum(gn * xhat, axis=0, keepdims=True)
        sums[1:2, :] += jnp.sum(gn, axis=0, keepdims=True)
        sums[2:3, :] += jnp.sum(dqb[r, :].astype(F32), axis=0, keepdims=True)
        return carry

    lax.fori_loop(0, frame_count // lb, finish, 0)
    sums[3:4, :] = dot_nt(jnp.ones((8, frame_count), BF), dvt[...])[0:1]
    dwq[...] = dot_tn(dqb[...], nb[...]).astype(BF)
    dwk[...] = dot_nn(dkt[...], nb[...]).astype(BF)
    dwv[...] = dot_nn(dvt[...], nb[...]).astype(BF)


def attend_back(x, gmid, nb, qaug, kk, vv, mixed, dmixed, kaug, wq, wk, wv, vec):
    frame_count, width = x.shape
    square = jax.ShapeDtypeStruct((width, width), BF)
    return pl.pallas_call(
        functools.partial(attend_back_kernel, ub=512, lb=512),
        out_shape=[
            jax.ShapeDtypeStruct((frame_count, width), BF),
            square,
            square,
            square,
            jax.ShapeDtypeStruct((8, width), F32),
        ],
        in_specs=[VMEM_SPEC] * 13,
        out_specs=[VMEM_SPEC] * 5,
        scratch_shapes=[
            pltpu.VMEM((frame_count, 128), F32),
            pltpu.VMEM((frame_count, width), BF),
            pltpu.VMEM((width, frame_count), BF),
            pltpu.VMEM((width, frame_count), BF),
        ],
        compiler_params=pltpu.CompilerParams(vmem_limit_bytes=VMEM_LIMIT),
        name="attend_backward",
    )(x, gmid, nb, qaug, kk, vv, mixed, dmixed, kaug, wq, wk, wv, vec)


def bits_differ(a, b, size):
    total, bit = 0, 1
    while bit < size:
        total = total + bit * lax.rem(a // bit + b // bit, 2)
        bit *= 2
    return total


def remote(src, dst, send, recv, device):
    return pltpu.make_async_remote_copy(
        src_ref=src,
        dst_ref=dst,
        send_sem=send,
        recv_sem=recv,
        device_id=(device,),
        device_id_type=MESH,
    )


def spread_rows(blocks, share, width):
    count, height, lanes = blocks.shape
    source = lax.broadcasted_iota(jnp.int32, (lanes, width), 0)
    target = lax.broadcasted_iota(jnp.int32, (lanes, width), 1)
    pick = jnp.where(source == lax.rem(target, share), 1.0, 0.0).astype(BF)
    spread = dot_nn(blocks.reshape(count * height, lanes).astype(BF), pick)
    owner = lax.broadcasted_iota(jnp.int32, (count, height, width), 0)
    place = lax.broadcasted_iota(jnp.int32, (count, height, width), 2)
    spread = spread.reshape(count, height, width)
    return jnp.sum(jnp.where(owner == place // share, spread, 0.0), axis=0)


SECOND_DUTIES = ((0, 0, 2), (1, 0, 3), (2, 1, 1), (4, 1, 2), (6, 1, 3))


def gather_attend_kernel(n, tb, lb, *refs):
    (lengths, x, sq, sk, sv, so, su, sd) = refs[:8]
    vectors, refs = refs[8:17], refs[17:]
    (wq, wk, wv, wo, wup, wdn, table, bup, qq_h, kk_h, vv_h, raised_h, part_h) = refs[:13]
    (nb_h, mixed_h, middle_h) = refs[13:16]
    (xhat, nb, mixed, middle, kaug, qbuf, kbuf, vbuf, stage, part, svec, vec) = refs[16:28]
    (own_sem, near_s, near_r, core_s, core_r, far_s, far_r, fwd_s, fwd_r) = refs[28:37]
    (bown_sem, bfar_s, bfar_r, bnear_s, bnear_r, bcore_s, bcore_r, out_sem, end_sem) = refs[37:46]
    stage_sem = refs[46]
    far, near = levels_of(n)
    share = 512 // n
    frame_count, width = x.shape
    pairs = HEADS // 2
    me = lax.axis_index("dp")
    top, mid, core = announce(n, me, far, near)
    lane = lax.broadcasted_iota(jnp.int32, (1, 128), 1)
    svec[...] = jnp.zeros_like(svec)
    for v, vector in enumerate(vectors):
        length = vector.shape[0]
        svec[v : v + 1, :length] = vector[...].astype(F32).reshape(1, length)

    def index(t, m, c):
        return (t * near + m) * 2 + c

    sibling = index(top, mid, 1 - core)
    first = list(zip((sq, sk, sv), (wq, wk, wv)))
    second = list(zip((svec, so, su, sd), (vec, wo, wup, wdn)))

    def near_copy(a, k):
        peer = index(top, lax.rem(mid + k, near), core)
        src, dst = first[a]
        return remote(src, dst.at[top, mid, core], near_s.at[a, k - 1], near_r.at[a, k - 1], peer)

    def core_copy(a):
        ref = first[a][1].at[top, :, core]
        return remote(ref, ref, core_s.at[a], core_r.at[a], sibling)

    def far_copy(a, k):
        ref = first[a][1].at[top, :, core]
        peer = index(bits_differ(top, k, far), mid, core)
        return remote(ref, ref, far_s.at[a, k - 1], far_r.at[a, k - 1], peer)

    def fwd_copy(a, k):
        ref = first[a][1].at[bits_differ(top, k, far), :, core]
        return remote(ref, ref, fwd_s.at[a, k - 1], fwd_r.at[a, k - 1], sibling)

    def bfar_copy(a, k):
        src, dst = second[a]
        peer = index(bits_differ(top, k, far), mid, core)
        return remote(src, dst.at[top, mid, core], bfar_s.at[a, k - 1], bfar_r.at[a, k - 1], peer)

    def bnear_copy(a, k):
        ref = second[a][1].at[:, mid, core]
        peer = index(top, lax.rem(mid + k, near), core)
        return remote(ref, ref, bnear_s.at[a, k - 1], bnear_r.at[a, k - 1], peer)

    def bcore_copy(a):
        ref = second[a][1].at[:, :, core]
        return remote(ref, ref, bcore_s.at[a], bcore_r.at[a], sibling)

    def own_copy(a):
        src, dst = first[a]
        return pltpu.make_async_copy(src, dst.at[top, mid, core], own_sem.at[a])

    def bown_copy(a):
        src, dst = second[a]
        return pltpu.make_async_copy(src, dst.at[top, mid, core], bown_sem.at[a])

    def stats(i, carry):
        r = rows(i * lb, lb)
        xhat[r, :] = normal_stats(x[r, :].astype(F32))[0]
        part[r, :] = jnp.zeros((lb, 128), F32)
        position = lax.broadcasted_iota(jnp.int32, (lb, 128), 0) + i * lb
        lanes = lax.broadcasted_iota(jnp.int32, (lb, 128), 1)
        same = segment_lanes(lengths, position, lanes)
        slot = lax.rem(lanes, 64)
        kaug[r, :] = jnp.where(
            slot < 3, jnp.where(same, 0.0, EXCLUDED), jnp.where(slot < 6, 1.0, 0.0)
        ).astype(BF)
        return carry

    lax.fori_loop(0, frame_count // lb, stats, 0)
    await_peers(far, near)
    for k in range(1, far):
        bfar_copy(0, k).start()
    bown_copy(0).start()
    for a in range(3):
        for k in range(1, near):
            near_copy(a, k).start()
        own_copy(a).start()
    for a in range(1, 4):
        for k in range(1, far):
            bfar_copy(a, k).start()
        bown_copy(a).start()

    bown_copy(0).wait()
    for k in range(1, far):
        bfar_copy(0, k).wait_recv()
    for k in range(1, near):
        bnear_copy(0, k).start()
    for a in range(3):
        own_copy(a).wait()
        for k in range(1, near):
            near_copy(a, k).wait_recv()
        core_copy(a).start()
    for k in range(1, near):
        bnear_copy(0, k).wait_recv()
    bcore_copy(0).start()
    for k in range(1, far):
        for a in range(3):
            far_copy(a, k).start()
    bcore_copy(0).wait_recv()
    blocks = vec[...].reshape(n, 16, 128)
    table[...] = spread_rows(blocks, share, width)
    gain, shift = table[0:1, :], table[1:2, :]

    def norm(i, carry):
        r = rows(i * lb, lb)
        nb[r, :] = (xhat[r, :] * gain + shift).astype(BF)
        return carry

    lax.fori_loop(0, frame_count // lb, norm, 0)
    nb_copy = pltpu.make_async_copy(nb, nb_h, end_sem.at[0])
    nb_copy.start()
    for a in range(3):
        core_copy(a).wait_recv()

    def second_near(a):
        bown_copy(a).wait()
        for k in range(1, far):
            bfar_copy(a, k).wait_recv()
        for k in range(1, near):
            bnear_copy(a, k).start()

    def second_core(a):
        for k in range(1, near):
            bnear_copy(a, k).wait_recv()
        bcore_copy(a).start()

    second_near(1)

    def out_copies(p, slot):
        cols = rows(p * 128, 128)
        return [
            pltpu.make_async_copy(buf.at[slot], out.at[:, cols], out_sem.at[slot, a])
            for a, (buf, out) in enumerate(((qbuf, qq_h), (kbuf, kk_h), (vbuf, vv_h)))
        ]

    def stage_copies(p, half):
        return [
            pltpu.make_async_copy(
                stage.at[half, j, :, pl.ds(b * tb, tb)],
                raised_h.at[2 * p + half, b, pl.ds(j * tb, tb)],
                stage_sem.at[half, j, b],
            )
            for j in range(frame_count // tb)
            for b in range(frame_count // tb)
        ]

    def pair_step(i, carry):
        p = bits_differ(top, i, far)
        slot = lax.rem(i, 2)
        cols = rows(p * 128, 128)

        @pl.when(i > 0)
        def _():
            for a in range(3):
                fwd_copy(a, i).wait_recv()

        @pl.when(i > 1)
        def _():
            for copy in out_copies(bits_differ(top, i - 2, far), slot):
                copy.wait()

        weights = jnp.concatenate(
            [w[p].reshape(128, width) for w in (wq, wk, wv)], axis=0
        )
        bq, bv = table[2:3, cols], table[3:4, cols]

        def project(j, inner):
            r = rows(j * lb, lb)
            got = dot_nt(nb[r, :], weights)
            qbuf[slot, r, :] = ((got[:, :128] + bq).astype(BF).astype(F32) * 0.125).astype(BF)
            kbuf[slot, r, :] = got[:, 128:256].astype(BF)
            vbuf[slot, r, :] = (got[:, 256:] + bv).astype(BF)
            return inner

        lax.fori_loop(0, frame_count // lb, project, 0)
        for half in range(2):
            own = own_lanes(lane, half)
            base = 64 - 64 * half
            key = jnp.where(own, kbuf[slot], kaug[...])
            value = jnp.where(own, vbuf[slot], jnp.ones((1, 128), BF))

            @pl.when(i > 0)
            def _():
                for copy in stage_copies(bits_differ(top, i - 1, far), half):
                    copy.wait()

            def block(j):
                r = pl.ds(j * tb, tb)
                position = lax.broadcasted_iota(jnp.int32, (tb, 128), 0) + j * tb
                lanes = lax.broadcasted_iota(jnp.int32, (tb, 128), 1)
                mark = jnp.where(segment_lanes(lengths, position, lanes), 1.0, 0.0).astype(BF)
                query = jnp.where(own, qbuf[slot, r, :], mark)
                scores = dot_nt(query, key)
                peak = jnp.max(scores, axis=1, keepdims=True)
                raised = jnp.exp(scores - peak).astype(BF)
                stage[half, j] = raised
                got = dot_nn(raised, value)
                inverse = 1.0 / got[:, base : base + 1]
                part[r, :] = jnp.where(lane == 2 * p + half, inverse, part[r, :])
                got = (got * inverse).astype(BF)
                if half == 0:
                    mixed[r, cols] = got
                else:
                    mixed[r, cols] = jnp.where(own, got, mixed[r, cols])
            for j in range(frame_count // tb):
                block(j)
            for copy in stage_copies(p, half):
                copy.start()
            if half == 0:

                @pl.when(i < far - 1)
                def _():
                    for a in range(3):
                        far_copy(a, i + 1).wait_recv()
                        fwd_copy(a, i + 1).start()

            for step, duty, a in SECOND_DUTIES:
                if step % 2 == half:
                    act = second_near if duty == 0 else second_core
                    pl.when(i == step // 2)(functools.partial(act, a))

        for copy in out_copies(p, slot):
            copy.start()
        return carry

    lax.fori_loop(0, pairs, pair_step, 0)
    mixed_copy = pltpu.make_async_copy(mixed, mixed_h, end_sem.at[1])
    mixed_copy.start()
    part_copy = pltpu.make_async_copy(part, part_h, end_sem.at[3])
    part_copy.start()
    bcore_copy(1).wait_recv()
    out_weight = wo[...].reshape(width, width)
    bo = table[4:5, :]
    bup[...] = spread_rows(vec[...].reshape(n, 16, 128)[:, 8:16], 4 * share, 4 * width)

    def finish(i, carry):
        r = rows(i * lb, lb)
        middle[r, :] = x[r, :].astype(F32) + (dot_nt(mixed[r, :], out_weight) + bo)
        return carry

    lax.fori_loop(0, frame_count // lb, finish, 0)
    middle_copy = pltpu.make_async_copy(middle, middle_h, end_sem.at[2])
    middle_copy.start()
    for i in (pairs - 2, pairs - 1):
        for copy in out_copies(bits_differ(top, i, far), i % 2):
            copy.wait()
    for half in range(2):
        for copy in stage_copies(bits_differ(top, pairs - 1, far), half):
            copy.wait()
    part_copy.wait()
    nb_copy.wait()
    mixed_copy.wait()
    for a in range(3):
        for k in range(1, near):
            near_copy(a, k).wait_send()
        core_copy(a).wait_send()
        for k in range(1, far):
            far_copy(a, k).wait_send()
            fwd_copy(a, k).wait_send()
    bcore_copy(2).wait_recv()
    bcore_copy(3).wait_recv()
    for a in range(4):
        for k in range(1, far):
            bfar_copy(a, k).wait_send()
        for k in range(1, near):
            bnear_copy(a, k).wait_send()
        bcore_copy(a).wait_send()
    middle_copy.wait()


def gather_attend(n, lengths, x, shards, vectors):
    far, near = levels_of(n)
    frame_count, width = x.shape
    lead = (far, near, 2)
    share = width // n
    square = jax.ShapeDtypeStruct(lead + (share, width), BF)
    low = jax.ShapeDtypeStruct((frame_count, width), BF)
    dma = pltpu.SemaphoreType.DMA
    tb = 512
    return pl.pallas_call(
        functools.partial(gather_attend_kernel, n, tb, 512),
        out_shape=[
            square,
            square,
            square,
            square,
            jax.ShapeDtypeStruct(lead + (4 * share, width), BF),
            jax.ShapeDtypeStruct(lead + (share, 4 * width), BF),
            jax.ShapeDtypeStruct((16, width), F32),
            jax.ShapeDtypeStruct((8, 4 * width), F32),
            low,
            low,
            low,
            jax.ShapeDtypeStruct((HEADS, frame_count // tb, frame_count, tb), BF),
            jax.ShapeDtypeStruct((frame_count, 128), F32),
            low,
            low,
            jax.ShapeDtypeStruct((frame_count, width), F32),
        ],
        in_specs=[SMEM_SPEC, VMEM_SPEC] + [HBM_SPEC] * 6 + [VMEM_SPEC] * 9,
        out_specs=[VMEM_SPEC] * 4 + [HBM_SPEC] * 2 + [VMEM_SPEC] * 2 + [HBM_SPEC] * 8,
        scratch_shapes=[
            pltpu.VMEM((frame_count, width), F32),
            pltpu.VMEM((frame_count, width), BF),
            pltpu.VMEM((frame_count, width), BF),
            pltpu.VMEM((frame_count, width), F32),
            pltpu.VMEM((frame_count, 128), BF),
            pltpu.VMEM((2, frame_count, 128), BF),
            pltpu.VMEM((2, frame_count, 128), BF),
            pltpu.VMEM((2, frame_count, 128), BF),
            pltpu.VMEM((2, frame_count // tb, tb, frame_count), BF),
            pltpu.VMEM((frame_count, 128), F32),
            pltpu.VMEM((16, 128), F32),
            pltpu.VMEM(lead + (16, 128), F32),
            dma((3,)),
            dma((3, near - 1)),
            dma((3, near - 1)),
            dma((3,)),
            dma((3,)),
            dma((3, far - 1)),
            dma((3, far - 1)),
            dma((3, far - 1)),
            dma((3, far - 1)),
            dma((4,)),
            dma((4, far - 1)),
            dma((4, far - 1)),
            dma((4, near - 1)),
            dma((4, near - 1)),
            dma((4,)),
            dma((4,)),
            dma((2, 3)),
            dma((4,)),
            dma((2, frame_count // tb, frame_count // tb)),
        ],
        compiler_params=pltpu.CompilerParams(
            collective_id=2, has_side_effects=True, vmem_limit_bytes=VMEM_LIMIT
        ),
        name="gather_attend",
    )(lengths, x, *shards, *vectors)


def both_back_kernel(n, tb, ub, lb, *refs):
    (lengths, middle_h, gout_h, mixed_h, wo_h, wup_h, wdn_h, x_h, nb_h) = refs[:9]
    (qq_h, kk_h, vv_h, raised_h, part, wq, wk, wv, table, bup) = refs[9:19]
    (layer_h, grad_h, gq, gk, gv, go, gu, gd, gc) = refs[19:28]
    (wide, dqb, x, grad, gmid, mixed, dmixed, layer, nb, wo, wup, wdn) = refs[28:40]
    (qbuf, kbuf, vbuf, dq, dkt, dvt, sums, sum_up, biases) = refs[40:49]
    (parts, core_in, core_sum, near_in, near_sum, far_in) = refs[49:55]
    (core_in2, near_in2, near_sum2, far_in2) = (refs[55 + 3 * j : 58 + 3 * j] for j in range(4))
    (cparts, ccore_in, ccore_sum, cnear_in, cnear_sum, cfar_in) = refs[67:73]
    (row_sem, weight_sem, in_sem, end_sem, raised_sem) = refs[73:78]
    (core_s, core_r, near_s, near_r, far_s, far_r) = refs[78:84]
    (core2_s, core2_r, near2_s, near2_r, far2_s, far2_r) = refs[84:90]
    (ccore_s, ccore_r, cnear_s, cnear_r, cfar_s, cfar_r) = refs[90:]
    normed, glow, gbl = dqb, x, grad
    far, near = levels_of(n)
    frame_count, width = gmid.shape
    hidden = 4 * width
    share = width // n
    pairs = HEADS // 2
    last = pairs - 1
    me = lax.axis_index("dp")
    top, mid, core = announce(n, me, far, near)
    lane = lax.broadcasted_iota(jnp.int32, (1, 128), 1)
    finish_row = lengths[0, 0] + lengths[0, 1]

    def index(t, m, c):
        return (t * near + m) * 2 + c

    sibling = index(top, mid, 1 - core)
    big = (wo, wup, wdn)

    def row_copies(i):
        r = rows(i * tb, tb)
        return [
            pltpu.make_async_copy(middle_h.at[r], gmid.at[r], row_sem.at[i, 0]),
            pltpu.make_async_copy(gout_h.at[r], glow.at[r], row_sem.at[i, 1]),
        ]

    def layer_copy(i):
        r = rows(i * tb, tb)
        return pltpu.make_async_copy(layer.at[r], layer_h.at[r], row_sem.at[i, 2])

    weight_copies = [
        pltpu.make_async_copy(src, dst, weight_sem.at[a])
        for a, (src, dst) in enumerate(
            ((wup_h, wup), (wdn_h, wdn), (wo_h, wo), (mixed_h, mixed), (nb_h, nb))
        )
    ]
    for copy in row_copies(0) + weight_copies[:3]:
        copy.start()
    for i in range(1, frame_count // tb):
        for copy in row_copies(i):
            copy.start()
    for copy in weight_copies[3:]:
        copy.start()

    def core2_copy(a):
        return remote(
            big[a].at[:, :, 1 - core], core_in2[a], core2_s.at[a], core2_r.at[a], sibling
        )

    def near2_copy(a, k):
        peer = lax.rem(mid + k, near)
        return remote(
            big[a].at[:, peer, core],
            near_in2[a].at[k - 1],
            near2_s.at[a, k - 1],
            near2_r.at[a, k - 1],
            index(top, peer, core),
        )

    def far2_copy(a, k):
        peer = bits_differ(top, k, far)
        return remote(
            near_sum2[a].at[peer],
            far_in2[a].at[k - 1],
            far2_s.at[a, k - 1],
            far2_r.at[a, k - 1],
            index(peer, mid, core),
        )

    def second_near(a):
        core2_copy(a).wait_recv()

        def add(f, inner):
            big[a][f, :, core] = (
                big[a][f, :, core].astype(F32) + core_in2[a][f].astype(F32)
            ).astype(BF)
            return inner

        lax.fori_loop(0, far, add, 0)
        for k in range(1, near):
            near2_copy(a, k).start()

    def second_far(a):
        for k in range(1, near):
            near2_copy(a, k).wait_recv()

        def add(f, inner):
            total = big[a][f, mid, core].astype(F32)
            for k in range(near - 1):
                total = total + near_in2[a][k, f].astype(F32)
            near_sum2[a][f] = total.astype(BF)
            return inner

        lax.fori_loop(0, far, add, 0)
        for k in range(1, far):
            far2_copy(a, k).start()

    def core_copy(j):
        return remote(
            parts.at[j, :, :, 1 - core], core_in.at[j], core_s.at[j], core_r.at[j], sibling
        )

    def near_copy(j, k):
        peer = lax.rem(mid + k, near)
        return remote(
            core_sum.at[j, peer],
            near_in.at[j, k - 1],
            near_s.at[j, k - 1],
            near_r.at[j, k - 1],
            index(top, peer, core),
        )

    def far_copy(j):
        peer = index(bits_differ(top, last - j, far), mid, core)
        return remote(near_sum.at[j], far_in.at[j], far_s.at[j], far_r.at[j], peer)

    def add_core(j):
        for m in range(near):
            core_sum[j, m] = (
                parts[j, :, m, core].astype(F32) + core_in[j, :, m].astype(F32)
            ).astype(BF)

    def add_near(j):
        total = core_sum[j, mid].astype(F32)
        for k in range(near - 1):
            total = total + near_in[j, k].astype(F32)
        return total

    def pair_near(j):
        core_copy(j).wait_recv()
        add_core(j)
        for k in range(1, near):
            near_copy(j, k).start()

    def pair_far(j):
        for k in range(1, near):
            near_copy(j, k).wait_recv()
        near_sum[j] = add_near(j).astype(BF)
        far_copy(j).start()

    def in_copies(p, slot):
        cols = rows(p * 128, 128)
        return [
            pltpu.make_async_copy(src.at[:, cols], buf.at[slot], in_sem.at[slot, a])
            for a, (src, buf) in enumerate(((qq_h, qbuf), (kk_h, kbuf), (vv_h, vbuf)))
        ]

    def raised_copies(p, half):
        return [
            pltpu.make_async_copy(
                raised_h.at[2 * p + half, j], wide.at[3 * half + j], raised_sem.at[half, j]
            )
            for j in range(frame_count // ub)
        ]

    gain2, shift2, bdn = (table[i : i + 1, :] for i in range(5, 8))
    sums[...] = jnp.zeros_like(sums)
    sum_up[...] = jnp.zeros_like(sum_up)
    for copy in weight_copies[:3]:
        copy.wait()

    def block(i, carry):
        r = rows(i * tb, tb)
        for copy in row_copies(i):
            copy.wait()
        up_rows, down_rows = wup[...].reshape(hidden, width), wdn[...].reshape(width, hidden)
        valid = lax.broadcasted_iota(jnp.int32, (tb, 1), 0) + i * tb < finish_row
        row = gmid[r, :]
        xhat, inv = normal_stats(row)
        normed_rows = (xhat * gain2 + shift2).astype(BF)
        normed[r, :] = normed_rows
        up = dot_nt(normed_rows, up_rows) + bup[0:1, :]
        cdf = 0.5 * (1.0 + lax.erf(up * (1.0 / math.sqrt(2.0))))
        low = (up * cdf).astype(BF)
        for c in range(4):
            wide[c, r, :] = low[:, 512 * c : 512 * c + 512]
        down = dot_nt(low, down_rows) + bdn
        layer[r, :] = jnp.where(valid, row + down, 0.0).astype(BF)
        layer_copy(i).start()
        grow = jnp.where(valid, glow[r, :].astype(F32), 0.0)
        gl = grow.astype(BF)
        glow[r, :] = gl
        slope = cdf + up * jnp.exp(-0.5 * up * up) * (1.0 / math.sqrt(2.0 * math.pi))
        gu = (dot_nn(gl, down_rows) * slope).astype(BF)
        for c in range(4):
            wide[4 + c, r, :] = gu[:, 512 * c : 512 * c + 512]
        gn = dot_nn(gu, up_rows)
        scaled = gn * gain2
        gm = grow + inv * (
            scaled
            - jnp.mean(scaled, axis=-1, keepdims=True)
            - xhat * jnp.mean(scaled * xhat, axis=-1, keepdims=True)
        )
        gmid[r, :] = gm
        gb = gm.astype(BF)
        gbl[r, :] = gb
        dmixed[r, :] = dot_nn(gb, wo[...].reshape(width, width)).astype(BF)
        sums[4:5, :] += jnp.sum(gb.astype(F32), axis=0, keepdims=True)
        sums[5:6, :] += jnp.sum(gn * xhat, axis=0, keepdims=True)
        sums[6:7, :] += jnp.sum(gn, axis=0, keepdims=True)
        sums[7:8, :] += jnp.sum(grow, axis=0, keepdims=True)
        sum_up[0:1, :] += jnp.sum(gu.astype(F32), axis=0, keepdims=True)
        return carry

    lax.fori_loop(0, frame_count // tb, block, 0)
    weight_copies[3].wait()
    wo[...] = dot_tn(gbl[...], mixed[...]).astype(BF).reshape(wo.shape)
    await_peers(far, near)
    core2_copy(0).start()

    def down_part(c, carry):
        got = dot_tn(glow[...], wide[c]).astype(BF)
        wdn[:, :, :, :, rows(c * 512, 512)] = got.reshape(far, near, 2, share, 512)
        return carry

    lax.fori_loop(0, 4, down_part, 0)
    core2_copy(2).start()
    x_copy = pltpu.make_async_copy(x_h, x, end_sem.at[0])
    x_copy.start()
    for copy in raised_copies(bits_differ(top, last, far), 0):
        copy.start()
    for copy in in_copies(bits_differ(top, last, far), 0):
        copy.start()
    second_near(0)

    def up_part(c, carry):
        wup[c] = dot_tn(wide[4 + c], normed[...]).astype(BF).reshape(near, 2, 4 * share, width)
        return carry

    lax.fori_loop(0, 4, up_part, 0)
    core2_copy(1).start()
    for copy in raised_copies(bits_differ(top, last, far), 1):
        copy.start()
    plain = sums[...].T
    pieces = sum_up[...].T.reshape(n, 4, share, 8)
    found = jnp.zeros((width, 128), F32)
    for v in range(4, 8):
        found = jnp.where(lane == v, plain[:, v : v + 1], found)
    for k in range(4):
        found = jnp.where(lane == 8 + k, pieces[:, k].reshape(width, 8)[:, 0:1], found)
    biases[...] = found
    second_near(2)
    weight_copies[4].wait()

    def pair_step(i, carry):
        p = bits_differ(top, last - i, far)
        slot = lax.rem(i, 2)
        cols = rows(p * 128, 128)
        for copy in in_copies(p, slot):
            copy.wait()

        @pl.when(i < last)
        def _():
            for copy in in_copies(bits_differ(top, last - i - 1, far), 1 - slot):
                copy.start()

        grad_pair = dmixed[:, cols].astype(F32)
        mixed_pair = mixed[:, cols].astype(F32)
        turned_query = qbuf[slot].T
        for half in range(2):
            own = own_lanes(lane, half)
            base = 64 - 64 * half
            for copy in raised_copies(p, half):
                copy.wait()
            inverse = jnp.sum(jnp.where(lane == 2 * p + half, part[...], 0.0), axis=1, keepdims=True)
            grad_head = jnp.where(own, (grad_pair * inverse).astype(BF), jnp.zeros((1, 128), BF))
            delta = jnp.sum(grad_head.astype(F32) * mixed_pair, axis=1, keepdims=True)
            high, middle_piece, low = three_pieces(-delta)
            grad_head = jnp.where(lane == base + 3, high, grad_head)
            grad_head = jnp.where(lane == base + 4, middle_piece, grad_head)
            grad_head = jnp.where(lane == base + 5, low, grad_head)
            turned_grad = grad_head.T
            here = pl.ds(pl.multiple_of(p * 128 + 64 * half, 64), 64)
            part_rows = slice(64 * half, 64 * half + 64)
            ones = jnp.where(
                (lane >= base + 3) & (lane < base + 6), jnp.ones((1, 128), F32), 0.0
            ).astype(BF)
            for j in range(frame_count // ub):
                r = pl.ds(j * ub, ub)
                value = jnp.where(own, vbuf[slot, r, :], ones)
                weights = wide[3 * half + j]
                gs = (weights.astype(F32) * dot_nt(grad_head, value)).astype(BF)
                dvt[here, r] = dot_nn(turned_grad, weights)[part_rows].astype(BF)
                dkt[here, r] = dot_nn(turned_query, gs)[part_rows].astype(BF)
                step = dot_nn(gs, kbuf[slot, r, :])
                if j == 0:
                    dq[...] = step
                else:
                    dq[...] += step

            @pl.when(i < last)
            def _():
                for copy in raised_copies(bits_differ(top, last - i - 1, far), half):
                    copy.start()

            done = (dq[...] * 0.125).astype(BF)
            if half == 0:
                dqb[:, cols] = done
                pl.when(i == 0)(functools.partial(second_near, 1))
                pl.when(i > 0)(functools.partial(pair_near, i - 1))
                pl.when(i == last)(functools.partial(pair_far, 0))
            else:
                dqb[:, cols] = jnp.where(own, done, dqb[:, cols])
                for step_index, a in ((0, 0), (1, 2), (2, 1)):
                    pl.when(i == step_index)(functools.partial(second_far, a))
                pl.when(i == last)(functools.partial(pair_far, 1))

        pair_rows = rows(p * 128, 128)
        shape = (near, 2, share, width)
        found = (
            dot_tn(dqb[:, cols], nb[...]),
            dot_nn(dkt[pair_rows, :], nb[...]),
            dot_nn(dvt[pair_rows, :], nb[...]),
        )
        for a in range(3):
            parts[i, a] = found[a].astype(BF).reshape(shape)
        core_copy(i).start()
        by_query = dot_tn(dqb[:, cols], jnp.ones((frame_count, 128), BF))
        column = (
            by_query[:, 0:1],
            jnp.sum(dkt[pair_rows, :].astype(F32), axis=1, keepdims=True),
            jnp.sum(dvt[pair_rows, :].astype(F32), axis=1, keepdims=True),
        )
        held = [w[pair_rows, :].astype(F32) for w in (wq, wk, wv)]
        with_rows = sum(g * w for g, w in zip(found, held))
        alone = sum(c * w for c, w in zip(column, held))
        sums[0:1, :] += jnp.sum(with_rows, axis=0, keepdims=True)
        sums[1:2, :] += jnp.sum(alone, axis=0, keepdims=True)
        biases[pair_rows, :] = jnp.where(
            lane == 2, column[0], jnp.where(lane == 3, column[2], biases[pair_rows, :])
        )
        return carry

    sums[...] = jnp.zeros_like(sums)
    lax.fori_loop(0, pairs, pair_step, 0)

    gain, shift = table[0:1, :], table[1:2, :]
    sums[0:1, :] = (sums[0:1, :] - shift * sums[1:2, :]) / gain
    plain = sums[...].T
    found = jnp.where(lane == 0, plain[:, 0:1], biases[...])
    found = jnp.where(lane == 1, plain[:, 1:2], found)
    cparts[...] = found.astype(BF).reshape(far, near, 2, share, 128)
    ccore = remote(cparts.at[:, :, 1 - core], ccore_in, ccore_s, ccore_r, sibling)
    ccore.start()
    pair_near(last)
    pair_far(last - 1)
    cnear, cfar = [], []
    for k in range(1, near):
        peer = lax.rem(mid + k, near)
        cnear.append(
            remote(
                ccore_sum.at[peer],
                cnear_in.at[k - 1],
                cnear_s.at[k - 1],
                cnear_r.at[k - 1],
                index(top, peer, core),
            )
        )
    for k in range(1, far):
        peer = bits_differ(top, k, far)
        cfar.append(
            remote(
                cnear_sum.at[peer],
                cfar_in.at[k - 1],
                cfar_s.at[k - 1],
                cfar_r.at[k - 1],
                index(peer, mid, core),
            )
        )
    x_copy.wait()

    def finish(i, carry):
        r = rows(i * lb, lb)
        gn = dot_nn(dqb[r, :], wq[...]) + dot_tn(dkt[:, r], wk[...]) + dot_tn(dvt[:, r], wv[...])
        xhat, inv = normal_stats(x[r, :].astype(F32))
        scaled = gn * gain
        grad[r, :] = (
            gmid[r, :]
            + inv
            * (
                scaled
                - jnp.mean(scaled, axis=-1, keepdims=True)
                - xhat * jnp.mean(scaled * xhat, axis=-1, keepdims=True)
            )
        ).astype(BF)

        @pl.when(i == 0)
        def _():
            ccore.wait_recv()
            for m in range(near):
                ccore_sum[m] = (
                    cparts[:, m, core].astype(F32) + ccore_in[:, m].astype(F32)
                ).astype(BF)
            for copy in cnear:
                copy.start()

        @pl.when(i == 1)
        def _():
            for copy in cnear:
                copy.wait_recv()
            total = ccore_sum[mid].astype(F32)
            for k in range(near - 1):
                total = total + cnear_in[k].astype(F32)
            cnear_sum[...] = total.astype(BF)
            for copy in cfar:
                copy.start()

        return carry

    lax.fori_loop(0, frame_count // lb, finish, 0)
    grad_copy = pltpu.make_async_copy(grad, grad_h, end_sem.at[1])
    grad_copy.start()
    for k in range(1, near):
        near_copy(last, k).wait_recv()
    total = add_near(last)
    for j in range(last):
        far_copy(j).wait_recv()
        total = total + far_in[j].astype(F32)
    gq[...] = total[0]
    gk[...] = total[1]
    gv[...] = total[2]
    for a, out in enumerate((go, gu, gd)):
        for k in range(1, far):
            far2_copy(a, k).wait_recv()
        total = near_sum2[a][top].astype(F32)
        for k in range(far - 1):
            total = total + far_in2[a][k].astype(F32)
        out[...] = total
    for copy in cfar:
        copy.wait_recv()
    total = cnear_sum[top].astype(F32)
    for k in range(far - 1):
        total = total + cfar_in[k].astype(F32)
    gc[...] = total
    for a in range(3):
        core2_copy(a).wait_send()
        for k in range(1, near):
            near2_copy(a, k).wait_send()
        for k in range(1, far):
            far2_copy(a, k).wait_send()
    for j in range(pairs):
        core_copy(j).wait_send()
        for k in range(1, near):
            near_copy(j, k).wait_send()
        if j < last:
            far_copy(j).wait_send()
    ccore.wait_send()
    for copy in cnear + cfar:
        copy.wait_send()
    for i in range(frame_count // tb):
        layer_copy(i).wait()
    grad_copy.wait()


def both_back(n, lengths, middle, gout, mixed, big, x, nb, qkv, raised, part, weights, table, bup):
    far, near = levels_of(n)
    frame_count, width = x.shape
    share = width // n
    pairs = HEADS // 2
    blocks = [p.shape[3:] for p in big]
    row_block = jax.ShapeDtypeStruct((share, width), F32)
    low = jax.ShapeDtypeStruct((frame_count, width), BF)
    low_rows = pltpu.VMEM((frame_count, width), BF)
    pair_rows = pltpu.VMEM((2, frame_count, 128), BF)
    dma = pltpu.SemaphoreType.DMA
    tb, ub = 256, raised.shape[3]
    return pl.pallas_call(
        functools.partial(both_back_kernel, n, tb, ub, 512),
        out_shape=[low, low, row_block, row_block, row_block]
        + [jax.ShapeDtypeStruct(b, F32) for b in blocks]
        + [jax.ShapeDtypeStruct((share, 128), F32)],
        in_specs=[SMEM_SPEC] + [HBM_SPEC] * 12 + [VMEM_SPEC] * 6,
        out_specs=[HBM_SPEC] * 2 + [VMEM_SPEC] * 7,
        scratch_shapes=[
            pltpu.VMEM((8, frame_count, 512), BF),
            low_rows,
            low_rows,
            low_rows,
            pltpu.VMEM((frame_count, width), F32),
            low_rows,
            low_rows,
            low_rows,
            low_rows,
        ]
        + [pltpu.VMEM(p.shape, BF) for p in big]
        + [
            pair_rows,
            pair_rows,
            pair_rows,
            pltpu.VMEM((frame_count, 128), F32),
            pltpu.VMEM((width, frame_count), BF),
            pltpu.VMEM((width, frame_count), BF),
            pltpu.VMEM((8, width), F32),
            pltpu.VMEM((8, 4 * width), F32),
            pltpu.VMEM((width, 128), F32),
            pltpu.VMEM((pairs, 3, near, 2, share, width), BF),
            pltpu.VMEM((pairs, 3, near, share, width), BF),
            pltpu.VMEM((pairs, near, 3, share, width), BF),
            pltpu.VMEM((pairs, near - 1, 3, share, width), BF),
            pltpu.VMEM((pairs, 3, share, width), BF),
            pltpu.VMEM((pairs - 1, 3, share, width), BF),
        ]
        + [pltpu.VMEM((far, near) + b, BF) for b in blocks]
        + [pltpu.VMEM((near - 1, far) + b, BF) for b in blocks]
        + [pltpu.VMEM((far,) + b, BF) for b in blocks]
        + [pltpu.VMEM((far - 1,) + b, BF) for b in blocks]
        + [
            pltpu.VMEM((far, near, 2, share, 128), BF),
            pltpu.VMEM((far, near, share, 128), BF),
            pltpu.VMEM((near, far, share, 128), BF),
            pltpu.VMEM((near - 1, far, share, 128), BF),
            pltpu.VMEM((far, share, 128), BF),
            pltpu.VMEM((far - 1, share, 128), BF),
            dma((frame_count // tb, 3)),
            dma((5,)),
            dma((2, 3)),
            dma((2,)),
            dma((2, frame_count // ub)),
            dma((pairs,)),
            dma((pairs,)),
            dma((pairs, near - 1)),
            dma((pairs, near - 1)),
            dma((pairs,)),
            dma((pairs,)),
            dma((3,)),
            dma((3,)),
            dma((3, near - 1)),
            dma((3, near - 1)),
            dma((3, far - 1)),
            dma((3, far - 1)),
            dma,
            dma,
            dma((near - 1,)),
            dma((near - 1,)),
            dma((far - 1,)),
            dma((far - 1,)),
        ],
        compiler_params=pltpu.CompilerParams(
            collective_id=3, has_side_effects=True, vmem_limit_bytes=67043328
        ),
        name="both_back",
    )(lengths, middle, gout, mixed, *big, x, nb, *qkv, raised, part, *weights, table, bup)


def hand_out_kernel(pieces, *refs):
    rows_in, ins, rows_out, outs = refs[:2], refs[2:9], refs[9:11], refs[11:26]
    rows_held, held, lanes = refs[26:28], refs[28:34], refs[34]
    read_sem, write_sem, in_sem, out_sem = refs[35:]
    size = rows_held[0].shape[0] // pieces
    reads, writes = [], []
    for j in range(pieces):
        for b in range(2):
            r = pl.ds(j * size, size)
            reads.append(
                pltpu.make_async_copy(rows_in[b].at[r], rows_held[b].at[r], read_sem.at[b, j])
            )
            writes.append(
                pltpu.make_async_copy(rows_held[b].at[r], rows_out[b].at[r], write_sem.at[b, j])
            )
    small_in = [pltpu.make_async_copy(ins[a], held[a], in_sem.at[a]) for a in range(6)]
    small_in.append(pltpu.make_async_copy(ins[6], lanes, in_sem.at[6]))
    small_out = [pltpu.make_async_copy(held[a], outs[a], out_sem.at[a]) for a in range(6)]
    for copy in small_in + reads:
        copy.start()
    for read, write in zip(reads, writes):
        read.wait()
        write.start()
    for a in range(6):
        small_in[a].wait()
        small_out[a].start()
    small_in[6].wait()
    turned = lanes[...].T
    for v in range(8):
        outs[6 + v][...] = turned[v : v + 1, :]
    outs[14][...] = turned[8:12, :]
    for copy in writes + small_out:
        copy.wait()


def hand_out(large, totals):
    share = totals[0].shape[0]
    line = jax.ShapeDtypeStruct((1, share), F32)
    dma = pltpu.SemaphoreType.DMA
    pieces = 4
    return pl.pallas_call(
        functools.partial(hand_out_kernel, pieces),
        out_shape=[jax.ShapeDtypeStruct(a.shape, a.dtype) for a in large]
        + [jax.ShapeDtypeStruct(t.shape, F32) for t in totals[:6]]
        + [line] * 8
        + [jax.ShapeDtypeStruct((4, share), F32)],
        in_specs=[HBM_SPEC] * 9,
        out_specs=[HBM_SPEC] * 8 + [VMEM_SPEC] * 9,
        scratch_shapes=[pltpu.VMEM(a.shape, a.dtype) for a in large]
        + [pltpu.VMEM(t.shape, F32) for t in totals]
        + [dma((2, pieces)), dma((2, pieces)), dma((7,)), dma((6,))],
        compiler_params=pltpu.CompilerParams(vmem_limit_bytes=60 << 20),
        name="hand_out",
    )(*large, *totals)


def per_device_fused(n, frames, lengths, vectors, up_bias, weights, grad_out):
    width = frames.shape[2]
    x = frames[0]
    got = gather_attend(n, lengths, x, tuple(w.T for w in weights), vectors + (up_bias,))
    wq, wk, wv = (w.reshape(n * w.shape[3], w.shape[4]) for w in got[:3])
    table, bup, qq, kk, vv, raised, part, nb, mixed, middle = got[6:]
    sums = both_back(
        n,
        lengths,
        middle,
        grad_out[0],
        mixed,
        got[3:6],
        x,
        nb,
        (qq, kk, vv),
        raised,
        part,
        (wq, wk, wv),
        table,
        bup,
    )
    layer_out, grad_x, *outs = hand_out(sums[:2], sums[2:])
    gq, gk, gv, go, gu, gd = (g.T for g in outs[:6])
    line = [v.reshape(-1) for v in outs[6:14]]
    return (
        layer_out[None],
        grad_x[None],
        line[0],
        line[1],
        gq,
        line[2],
        gk,
        gv,
        line[3],
        go,
        line[4],
        line[5],
        line[6],
        gu,
        outs[14].reshape(-1),
        gd,
        line[7],
    )


def per_device(
    n,
    frames,
    lengths,
    attn_gain,
    attn_shift,
    query_weight,
    query_bias,
    key_weight,
    value_weight,
    value_bias,
    out_weight,
    out_bias,
    mlp_gain,
    mlp_shift,
    up_weight,
    up_bias,
    down_weight,
    down_bias,
    grad_out,
):
    slots, frame_count, width = frames.shape
    assert slots == 1
    share = width // n
    vectors = (
        attn_gain,
        attn_shift,
        query_bias,
        value_bias,
        out_bias,
        mlp_gain,
        mlp_shift,
        down_bias,
    )
    far, near = levels_of(n)
    if share % 16 == 0 and far == HEADS // 2:
        return per_device_fused(
            n,
            frames,
            lengths,
            vectors,
            up_bias,
            (query_weight, key_weight, value_weight, out_weight, up_weight, down_weight),
            grad_out,
        )
    packed = jnp.concatenate(
        [jnp.stack(vectors, axis=1), up_bias.reshape(share, 4), jnp.zeros((share, 116), BF)], axis=1
    )
    shards = (
        query_weight.T,
        key_weight.T,
        value_weight.T,
        out_weight.T,
        up_weight.T,
        down_weight.T,
        packed,
    )
    full = gather_all(n, shards)
    wq, wk, wv, wo, wup, wdn, vec = (
        f.reshape(n * f.shape[3], f.shape[4]) for f in full
    )
    bup = vec[:, 8:12].reshape(1, 4 * width)
    x = frames[0]
    nb, qaug, kk, vv, mixed, middle, kaug = attend(lengths, x, wq, wk, wv, wo, vec)
    layer_out, gmid, dmixed, dwo, dwup, dwdn, sums_two, sum_up = feed(
        lengths, middle, grad_out[0], mixed, wup, wdn, wo, vec, bup
    )
    grad_x, dwq, dwk, dwv, sums_one = attend_back(
        x, gmid, nb, qaug, kk, vv, mixed, dmixed, kaug, wq, wk, wv, vec
    )
    columns = jnp.concatenate(
        [
            sums_one[:4].T,
            sums_two[:4].T,
            sum_up[0].reshape(width, 4),
            jnp.zeros((width, 116), F32),
        ],
        axis=1,
    ).astype(BF)

    def split(g):
        return g.reshape(far, near, 2, g.shape[0] // n, g.shape[1])

    gq, gk, gv, go, gu, gd, gc = scatter_all(
        n, tuple(split(g) for g in (dwq, dwk, dwv, dwo, dwup, dwdn, columns))
    )
    return (
        layer_out[None],
        grad_x[None],
        gc[:, 0],
        gc[:, 1],
        gq.T,
        gc[:, 2],
        gk.T,
        gv.T,
        gc[:, 3],
        go.T,
        gc[:, 4],
        gc[:, 5],
        gc[:, 6],
        gu.T,
        gc[:, 8:12].reshape(4 * share),
        gd.T,
        gc[:, 7],
    )


def solution(mesh):
    row, col, vector = P("dp", None, None), P(None, "dp"), P("dp")
    return jax.shard_map(
        functools.partial(per_device, mesh.shape["dp"]),
        mesh=mesh,
        in_specs=(
            row,
            P("dp", None),
            vector,
            vector,
            col,
            vector,
            col,
            col,
            vector,
            col,
            vector,
            vector,
            vector,
            col,
            vector,
            col,
            vector,
            row,
        ),
        out_specs=(
            row,
            row,
            vector,
            vector,
            col,
            vector,
            col,
            col,
            vector,
            col,
            vector,
            vector,
            vector,
            col,
            vector,
            col,
            vector,
        ),
        check_vma=False,
    )
```

```python
import functools
import math

import jax
import jax.numpy as jnp
from jax import lax
from jax.experimental import pallas as pl
from jax.experimental.pallas import tpu as pltpu
from jax.sharding import PartitionSpec as P

HEADS = 8
EPS = 1e-05
MESH = pl.DeviceIdType.MESH
F32 = jnp.float32
BF = jnp.bfloat16
VMEM_SPEC = pl.BlockSpec(memory_space=pltpu.VMEM)
SMEM_SPEC = pl.BlockSpec(memory_space=pltpu.SMEM)
HBM_SPEC = pl.BlockSpec(memory_space=pl.ANY)
EXCLUDED = -1e30
VMEM_LIMIT = 62 << 20


def dot_nn(a, b):
    return lax.dot_general(a, b, (((1,), (0,)), ((), ())), preferred_element_type=F32)


def dot_nt(a, b):
    return lax.dot_general(a, b, (((1,), (1,)), ((), ())), preferred_element_type=F32)


def dot_tn(a, b):
    return lax.dot_general(a, b, (((0,), (0,)), ((), ())), preferred_element_type=F32)


def levels_of(n):
    rest = n // 2
    bits = rest.bit_length() - 1
    near = 2 ** ((bits + 1) // 2)
    return rest // near, near


def rows(start, size):
    return pl.ds(pl.multiple_of(start, size), size)


def normal_stats(block):
    mean = jnp.mean(block, axis=-1, keepdims=True)
    centered = block - mean
    inv = lax.rsqrt(jnp.mean(centered * centered, axis=-1, keepdims=True) + EPS)
    return centered * inv, inv


def announce(n, me, far, near):
    barrier = pltpu.get_barrier_semaphore()
    core = lax.rem(me, 2)
    mid = lax.rem(me // 2, near)
    top = me // (2 * near)
    peers = [(lax.rem(top + k, far) * near + mid) * 2 + core for k in range(1, far)]
    peers += [(top * near + lax.rem(mid + k, near)) * 2 + core for k in range(1, near)]
    peers += [(top * near + mid) * 2 + 1 - core]
    for peer in peers:
        pl.semaphore_signal(barrier, inc=1, device_id=(peer,), device_id_type=MESH)
    return top, mid, core


def await_peers(far, near):
    pl.semaphore_wait(pltpu.get_barrier_semaphore(), far + near - 1)


def everyone_barrier(n, me, far, near):
    place = announce(n, me, far, near)
    await_peers(far, near)
    return place


def gather_kernel(n, count, *refs):
    shards, outs = refs[:count], refs[count : 2 * count]
    own_sem, far_s, far_r, near_s, near_r, core_s, core_r = refs[2 * count :]
    far, near = levels_of(n)
    me = lax.axis_index("dp")
    top, mid, core = everyone_barrier(n, me, far, near)

    def index(t, m, c):
        return (t * near + m) * 2 + c

    far_copies, near_copies = {}, {}
    for a in range(count):
        for k in range(1, far):
            copy = pltpu.make_async_remote_copy(
                src_ref=shards[a],
                dst_ref=outs[a].at[top, mid, core],
                send_sem=far_s.at[a, k - 1],
                recv_sem=far_r.at[a, k - 1],
                device_id=(index(lax.rem(top + k, far), mid, core),),
                device_id_type=MESH,
            )
            copy.start()
            far_copies[a, k] = copy
        pltpu.make_async_copy(shards[a], outs[a].at[top, mid, core], own_sem.at[a]).start()
    for a in range(count):
        pltpu.make_async_copy(shards[a], outs[a].at[top, mid, core], own_sem.at[a]).wait()
        for k in range(1, far):
            far_copies[a, k].wait_recv()
        for k in range(1, near):
            copy = pltpu.make_async_remote_copy(
                src_ref=outs[a].at[:, mid, core],
                dst_ref=outs[a].at[:, mid, core],
                send_sem=near_s.at[a, k - 1],
                recv_sem=near_r.at[a, k - 1],
                device_id=(index(top, lax.rem(mid + k, near), core),),
                device_id_type=MESH,
            )
            copy.start()
            near_copies[a, k] = copy
    core_copies = []
    for a in range(count):
        for k in range(1, near):
            near_copies[a, k].wait_recv()
        copy = pltpu.make_async_remote_copy(
            src_ref=outs[a].at[:, :, core],
            dst_ref=outs[a].at[:, :, core],
            send_sem=core_s.at[a],
            recv_sem=core_r.at[a],
            device_id=(index(top, mid, 1 - core),),
            device_id_type=MESH,
        )
        copy.start()
        core_copies.append(copy)
    for a in range(count):
        core_copies[a].wait_recv()
    for a in range(count):
        for k in range(1, far):
            far_copies[a, k].wait_send()
        for k in range(1, near):
            near_copies[a, k].wait_send()
        core_copies[a].wait_send()


def gather_all(n, shards):
    far, near = levels_of(n)
    count = len(shards)
    return pl.pallas_call(
        functools.partial(gather_kernel, n, count),
        out_shape=[jax.ShapeDtypeStruct((far, near, 2) + s.shape, s.dtype) for s in shards],
        in_specs=[VMEM_SPEC] * count,
        out_specs=[HBM_SPEC] * count,
        scratch_shapes=[
            pltpu.SemaphoreType.DMA((count,)),
            pltpu.SemaphoreType.DMA((count, far - 1)),
            pltpu.SemaphoreType.DMA((count, far - 1)),
            pltpu.SemaphoreType.DMA((count, near - 1)),
            pltpu.SemaphoreType.DMA((count, near - 1)),
            pltpu.SemaphoreType.DMA((count,)),
            pltpu.SemaphoreType.DMA((count,)),
        ],
        compiler_params=pltpu.CompilerParams(
            collective_id=0, has_side_effects=True, vmem_limit_bytes=32 << 20
        ),
        name="gather_params",
    )(*shards)


def scatter_kernel(n, count, *refs):
    parts, outs = refs[:count], refs[count : 2 * count]
    pos = 2 * count
    core_in, core_sum = refs[pos : pos + count], refs[pos + count : pos + 2 * count]
    pos += 2 * count
    near_in, near_sum = refs[pos : pos + count], refs[pos + count : pos + 2 * count]
    pos += 2 * count
    far_in = refs[pos : pos + count]
    core_s, core_r, near_s, near_r, far_s, far_r = refs[pos + count :]
    far, near = levels_of(n)
    me = lax.axis_index("dp")
    top, mid, core = everyone_barrier(n, me, far, near)

    def index(t, m, c):
        return (t * near + m) * 2 + c

    core_copies, near_copies, far_copies = [], {}, {}
    for a in range(count):
        copy = pltpu.make_async_remote_copy(
            src_ref=parts[a].at[:, :, 1 - core],
            dst_ref=core_in[a],
            send_sem=core_s.at[a],
            recv_sem=core_r.at[a],
            device_id=(index(top, mid, 1 - core),),
            device_id_type=MESH,
        )
        copy.start()
        core_copies.append(copy)
    for a in range(count):
        core_copies[a].wait_recv()

        def add_core(i, carry, a=a):
            f, m = i // near, lax.rem(i, near)
            core_sum[a][m, f] = (
                parts[a][f, m, core].astype(F32) + core_in[a][f, m].astype(F32)
            ).astype(BF)
            return carry

        lax.fori_loop(0, far * near, add_core, 0)
        for k in range(1, near):
            peer = lax.rem(mid + k, near)
            copy = pltpu.make_async_remote_copy(
                src_ref=core_sum[a].at[peer],
                dst_ref=near_in[a].at[k - 1],
                send_sem=near_s.at[a, k - 1],
                recv_sem=near_r.at[a, k - 1],
                device_id=(index(top, peer, core),),
                device_id_type=MESH,
            )
            copy.start()
            near_copies[a, k] = copy
    for a in range(count):
        for k in range(1, near):
            near_copies[a, k].wait_recv()

        def add_near(f, carry, a=a):
            total = core_sum[a][mid, f].astype(F32)
            for k in range(near - 1):
                total = total + near_in[a][k, f].astype(F32)
            near_sum[a][f] = total.astype(BF)
            return carry

        lax.fori_loop(0, far, add_near, 0)
        for k in range(1, far):
            peer = lax.rem(top + k, far)
            copy = pltpu.make_async_remote_copy(
                src_ref=near_sum[a].at[peer],
                dst_ref=far_in[a].at[k - 1],
                send_sem=far_s.at[a, k - 1],
                recv_sem=far_r.at[a, k - 1],
                device_id=(index(peer, mid, core),),
                device_id_type=MESH,
            )
            copy.start()
            far_copies[a, k] = copy
    for a in range(count):
        for k in range(1, far):
            far_copies[a, k].wait_recv()
        total = near_sum[a][top].astype(F32)
        for k in range(far - 1):
            total = total + far_in[a][k].astype(F32)
        outs[a][...] = total
    for a in range(count):
        core_copies[a].wait_send()
        for k in range(1, near):
            near_copies[a, k].wait_send()
        for k in range(1, far):
            far_copies[a, k].wait_send()


def scatter_all(n, parts):
    far, near = levels_of(n)
    count = len(parts)
    blocks = [p.shape[3:] for p in parts]
    return pl.pallas_call(
        functools.partial(scatter_kernel, n, count),
        out_shape=[jax.ShapeDtypeStruct(b, F32) for b in blocks],
        in_specs=[VMEM_SPEC] * count,
        out_specs=[VMEM_SPEC] * count,
        scratch_shapes=[pltpu.VMEM((far, near) + b, BF) for b in blocks]
        + [pltpu.VMEM((near, far) + b, BF) for b in blocks]
        + [pltpu.VMEM((near - 1, far) + b, BF) for b in blocks]
        + [pltpu.VMEM((far,) + b, BF) for b in blocks]
        + [pltpu.VMEM((far - 1,) + b, BF) for b in blocks]
        + [
            pltpu.SemaphoreType.DMA((count,)),
            pltpu.SemaphoreType.DMA((count,)),
            pltpu.SemaphoreType.DMA((count, near - 1)),
            pltpu.SemaphoreType.DMA((count, near - 1)),
            pltpu.SemaphoreType.DMA((count, far - 1)),
            pltpu.SemaphoreType.DMA((count, far - 1)),
        ],
        compiler_params=pltpu.CompilerParams(
            collective_id=1, has_side_effects=True, vmem_limit_bytes=VMEM_LIMIT
        ),
        name="scatter_grads",
    )(*parts)


def segment_lanes(lengths, position, lane):
    leading = lengths[0, 0]
    finish = leading + lengths[0, 1]
    segment = jnp.where(position < leading, 0, jnp.where(position < finish, 1, 2))
    return lax.rem(lane, 64) == segment


def three_pieces(column):
    high = column.astype(BF)
    rest = column - high.astype(F32)
    middle = rest.astype(BF)
    return high, middle, (rest - middle.astype(F32)).astype(BF)


def own_lanes(lane, half):
    return (lane < 64) if half == 0 else (lane >= 64)


def attend_kernel(
    lengths, x, wq, wk, wv, wo, vec, nb, qaug, kk, vv, mixed, middle, kaug, qbuf, *, tb, lb
):
    frame_count = x.shape[0]
    lane = lax.broadcasted_iota(jnp.int32, (1, 128), 1)
    table = vec[...].astype(F32).T
    gain, shift, bq, bv, bo = (table[i : i + 1] for i in range(5))

    def project(i, carry):
        r = rows(i * lb, lb)
        xhat, _ = normal_stats(x[r, :].astype(F32))
        normed = (xhat * gain + shift).astype(BF)
        nb[r, :] = normed
        qbuf[r, :] = ((dot_nt(normed, wq[...]) + bq).astype(BF).astype(F32) * 0.125).astype(BF)
        kk[r, :] = dot_nt(normed, wk[...]).astype(BF)
        vv[r, :] = (dot_nt(normed, wv[...]) + bv).astype(BF)
        position = lax.broadcasted_iota(jnp.int32, (lb, 128), 0) + i * lb
        lanes = lax.broadcasted_iota(jnp.int32, (lb, 128), 1)
        same = segment_lanes(lengths, position, lanes)
        slot = lax.rem(lanes, 64)
        kaug[r, :] = jnp.where(
            slot < 3, jnp.where(same, 0.0, EXCLUDED), jnp.where(slot < 6, 1.0, 0.0)
        ).astype(BF)
        return carry

    lax.fori_loop(0, frame_count // lb, project, 0)

    def pair_step(p, carry):
        cols = rows(p * 128, 128)
        for half in range(2):
            own = own_lanes(lane, half)
            base = 64 - 64 * half
            key = jnp.where(own, kk[:, cols], kaug[...])
            value = jnp.where(own, vv[:, cols], jnp.ones((1, 128), BF))
            head = pl.multiple_of((2 * p + half) * 128, 128)

            def block(i, inner, half=half, own=own, base=base, key=key, value=value, head=head):
                r = rows(i * tb, tb)
                position = lax.broadcasted_iota(jnp.int32, (tb, 128), 0) + i * tb
                lanes = lax.broadcasted_iota(jnp.int32, (tb, 128), 1)
                mark = jnp.where(segment_lanes(lengths, position, lanes), 1.0, 0.0).astype(BF)
                query = jnp.where(own, qbuf[r, cols], mark)
                scores = dot_nt(query, key)
                top = jnp.max(scores, axis=1, keepdims=True)
                raised = jnp.exp(scores - top).astype(BF)
                got = dot_nn(raised, value)
                total = got[:, base : base + 1]
                got = (got * (1.0 / total)).astype(BF)
                if half == 0:
                    mixed[r, cols] = got
                else:
                    mixed[r, cols] = jnp.where(own, got, mixed[r, cols])
                high, mid, low = three_pieces(-(top + jnp.log(total)))
                query = jnp.where(lane == base + 3, high, query)
                query = jnp.where(lane == base + 4, mid, query)
                qaug[r, pl.ds(head, 128)] = jnp.where(lane == base + 5, low, query)
                return inner

            lax.fori_loop(0, frame_count // tb, block, 0, unroll=True)
        return carry

    lax.fori_loop(0, HEADS // 2, pair_step, 0)

    def finish(i, carry):
        r = rows(i * lb, lb)
        middle[r, :] = x[r, :].astype(F32) + (dot_nt(mixed[r, :], wo[...]) + bo)
        return carry

    lax.fori_loop(0, frame_count // lb, finish, 0)


def attend(lengths, x, wq, wk, wv, wo, vec):
    frame_count, width = x.shape
    low = jax.ShapeDtypeStruct((frame_count, width), BF)
    return pl.pallas_call(
        functools.partial(attend_kernel, tb=512, lb=512),
        out_shape=[
            low,
            jax.ShapeDtypeStruct((frame_count, HEADS * 128), BF),
            low,
            low,
            low,
            jax.ShapeDtypeStruct((frame_count, width), F32),
            jax.ShapeDtypeStruct((frame_count, 128), BF),
        ],
        in_specs=[SMEM_SPEC] + [VMEM_SPEC] * 6,
        out_specs=[VMEM_SPEC] * 7,
        scratch_shapes=[pltpu.VMEM((frame_count, width), BF)],
        compiler_params=pltpu.CompilerParams(vmem_limit_bytes=VMEM_LIMIT),
        name="attend_forward",
    )(lengths, x, wq, wk, wv, wo, vec)


def feed_kernel(
    lengths,
    middle,
    gout,
    mixed,
    wup,
    wdn,
    wo,
    vec,
    bup,
    layer_out,
    gmid,
    dmixed,
    dwo,
    dwup,
    dwdn,
    sums,
    sum_up,
    nb,
    act,
    gup,
    glow,
    gbl,
    *,
    tb,
):
    frame_count = middle.shape[0]
    finish = lengths[0, 0] + lengths[0, 1]
    table = vec[...].astype(F32).T
    gain, shift, bdn = (table[i : i + 1] for i in range(5, 8))
    sums[...] = jnp.zeros_like(sums)
    sum_up[...] = jnp.zeros_like(sum_up)

    def block(i, carry):
        r = rows(i * tb, tb)
        valid = lax.broadcasted_iota(jnp.int32, (tb, 1), 0) + i * tb < finish
        mid = middle[r, :]
        xhat, inv = normal_stats(mid)
        normed = (xhat * gain + shift).astype(BF)
        nb[r, :] = normed
        up = dot_nt(normed, wup[...]) + bup[...].astype(F32)
        cdf = 0.5 * (1.0 + lax.erf(up * (1.0 / math.sqrt(2.0))))
        low = (up * cdf).astype(BF)
        act[r, :] = low
        down = dot_nt(low, wdn[...]) + bdn
        layer_out[r, :] = jnp.where(valid, mid + down, 0.0).astype(BF)
        grow = jnp.where(valid, gout[r, :].astype(F32), 0.0)
        gl = grow.astype(BF)
        glow[r, :] = gl
        slope = cdf + up * jnp.exp(-0.5 * up * up) * (1.0 / math.sqrt(2.0 * math.pi))
        gu = (dot_nn(gl, wdn[...]) * slope).astype(BF)
        gup[r, :] = gu
        gn = dot_nn(gu, wup[...])
        scaled = gn * gain
        gm = grow + inv * (
            scaled
            - jnp.mean(scaled, axis=-1, keepdims=True)
            - xhat * jnp.mean(scaled * xhat, axis=-1, keepdims=True)
        )
        gmid[r, :] = gm
        gb = gm.astype(BF)
        gbl[r, :] = gb
        dmixed[r, :] = dot_nn(gb, wo[...]).astype(BF)
        sums[0:1, :] += jnp.sum(gb.astype(F32), axis=0, keepdims=True)
        sums[1:2, :] += jnp.sum(gn * xhat, axis=0, keepdims=True)
        sums[2:3, :] += jnp.sum(gn, axis=0, keepdims=True)
        sums[3:4, :] += jnp.sum(grow, axis=0, keepdims=True)
        sum_up[0:1, :] += jnp.sum(gu.astype(F32), axis=0, keepdims=True)
        return carry

    lax.fori_loop(0, frame_count // tb, block, 0)
    dwo[...] = dot_tn(gbl[...], mixed[...]).astype(BF)

    def weights(i, carry):
        c = rows(i * 512, 512)
        dwup[c, :] = dot_tn(gup[:, c], nb[...]).astype(BF)
        dwdn[:, c] = dot_tn(glow[...], act[:, c]).astype(BF)
        return carry

    lax.fori_loop(0, wup.shape[0] // 512, weights, 0)


def feed(lengths, middle, gout, mixed, wup, wdn, wo, vec, bup):
    frame_count, width = middle.shape
    hidden = wup.shape[0]
    low = jax.ShapeDtypeStruct((frame_count, width), BF)
    return pl.pallas_call(
        functools.partial(feed_kernel, tb=256),
        out_shape=[
            low,
            jax.ShapeDtypeStruct((frame_count, width), F32),
            low,
            jax.ShapeDtypeStruct((width, width), BF),
            jax.ShapeDtypeStruct((hidden, width), BF),
            jax.ShapeDtypeStruct((width, hidden), BF),
            jax.ShapeDtypeStruct((8, width), F32),
            jax.ShapeDtypeStruct((8, hidden), F32),
        ],
        in_specs=[SMEM_SPEC] + [VMEM_SPEC] * 8,
        out_specs=[VMEM_SPEC] * 8,
        scratch_shapes=[
            pltpu.VMEM((frame_count, width), BF),
            pltpu.VMEM((frame_count, hidden), BF),
            pltpu.VMEM((frame_count, hidden), BF),
            pltpu.VMEM((frame_count, width), BF),
            pltpu.VMEM((frame_count, width), BF),
        ],
        compiler_params=pltpu.CompilerParams(vmem_limit_bytes=VMEM_LIMIT),
        name="feed_forward_both",
    )(lengths, middle, gout, mixed, wup, wdn, wo, vec, bup)


def attend_back_kernel(
    x,
    gmid,
    nb,
    qaug,
    kk,
    vv,
    mixed,
    dmixed,
    kaug,
    wq,
    wk,
    wv,
    vec,
    grad_x,
    dwq,
    dwk,
    dwv,
    sums,
    dq,
    dqb,
    dkt,
    dvt,
    *,
    ub,
    lb,
):
    frame_count = x.shape[0]
    lane = lax.broadcasted_iota(jnp.int32, (1, 128), 1)
    gain = vec[...].astype(F32).T[0:1]

    def pair_step(p, carry):
        cols = rows(p * 128, 128)
        grad_pair = dmixed[:, cols]
        product = grad_pair.astype(F32) * mixed[:, cols].astype(F32)
        for half in range(2):
            own = own_lanes(lane, half)
            base = 64 - 64 * half
            delta = jnp.sum(jnp.where(own, product, 0.0), axis=1, keepdims=True)
            high, mid, low = three_pieces(-delta)
            grad = jnp.where(own, grad_pair, jnp.zeros((1, 128), BF))
            grad = jnp.where(lane == base + 3, high, grad)
            grad = jnp.where(lane == base + 4, mid, grad)
            grad = jnp.where(lane == base + 5, low, grad)
            query = qaug[:, pl.ds(pl.multiple_of((2 * p + half) * 128, 128), 128)]
            here = pl.ds(pl.multiple_of(p * 128 + 64 * half, 64), 64)
            part = slice(64 * half, 64 * half + 64)
            ones = jnp.where(
                (lane >= base + 3) & (lane < base + 6), jnp.ones((1, 128), F32), 0.0
            ).astype(BF)

            def block(i, inner):
                r = rows(i * ub, ub)
                key = jnp.where(own, kk[r, cols], kaug[r, :])
                value = jnp.where(own, vv[r, cols], ones)
                probs = jnp.exp(dot_nt(query, key))
                low_probs = probs.astype(BF)
                gs = (probs * dot_nt(grad, value)).astype(BF)
                dvt[here, r] = dot_tn(grad, low_probs)[part].astype(BF)
                dkt[here, r] = dot_tn(query, gs)[part].astype(BF)
                step = dot_nn(gs, kk[r, cols])
                if i == 0:
                    dq[...] = step
                else:
                    dq[...] += step
                return inner

            for i in range(frame_count // ub):
                block(i, 0)
            done = (dq[...] * 0.125).astype(BF)
            if half == 0:
                dqb[:, cols] = done
            else:
                dqb[:, cols] = jnp.where(own, done, dqb[:, cols])
        return carry

    lax.fori_loop(0, HEADS // 2, pair_step, 0)
    sums[...] = jnp.zeros_like(sums)

    def finish(i, carry):
        r = rows(i * lb, lb)
        gn = dot_nn(dqb[r, :], wq[...]) + dot_tn(dkt[:, r], wk[...]) + dot_tn(dvt[:, r], wv[...])
        xhat, inv = normal_stats(x[r, :].astype(F32))
        scaled = gn * gain
        grad_x[r, :] = (
            gmid[r, :]
            + inv
            * (
                scaled
                - jnp.mean(scaled, axis=-1, keepdims=True)
                - xhat * jnp.mean(scaled * xhat, axis=-1, keepdims=True)
            )
        ).astype(BF)
        sums[0:1, :] += jnp.sum(gn * xhat, axis=0, keepdims=True)
        sums[1:2, :] += jnp.sum(gn, axis=0, keepdims=True)
        sums[2:3, :] += jnp.sum(dqb[r, :].astype(F32), axis=0, keepdims=True)
        return carry

    lax.fori_loop(0, frame_count // lb, finish, 0)
    sums[3:4, :] = dot_nt(jnp.ones((8, frame_count), BF), dvt[...])[0:1]
    dwq[...] = dot_tn(dqb[...], nb[...]).astype(BF)
    dwk[...] = dot_nn(dkt[...], nb[...]).astype(BF)
    dwv[...] = dot_nn(dvt[...], nb[...]).astype(BF)


def attend_back(x, gmid, nb, qaug, kk, vv, mixed, dmixed, kaug, wq, wk, wv, vec):
    frame_count, width = x.shape
    square = jax.ShapeDtypeStruct((width, width), BF)
    return pl.pallas_call(
        functools.partial(attend_back_kernel, ub=512, lb=512),
        out_shape=[
            jax.ShapeDtypeStruct((frame_count, width), BF),
            square,
            square,
            square,
            jax.ShapeDtypeStruct((8, width), F32),
        ],
        in_specs=[VMEM_SPEC] * 13,
        out_specs=[VMEM_SPEC] * 5,
        scratch_shapes=[
            pltpu.VMEM((frame_count, 128), F32),
            pltpu.VMEM((frame_count, width), BF),
            pltpu.VMEM((width, frame_count), BF),
            pltpu.VMEM((width, frame_count), BF),
        ],
        compiler_params=pltpu.CompilerParams(vmem_limit_bytes=VMEM_LIMIT),
        name="attend_backward",
    )(x, gmid, nb, qaug, kk, vv, mixed, dmixed, kaug, wq, wk, wv, vec)


def bits_differ(a, b, size):
    total, bit = 0, 1
    while bit < size:
        total = total + bit * lax.rem(a // bit + b // bit, 2)
        bit *= 2
    return total


def remote(src, dst, send, recv, device):
    return pltpu.make_async_remote_copy(
        src_ref=src,
        dst_ref=dst,
        send_sem=send,
        recv_sem=recv,
        device_id=(device,),
        device_id_type=MESH,
    )


def spread_rows(blocks, share, width):
    count, height, lanes = blocks.shape
    source = lax.broadcasted_iota(jnp.int32, (lanes, width), 0)
    target = lax.broadcasted_iota(jnp.int32, (lanes, width), 1)
    pick = jnp.where(source == lax.rem(target, share), 1.0, 0.0).astype(BF)
    spread = dot_nn(blocks.reshape(count * height, lanes).astype(BF), pick)
    owner = lax.broadcasted_iota(jnp.int32, (count, height, width), 0)
    place = lax.broadcasted_iota(jnp.int32, (count, height, width), 2)
    spread = spread.reshape(count, height, width)
    return jnp.sum(jnp.where(owner == place // share, spread, 0.0), axis=0)


SECOND_DUTIES = ((0, 0, 3), (1, 0, 1), (3, 1, 2), (5, 1, 3), (6, 1, 1))


def gather_attend_kernel(n, tb, lb, *refs):
    (lengths, x, sq, sk, sv, so, su, sd) = refs[:8]
    vectors, refs = refs[8:17], refs[17:]
    (wq, wk, wv, wo, wup, wdn, table, bup, qq_h, kk_h, vv_h, raised_h, part_h) = refs[:13]
    (nb_h, mixed_h, middle_h) = refs[13:16]
    (xhat, nb, mixed, middle, kaug, qbuf, kbuf, vbuf, stage, part, svec, vec) = refs[16:28]
    (own_sem, near_s, near_r, core_s, core_r, far_s, far_r, fwd_s, fwd_r) = refs[28:37]
    (bown_sem, bfar_s, bfar_r, bnear_s, bnear_r, bcore_s, bcore_r, out_sem, end_sem) = refs[37:46]
    stage_sem = refs[46]
    far, near = levels_of(n)
    share = 512 // n
    frame_count, width = x.shape
    pairs = HEADS // 2
    me = lax.axis_index("dp")
    top, mid, core = announce(n, me, far, near)
    lane = lax.broadcasted_iota(jnp.int32, (1, 128), 1)
    svec[...] = jnp.zeros_like(svec)
    for v, vector in enumerate(vectors):
        length = vector.shape[0]
        svec[v : v + 1, :length] = vector[...].reshape(1, length)

    def index(t, m, c):
        return (t * near + m) * 2 + c

    sibling = index(top, mid, 1 - core)
    first = list(zip((sq, sk, sv), (wq, wk, wv)))
    second = list(zip((svec, so, su, sd), (vec, wo, wup, wdn)))

    def near_copy(a, k):
        peer = index(top, lax.rem(mid + k, near), core)
        src, dst = first[a]
        return remote(src, dst.at[top, mid, core], near_s.at[a, k - 1], near_r.at[a, k - 1], peer)

    def core_copy(a):
        ref = first[a][1].at[top, :, core]
        return remote(ref, ref, core_s.at[a], core_r.at[a], sibling)

    def far_copy(a, k):
        ref = first[a][1].at[top, :, core]
        peer = index(bits_differ(top, k, far), mid, core)
        return remote(ref, ref, far_s.at[a, k - 1], far_r.at[a, k - 1], peer)

    def fwd_copy(a, k):
        ref = first[a][1].at[bits_differ(top, k, far), :, core]
        return remote(ref, ref, fwd_s.at[a, k - 1], fwd_r.at[a, k - 1], sibling)

    def bfar_copy(a, k):
        src, dst = second[a]
        peer = index(bits_differ(top, k, far), mid, core)
        return remote(src, dst.at[top, mid, core], bfar_s.at[a, k - 1], bfar_r.at[a, k - 1], peer)

    def bnear_copy(a, k):
        ref = second[a][1].at[:, mid, core]
        peer = index(top, lax.rem(mid + k, near), core)
        return remote(ref, ref, bnear_s.at[a, k - 1], bnear_r.at[a, k - 1], peer)

    def bcore_copy(a):
        ref = second[a][1].at[:, :, core]
        return remote(ref, ref, bcore_s.at[a], bcore_r.at[a], sibling)

    def own_copy(a):
        src, dst = first[a]
        return pltpu.make_async_copy(src, dst.at[top, mid, core], own_sem.at[a])

    def bown_copy(a):
        src, dst = second[a]
        return pltpu.make_async_copy(src, dst.at[top, mid, core], bown_sem.at[a])

    def stats(i, carry):
        r = rows(i * lb, lb)
        xhat[r, :] = normal_stats(x[r, :].astype(F32))[0]
        part[r, :] = jnp.zeros((lb, 128), F32)
        position = lax.broadcasted_iota(jnp.int32, (lb, 128), 0) + i * lb
        lanes = lax.broadcasted_iota(jnp.int32, (lb, 128), 1)
        same = segment_lanes(lengths, position, lanes)
        slot = lax.rem(lanes, 64)
        kaug[r, :] = jnp.where(
            slot < 3, jnp.where(same, 0.0, EXCLUDED), jnp.where(slot < 6, 1.0, 0.0)
        ).astype(BF)
        return carry

    lax.fori_loop(0, frame_count // lb, stats, 0)
    await_peers(far, near)
    for k in range(1, far):
        bfar_copy(0, k).start()
    bown_copy(0).start()
    for a in range(3):
        for k in range(1, near):
            near_copy(a, k).start()
        own_copy(a).start()
    for a in (2, 3, 1):
        for k in range(1, far):
            bfar_copy(a, k).start()
        bown_copy(a).start()

    bown_copy(0).wait()
    for k in range(1, far):
        bfar_copy(0, k).wait_recv()
    for k in range(1, near):
        bnear_copy(0, k).start()
    for a in range(3):
        own_copy(a).wait()
        for k in range(1, near):
            near_copy(a, k).wait_recv()
        core_copy(a).start()
    for k in range(1, near):
        bnear_copy(0, k).wait_recv()
    bcore_copy(0).start()
    for k in range(1, far):
        for a in range(3):
            far_copy(a, k).start()
    bcore_copy(0).wait_recv()
    blocks = vec[...].reshape(n, 16, 128)
    table[...] = spread_rows(blocks, share, width)
    gain, shift = table[0:1, :], table[1:2, :]

    def norm(i, carry):
        r = rows(i * lb, lb)
        nb[r, :] = (xhat[r, :] * gain + shift).astype(BF)
        return carry

    lax.fori_loop(0, frame_count // lb, norm, 0)
    nb_copy = pltpu.make_async_copy(nb, nb_h, end_sem.at[0])
    nb_copy.start()
    for a in range(3):
        core_copy(a).wait_recv()

    def second_near(a):
        bown_copy(a).wait()
        for k in range(1, far):
            bfar_copy(a, k).wait_recv()
        for k in range(1, near):
            bnear_copy(a, k).start()

    def second_core(a):
        for k in range(1, near):
            bnear_copy(a, k).wait_recv()
        bcore_copy(a).start()

    second_near(2)

    def out_copies(p, slot):
        cols = rows(p * 128, 128)
        return [
            pltpu.make_async_copy(buf.at[slot], out.at[:, cols], out_sem.at[slot, a])
            for a, (buf, out) in enumerate(((qbuf, qq_h), (kbuf, kk_h), (vbuf, vv_h)))
        ]

    def stage_copies(p, half):
        return [
            pltpu.make_async_copy(
                stage.at[half, j, :, pl.ds(b * tb, tb)],
                raised_h.at[2 * p + half, b, pl.ds(j * tb, tb)],
                stage_sem.at[half, j, b],
            )
            for j in range(frame_count // tb)
            for b in range(frame_count // tb)
        ]

    def pair_step(i, carry):
        p = bits_differ(top, i, far)
        slot = lax.rem(i, 2)
        cols = rows(p * 128, 128)

        @pl.when(i > 0)
        def _():
            for a in range(3):
                fwd_copy(a, i).wait_recv()

        @pl.when(i > 1)
        def _():
            for copy in out_copies(bits_differ(top, i - 2, far), slot):
                copy.wait()

        weights = jnp.concatenate(
            [w[p].reshape(128, width) for w in (wq, wk, wv)], axis=0
        )
        bq, bv = table[2:3, cols], table[3:4, cols]

        def project(j, inner):
            r = rows(j * lb, lb)
            got = dot_nt(nb[r, :], weights)
            qbuf[slot, r, :] = ((got[:, :128] + bq).astype(BF).astype(F32) * 0.125).astype(BF)
            kbuf[slot, r, :] = got[:, 128:256].astype(BF)
            vbuf[slot, r, :] = (got[:, 256:] + bv).astype(BF)
            return inner

        lax.fori_loop(0, frame_count // lb, project, 0)
        for half in range(2):
            own = own_lanes(lane, half)
            base = 64 - 64 * half
            key = jnp.where(own, kbuf[slot], kaug[...])
            value = jnp.where(own, vbuf[slot], jnp.ones((1, 128), BF))

            @pl.when(i > 0)
            def _():
                for copy in stage_copies(bits_differ(top, i - 1, far), half):
                    copy.wait()

            def block(j):
                r = pl.ds(j * tb, tb)
                position = lax.broadcasted_iota(jnp.int32, (tb, 128), 0) + j * tb
                lanes = lax.broadcasted_iota(jnp.int32, (tb, 128), 1)
                mark = jnp.where(segment_lanes(lengths, position, lanes), 1.0, 0.0).astype(BF)
                query = jnp.where(own, qbuf[slot, r, :], mark)
                scores = dot_nt(query, key)
                peak = jnp.max(scores, axis=1, keepdims=True)
                raised = jnp.exp(scores - peak).astype(BF)
                stage[half, j] = raised
                got = dot_nn(raised, value)
                inverse = 1.0 / got[:, base : base + 1]
                part[r, :] = jnp.where(lane == 2 * p + half, inverse, part[r, :])
                got = (got * inverse).astype(BF)
                if half == 0:
                    mixed[r, cols] = got
                else:
                    mixed[r, cols] = jnp.where(own, got, mixed[r, cols])
            for j in range(frame_count // tb):
                block(j)
            for copy in stage_copies(p, half):
                copy.start()
            if half == 0:

                @pl.when(i < far - 1)
                def _():
                    for a in range(3):
                        far_copy(a, i + 1).wait_recv()
                        fwd_copy(a, i + 1).start()

            for step, duty, a in SECOND_DUTIES:
                if step % 2 == half:
                    act = second_near if duty == 0 else second_core
                    pl.when(i == step // 2)(functools.partial(act, a))

        for copy in out_copies(p, slot):
            copy.start()
        return carry

    lax.fori_loop(0, pairs, pair_step, 0)
    mixed_copy = pltpu.make_async_copy(mixed, mixed_h, end_sem.at[1])
    mixed_copy.start()
    part_copy = pltpu.make_async_copy(part, part_h, end_sem.at[3])
    part_copy.start()
    bcore_copy(1).wait_recv()
    out_weight = wo[...].reshape(width, width)
    bo = table[4:5, :]
    bup[...] = spread_rows(vec[...].reshape(n, 16, 128)[:, 8:16], 4 * share, 4 * width)

    def finish(i, carry):
        r = rows(i * lb, lb)
        middle[r, :] = x[r, :].astype(F32) + (dot_nt(mixed[r, :], out_weight) + bo)
        return carry

    lax.fori_loop(0, frame_count // lb, finish, 0)
    middle_copy = pltpu.make_async_copy(middle, middle_h, end_sem.at[2])
    middle_copy.start()
    for i in (pairs - 2, pairs - 1):
        for copy in out_copies(bits_differ(top, i, far), i % 2):
            copy.wait()
    for half in range(2):
        for copy in stage_copies(bits_differ(top, pairs - 1, far), half):
            copy.wait()
    part_copy.wait()
    nb_copy.wait()
    mixed_copy.wait()
    for a in range(3):
        for k in range(1, near):
            near_copy(a, k).wait_send()
        core_copy(a).wait_send()
        for k in range(1, far):
            far_copy(a, k).wait_send()
            fwd_copy(a, k).wait_send()
    bcore_copy(2).wait_recv()
    bcore_copy(3).wait_recv()
    for a in range(4):
        for k in range(1, far):
            bfar_copy(a, k).wait_send()
        for k in range(1, near):
            bnear_copy(a, k).wait_send()
        bcore_copy(a).wait_send()
    middle_copy.wait()


def gather_attend(n, lengths, x, shards, vectors):
    far, near = levels_of(n)
    frame_count, width = x.shape
    lead = (far, near, 2)
    share = width // n
    square = jax.ShapeDtypeStruct(lead + (share, width), BF)
    low = jax.ShapeDtypeStruct((frame_count, width), BF)
    dma = pltpu.SemaphoreType.DMA
    tb = 512
    return pl.pallas_call(
        functools.partial(gather_attend_kernel, n, tb, 512),
        out_shape=[
            square,
            square,
            square,
            square,
            jax.ShapeDtypeStruct(lead + (4 * share, width), BF),
            jax.ShapeDtypeStruct(lead + (share, 4 * width), BF),
            jax.ShapeDtypeStruct((16, width), F32),
            jax.ShapeDtypeStruct((8, 4 * width), F32),
            low,
            low,
            low,
            jax.ShapeDtypeStruct((HEADS, frame_count // tb, frame_count, tb), BF),
            jax.ShapeDtypeStruct((frame_count, 128), F32),
            low,
            low,
            jax.ShapeDtypeStruct((frame_count, width), F32),
        ],
        in_specs=[SMEM_SPEC, VMEM_SPEC] + [HBM_SPEC] * 6 + [VMEM_SPEC] * 9,
        out_specs=[VMEM_SPEC] * 4 + [HBM_SPEC] * 2 + [VMEM_SPEC] * 2 + [HBM_SPEC] * 8,
        scratch_shapes=[
            pltpu.VMEM((frame_count, width), F32),
            pltpu.VMEM((frame_count, width), BF),
            pltpu.VMEM((frame_count, width), BF),
            pltpu.VMEM((frame_count, width), F32),
            pltpu.VMEM((frame_count, 128), BF),
            pltpu.VMEM((2, frame_count, 128), BF),
            pltpu.VMEM((2, frame_count, 128), BF),
            pltpu.VMEM((2, frame_count, 128), BF),
            pltpu.VMEM((2, frame_count // tb, tb, frame_count), BF),
            pltpu.VMEM((frame_count, 128), F32),
            pltpu.VMEM((16, 128), BF),
            pltpu.VMEM(lead + (16, 128), BF),
            dma((3,)),
            dma((3, near - 1)),
            dma((3, near - 1)),
            dma((3,)),
            dma((3,)),
            dma((3, far - 1)),
            dma((3, far - 1)),
            dma((3, far - 1)),
            dma((3, far - 1)),
            dma((4,)),
            dma((4, far - 1)),
            dma((4, far - 1)),
            dma((4, near - 1)),
            dma((4, near - 1)),
            dma((4,)),
            dma((4,)),
            dma((2, 3)),
            dma((4,)),
            dma((2, frame_count // tb, frame_count // tb)),
        ],
        compiler_params=pltpu.CompilerParams(
            collective_id=2, has_side_effects=True, vmem_limit_bytes=VMEM_LIMIT
        ),
        name="gather_attend",
    )(lengths, x, *shards, *vectors)


def both_back_kernel(n, tb, ub, lb, *refs):
    (lengths, middle_h, gout_h, mixed_h, wo_h, wup_h, wdn_h, x_h, nb_h) = refs[:9]
    (qq_h, kk_h, vv_h, raised_h, wq_h, wk_h, wv_h, part, table, bup) = refs[9:19]
    (layer_h, grad_h, gq, gk, gv, go, gu, gd, gc) = refs[19:28]
    (wide, nb, x, grad, gmid, mixed, heads, layer, wo, wup, wdn, held) = refs[28:40]
    dmixed, refs = refs[40], refs[:40] + refs[41:]
    (qbuf, kbuf, vbuf, dqt, turned, sums, sum_up, biases) = refs[40:48]
    refs = refs[:48] + (None,) + refs[48:]
    (parts, core_in, core_sum, near_in, near_sum, far_in) = refs[49:55]
    (core_in2, near_in2, near_sum2, far_in2) = (refs[55 + 3 * j : 58 + 3 * j] for j in range(4))
    (cparts, ccore_in, ccore_sum, cnear_in, cnear_sum, cfar_in) = refs[67:73]
    (row_sem, weight_sem, in_sem, end_sem, raised_sem, held_sem) = refs[73:79]
    refs = refs[:78] + refs[79:]
    (core_s, core_r, near_s, near_r, far_s, far_r) = refs[78:84]
    (core2_s, core2_r, near2_s, near2_r, far2_s, far2_r) = refs[84:90]
    (ccore_s, ccore_r, cnear_s, cnear_r, cfar_s, cfar_r) = refs[90:]
    normed, glow, gbl = nb, x, grad
    far, near = levels_of(n)
    frame_count, width = gmid.shape
    hidden = 4 * width
    share = width // n
    pairs = HEADS // 2
    last = pairs - 1
    me = lax.axis_index("dp")
    top, mid, core = announce(n, me, far, near)
    lane = lax.broadcasted_iota(jnp.int32, (1, 128), 1)
    finish_row = lengths[0, 0] + lengths[0, 1]

    def index(t, m, c):
        return (t * near + m) * 2 + c

    sibling = index(top, mid, 1 - core)
    big = (wo, wup, wdn)

    def row_copies(i):
        r = rows(i * tb, tb)
        return [
            pltpu.make_async_copy(middle_h.at[r], gmid.at[r], row_sem.at[i, 0]),
            pltpu.make_async_copy(gout_h.at[r], glow.at[r], row_sem.at[i, 1]),
            pltpu.make_async_copy(mixed_h.at[r], mixed.at[r], row_sem.at[i, 3]),
        ]

    def layer_copy(i):
        r = rows(i * tb, tb)
        return pltpu.make_async_copy(layer.at[r], layer_h.at[r], row_sem.at[i, 2])

    weight_copies = [
        pltpu.make_async_copy(src, dst, weight_sem.at[a])
        for a, (src, dst) in enumerate(
            ((wup_h, wup), (wdn_h, wdn), (wo_h, wo))
        )
    ]
    held_copies = [
        pltpu.make_async_copy(w, held.at[:, a], held_sem.at[a])
        for a, w in enumerate((wq_h, wk_h, wv_h))
    ]
    nb_copy = pltpu.make_async_copy(nb_h, nb, end_sem.at[2])
    for copy in row_copies(0) + weight_copies:
        copy.start()
    for i in range(1, frame_count // tb):
        for copy in row_copies(i):
            copy.start()
    for copy in held_copies:
        copy.start()

    def core2_copy(a):
        return remote(
            big[a].at[:, :, 1 - core], core_in2[a], core2_s.at[a], core2_r.at[a], sibling
        )

    def near2_copy(a, k):
        peer = lax.rem(mid + k, near)
        return remote(
            big[a].at[:, peer, core],
            near_in2[a].at[k - 1],
            near2_s.at[a, k - 1],
            near2_r.at[a, k - 1],
            index(top, peer, core),
        )

    def far2_copy(a, k):
        peer = bits_differ(top, k, far)
        return remote(
            near_sum2[a].at[peer],
            far_in2[a].at[k - 1],
            far2_s.at[a, k - 1],
            far2_r.at[a, k - 1],
            index(peer, mid, core),
        )

    def second_near(a):
        core2_copy(a).wait_recv()

        def add(f, inner):
            big[a][f, :, core] = (
                big[a][f, :, core].astype(F32) + core_in2[a][f].astype(F32)
            ).astype(BF)
            return inner

        lax.fori_loop(0, far, add, 0)
        for k in range(1, near):
            near2_copy(a, k).start()

    def second_far(a):
        for k in range(1, near):
            near2_copy(a, k).wait_recv()

        def add(f, inner):
            total = big[a][f, mid, core].astype(F32)
            for k in range(near - 1):
                total = total + near_in2[a][k, f].astype(F32)
            near_sum2[a][f] = total.astype(BF)
            return inner

        lax.fori_loop(0, far, add, 0)
        for k in range(1, far):
            far2_copy(a, k).start()

    def core_copy(j):
        return remote(
            parts.at[j, :, :, 1 - core], core_in.at[j], core_s.at[j], core_r.at[j], sibling
        )

    def near_copy(j, k):
        peer = lax.rem(mid + k, near)
        return remote(
            core_sum.at[j, peer],
            near_in.at[j, k - 1],
            near_s.at[j, k - 1],
            near_r.at[j, k - 1],
            index(top, peer, core),
        )

    def far_copy(j):
        peer = index(bits_differ(top, last - j, far), mid, core)
        return remote(near_sum.at[j], far_in.at[j], far_s.at[j], far_r.at[j], peer)

    def add_core(j):
        for m in range(near):
            core_sum[j, m] = (
                parts[j, :, m, core].astype(F32) + core_in[j, :, m].astype(F32)
            ).astype(BF)

    def add_near(j):
        total = core_sum[j, mid].astype(F32)
        for k in range(near - 1):
            total = total + near_in[j, k].astype(F32)
        return total

    def pair_near(j):
        core_copy(j).wait_recv()
        add_core(j)
        for k in range(1, near):
            near_copy(j, k).start()

    def pair_far(j):
        for k in range(1, near):
            near_copy(j, k).wait_recv()
        near_sum[j] = add_near(j).astype(BF)
        far_copy(j).start()

    def in_copies(p, slot):
        cols = rows(p * 128, 128)
        return [
            pltpu.make_async_copy(src.at[:, cols], buf.at[slot], in_sem.at[slot, a])
            for a, (src, buf) in enumerate(((qq_h, qbuf), (kk_h, kbuf), (vv_h, vbuf)))
        ]

    def raised_copies(p, half):
        return [
            pltpu.make_async_copy(
                raised_h.at[2 * p + half, j], wide.at[3 * half + j], raised_sem.at[half, j]
            )
            for j in range(frame_count // ub)
        ]

    gain2, shift2, bdn = (table[i : i + 1, :] for i in range(5, 8))
    sums[...] = jnp.zeros_like(sums)
    sum_up[...] = jnp.zeros_like(sum_up)
    for copy in weight_copies:
        copy.wait()

    def build_heads(i):
        r = rows(i * tb, tb)
        for p in range(pairs):
            cols = slice(128 * p, 128 * p + 128)
            inverse = jnp.where(
                lane < 64, part[r, 2 * p : 2 * p + 1], part[r, 2 * p + 1 : 2 * p + 2]
            )
            scaled = (dmixed[:, cols].astype(F32) * inverse).astype(BF).astype(F32)
            product = scaled * mixed[r, cols].astype(F32)
            for half in range(2):
                own = own_lanes(lane, half)
                base = 64 - 64 * half
                delta = jnp.sum(jnp.where(own, -product, 0.0), axis=1, keepdims=True)
                rest = delta - delta.astype(BF).astype(F32)
                head = jnp.where(own, scaled, 0.0)
                head = jnp.where(lane == base + 3, delta, head)
                head = jnp.where(lane == base + 4, rest, head)
                at = 256 * p + 128 * half
                heads[r, at : at + 128] = head.astype(BF)

    def block(i, carry):
        r = rows(i * tb, tb)
        for copy in row_copies(i):
            copy.wait()
        build_heads(jnp.maximum(i - 1, 0))
        up_rows, down_rows = wup[...].reshape(hidden, width), wdn[...].reshape(width, hidden)
        valid = lax.broadcasted_iota(jnp.int32, (tb, 1), 0) + i * tb < finish_row
        row = gmid[r, :]
        xhat, inv = normal_stats(row)
        normed_rows = (xhat * gain2 + shift2).astype(BF)
        normed[r, :] = normed_rows
        up = dot_nt(normed_rows, up_rows) + bup[0:1, :]
        cdf = 0.5 * (1.0 + lax.erf(up * (1.0 / math.sqrt(2.0))))
        low = (up * cdf).astype(BF)
        for c in range(4):
            wide[c, r, :] = low[:, 512 * c : 512 * c + 512]
        down = dot_nt(low, down_rows) + bdn
        layer[r, :] = jnp.where(valid, row + down, 0.0).astype(BF)
        layer_copy(i).start()
        grow = jnp.where(valid, glow[r, :].astype(F32), 0.0)
        gl = grow.astype(BF)
        glow[r, :] = gl
        slope = cdf + up * jnp.exp(-0.5 * up * up) * (1.0 / math.sqrt(2.0 * math.pi))
        gu = (dot_nn(gl, down_rows) * slope).astype(BF)
        for c in range(4):
            wide[4 + c, r, :] = gu[:, 512 * c : 512 * c + 512]
        gn = dot_nn(gu, up_rows)
        scaled = gn * gain2
        gm = grow + inv * (
            scaled
            - jnp.mean(scaled, axis=-1, keepdims=True)
            - xhat * jnp.mean(scaled * xhat, axis=-1, keepdims=True)
        )
        gmid[r, :] = gm
        gb = gm.astype(BF)
        gbl[r, :] = gb
        dmixed[...] = dot_nn(gb, wo[...].reshape(width, width)).astype(BF)
        sums[4:5, :] += jnp.sum(gb.astype(F32), axis=0, keepdims=True)
        sums[5:6, :] += jnp.sum(gn * xhat, axis=0, keepdims=True)
        sums[6:7, :] += jnp.sum(gn, axis=0, keepdims=True)
        sums[7:8, :] += jnp.sum(grow, axis=0, keepdims=True)
        sum_up[0:1, :] += jnp.sum(gu.astype(F32), axis=0, keepdims=True)
        return carry

    dmixed[...] = jnp.zeros_like(dmixed)
    lax.fori_loop(0, frame_count // tb, block, 0)
    build_heads(frame_count // tb - 1)
    wo[...] = dot_tn(gbl[...], mixed[...]).astype(BF).reshape(wo.shape)
    await_peers(far, near)
    core2_copy(0).start()

    def down_part(c, carry):
        got = dot_tn(glow[...], wide[c]).astype(BF)
        wdn[:, :, :, :, rows(c * 512, 512)] = got.reshape(far, near, 2, share, 512)
        return carry

    lax.fori_loop(0, 4, down_part, 0)
    core2_copy(2).start()
    x_copy = pltpu.make_async_copy(x_h, x, end_sem.at[0])
    x_copy.start()
    for copy in raised_copies(bits_differ(top, last, far), 0):
        copy.start()
    for copy in in_copies(bits_differ(top, last, far), 0):
        copy.start()
    second_near(0)

    def up_part(c, carry):
        wup[c] = dot_tn(wide[4 + c], normed[...]).astype(BF).reshape(near, 2, 4 * share, width)
        return carry

    lax.fori_loop(0, 4, up_part, 0)
    core2_copy(1).start()
    nb_copy.start()
    for copy in raised_copies(bits_differ(top, last, far), 1):
        copy.start()
    plain = sums[...].T
    pieces = sum_up[...].T.reshape(n, 4, share, 8)
    found = jnp.zeros((width, 128), F32)
    for v in range(4, 8):
        found = jnp.where(lane == v, plain[:, v : v + 1], found)
    for k in range(4):
        found = jnp.where(lane == 8 + k, pieces[:, k].reshape(width, 8)[:, 0:1], found)
    biases[...] = found
    second_near(2)
    for copy in held_copies:
        copy.wait()
    nb_copy.wait()

    def pair_step(i, carry):
        p = bits_differ(top, last - i, far)
        slot = lax.rem(i, 2)
        cols = rows(p * 128, 128)
        for copy in in_copies(p, slot):
            copy.wait()

        @pl.when(i < last)
        def _():
            for copy in in_copies(bits_differ(top, last - i - 1, far), 1 - slot):
                copy.start()

        turned_query = qbuf[slot].T
        turned_key = kbuf[slot].T
        for half in range(2):
            own = own_lanes(lane, half)
            base = 64 - 64 * half
            for copy in raised_copies(p, half):
                copy.wait()
            grad_head = heads[:, rows((2 * p + half) * 128, 128)]
            turned_grad = grad_head.T
            part_rows = slice(64 * half, 64 * half + 64)
            ones = jnp.where(
                (lane >= base + 3) & (lane < base + 5), jnp.ones((1, 128), F32), 0.0
            ).astype(BF)
            for j in range(frame_count // ub):
                r = pl.ds(j * ub, ub)
                value = jnp.where(own, vbuf[slot, r, :], ones)
                weights = wide[3 * half + j]
                gs = (weights.astype(F32) * dot_nt(grad_head, value)).astype(BF)
                turned[p, 2, part_rows, r] = dot_nn(turned_grad, weights)[part_rows].astype(BF)
                turned[p, 1, part_rows, r] = dot_nn(turned_query, gs)[part_rows].astype(BF)
                step = dot_nn(turned_key[:, j * ub : j * ub + ub], gs.T)[part_rows]
                if j == 0:
                    dqt[...] = step
                else:
                    dqt[...] += step
            turned[p, 0, part_rows, :] = (dqt[...] * 0.125).astype(BF)

            @pl.when(i < last)
            def _():
                for copy in raised_copies(bits_differ(top, last - i - 1, far), half):
                    copy.start()

            if half == 0:
                pl.when(i == 0)(functools.partial(second_near, 1))
                pl.when(i > 0)(functools.partial(pair_near, i - 1))
                pl.when(i == last)(functools.partial(pair_far, 0))
            else:
                for step_index, a in ((0, 0), (1, 2), (2, 1)):
                    pl.when(i == step_index)(functools.partial(second_far, a))
                pl.when(i == last)(functools.partial(pair_far, 1))

        pair_rows = rows(p * 128, 128)
        shape = (near, 2, share, width)
        found = dot_nn(turned[p].reshape(3 * 128, frame_count), nb[...])
        found = [found[128 * a : 128 * a + 128] for a in range(3)]
        for a in range(3):
            parts[i, a] = found[a].astype(BF).reshape(shape)
        core_copy(i).start()
        column = [
            jnp.sum(turned[p, a].astype(F32), axis=1, keepdims=True) for a in range(3)
        ]
        own_weights = [held[p, a].reshape(128, width).astype(F32) for a in range(3)]
        with_rows = sum(g * w for g, w in zip(found, own_weights))
        alone = sum(c * w for c, w in zip(column, own_weights))
        sums[0:1, :] += jnp.sum(with_rows, axis=0, keepdims=True)
        sums[1:2, :] += jnp.sum(alone, axis=0, keepdims=True)
        biases[pair_rows, :] = jnp.where(
            lane == 2, column[0], jnp.where(lane == 3, column[2], biases[pair_rows, :])
        )
        return carry

    sums[...] = jnp.zeros_like(sums)
    lax.fori_loop(0, pairs, pair_step, 0)

    gain, shift = table[0:1, :], table[1:2, :]
    sums[0:1, :] = (sums[0:1, :] - shift * sums[1:2, :]) / gain
    plain = sums[...].T
    found = jnp.where(lane == 0, plain[:, 0:1], biases[...])
    found = jnp.where(lane == 1, plain[:, 1:2], found)
    cparts[...] = found.astype(BF).reshape(far, near, 2, share, 128)
    ccore = remote(cparts.at[:, :, 1 - core], ccore_in, ccore_s, ccore_r, sibling)
    ccore.start()
    pair_near(last)
    pair_far(last - 1)
    cnear, cfar = [], []
    for k in range(1, near):
        peer = lax.rem(mid + k, near)
        cnear.append(
            remote(
                ccore_sum.at[peer],
                cnear_in.at[k - 1],
                cnear_s.at[k - 1],
                cnear_r.at[k - 1],
                index(top, peer, core),
            )
        )
    for k in range(1, far):
        peer = bits_differ(top, k, far)
        cfar.append(
            remote(
                cnear_sum.at[peer],
                cfar_in.at[k - 1],
                cfar_s.at[k - 1],
                cfar_r.at[k - 1],
                index(peer, mid, core),
            )
        )
    x_copy.wait()

    def finish(i, carry):
        r = rows(i * lb, lb)
        gn = dot_tn(
            turned[:, :, :, r].reshape(3 * width, lb), held[...].reshape(3 * width, width)
        )
        xhat, inv = normal_stats(x[r, :].astype(F32))
        scaled = gn * gain
        grad[r, :] = (
            gmid[r, :]
            + inv
            * (
                scaled
                - jnp.mean(scaled, axis=-1, keepdims=True)
                - xhat * jnp.mean(scaled * xhat, axis=-1, keepdims=True)
            )
        ).astype(BF)

        @pl.when(i == 0)
        def _():
            ccore.wait_recv()
            for m in range(near):
                ccore_sum[m] = (
                    cparts[:, m, core].astype(F32) + ccore_in[:, m].astype(F32)
                ).astype(BF)
            for copy in cnear:
                copy.start()

        @pl.when(i == 1)
        def _():
            for copy in cnear:
                copy.wait_recv()
            total = ccore_sum[mid].astype(F32)
            for k in range(near - 1):
                total = total + cnear_in[k].astype(F32)
            cnear_sum[...] = total.astype(BF)
            for copy in cfar:
                copy.start()

        return carry

    lax.fori_loop(0, frame_count // lb, finish, 0)
    grad_copy = pltpu.make_async_copy(grad, grad_h, end_sem.at[1])
    grad_copy.start()
    for k in range(1, near):
        near_copy(last, k).wait_recv()
    total = add_near(last)
    for j in range(last):
        far_copy(j).wait_recv()
        total = total + far_in[j].astype(F32)
    gq[...] = total[0]
    gk[...] = total[1]
    gv[...] = total[2]
    for a, out in enumerate((go, gu, gd)):
        for k in range(1, far):
            far2_copy(a, k).wait_recv()
        total = near_sum2[a][top].astype(F32)
        for k in range(far - 1):
            total = total + far_in2[a][k].astype(F32)
        out[...] = total
    for copy in cfar:
        copy.wait_recv()
    total = cnear_sum[top].astype(F32)
    for k in range(far - 1):
        total = total + cfar_in[k].astype(F32)
    gc[...] = total
    for a in range(3):
        core2_copy(a).wait_send()
        for k in range(1, near):
            near2_copy(a, k).wait_send()
        for k in range(1, far):
            far2_copy(a, k).wait_send()
    for j in range(pairs):
        core_copy(j).wait_send()
        for k in range(1, near):
            near_copy(j, k).wait_send()
        if j < last:
            far_copy(j).wait_send()
    ccore.wait_send()
    for copy in cnear + cfar:
        copy.wait_send()
    for i in range(frame_count // tb):
        layer_copy(i).wait()
    grad_copy.wait()


def both_back(n, lengths, middle, gout, mixed, big, x, nb, qkv, raised, part, weights, table, bup):
    far, near = levels_of(n)
    frame_count, width = x.shape
    share = width // n
    pairs = HEADS // 2
    blocks = [p.shape[3:] for p in big]
    row_block = jax.ShapeDtypeStruct((share, width), F32)
    low = jax.ShapeDtypeStruct((frame_count, width), BF)
    low_rows = pltpu.VMEM((frame_count, width), BF)
    pair_rows = pltpu.VMEM((2, frame_count, 128), BF)
    dma = pltpu.SemaphoreType.DMA
    tb, ub = 384, raised.shape[3]
    return pl.pallas_call(
        functools.partial(both_back_kernel, n, tb, ub, 512),
        out_shape=[low, low, row_block, row_block, row_block]
        + [jax.ShapeDtypeStruct(b, F32) for b in blocks]
        + [jax.ShapeDtypeStruct((share, 128), F32)],
        in_specs=[SMEM_SPEC] + [HBM_SPEC] * 15 + [VMEM_SPEC] * 3,
        out_specs=[HBM_SPEC] * 2 + [VMEM_SPEC] * 7,
        scratch_shapes=[
            pltpu.VMEM((8, frame_count, 512), BF),
            low_rows,
            low_rows,
            low_rows,
            pltpu.VMEM((frame_count, width), F32),
            low_rows,
            pltpu.VMEM((frame_count, HEADS * 128), BF),
            low_rows,
        ]
        + [pltpu.VMEM(p.shape, BF) for p in big]
        + [
            pltpu.VMEM((pairs, 3) + weights[0].shape[1:], BF),
            pltpu.VMEM((tb, width), BF),
            pair_rows,
            pair_rows,
            pair_rows,
            pltpu.VMEM((64, frame_count), F32),
            pltpu.VMEM((pairs, 3, 128, frame_count), BF),
            pltpu.VMEM((8, width), F32),
            pltpu.VMEM((8, 4 * width), F32),
            pltpu.VMEM((width, 128), F32),
            pltpu.VMEM((pairs, 3, near, 2, share, width), BF),
            pltpu.VMEM((pairs, 3, near, share, width), BF),
            pltpu.VMEM((pairs, near, 3, share, width), BF),
            pltpu.VMEM((pairs, near - 1, 3, share, width), BF),
            pltpu.VMEM((pairs, 3, share, width), BF),
            pltpu.VMEM((pairs - 1, 3, share, width), BF),
        ]
        + [pltpu.VMEM((far, near) + b, BF) for b in blocks]
        + [pltpu.VMEM((near - 1, far) + b, BF) for b in blocks]
        + [pltpu.VMEM((far,) + b, BF) for b in blocks]
        + [pltpu.VMEM((far - 1,) + b, BF) for b in blocks]
        + [
            pltpu.VMEM((far, near, 2, share, 128), BF),
            pltpu.VMEM((far, near, share, 128), BF),
            pltpu.VMEM((near, far, share, 128), BF),
            pltpu.VMEM((near - 1, far, share, 128), BF),
            pltpu.VMEM((far, share, 128), BF),
            pltpu.VMEM((far - 1, share, 128), BF),
            dma((frame_count // tb, 4)),
            dma((3,)),
            dma((2, 3)),
            dma((3,)),
            dma((2, frame_count // ub)),
            dma((3,)),
            dma((pairs,)),
            dma((pairs,)),
            dma((pairs, near - 1)),
            dma((pairs, near - 1)),
            dma((pairs,)),
            dma((pairs,)),
            dma((3,)),
            dma((3,)),
            dma((3, near - 1)),
            dma((3, near - 1)),
            dma((3, far - 1)),
            dma((3, far - 1)),
            dma,
            dma,
            dma((near - 1,)),
            dma((near - 1,)),
            dma((far - 1,)),
            dma((far - 1,)),
        ],
        compiler_params=pltpu.CompilerParams(
            collective_id=3, has_side_effects=True, vmem_limit_bytes=67043328
        ),
        name="both_back",
    )(lengths, middle, gout, mixed, *big, x, nb, *qkv, raised, *weights, part, table, bup)


def hand_out_kernel(pieces, *refs):
    rows_in, ins, rows_out, outs = refs[:2], refs[2:9], refs[9:11], refs[11:26]
    rows_held, held, lanes = refs[26:28], refs[28:34], refs[34]
    read_sem, write_sem, in_sem, out_sem = refs[35:]
    size = rows_held[0].shape[0] // pieces
    reads, writes = [], []
    for j in range(pieces):
        for b in range(2):
            r = pl.ds(j * size, size)
            reads.append(
                pltpu.make_async_copy(rows_in[b].at[r], rows_held[b].at[r], read_sem.at[b, j])
            )
            writes.append(
                pltpu.make_async_copy(rows_held[b].at[r], rows_out[b].at[r], write_sem.at[b, j])
            )
    small_in = [pltpu.make_async_copy(ins[a], held[a], in_sem.at[a]) for a in range(6)]
    small_in.append(pltpu.make_async_copy(ins[6], lanes, in_sem.at[6]))
    small_out = [pltpu.make_async_copy(held[a], outs[a], out_sem.at[a]) for a in range(6)]
    for copy in small_in + reads:
        copy.start()
    for read, write in zip(reads, writes):
        read.wait()
        write.start()
    for a in range(6):
        small_in[a].wait()
        small_out[a].start()
    small_in[6].wait()
    turned = lanes[...].T
    for v in range(8):
        outs[6 + v][...] = turned[v : v + 1, :]
    share = turned.shape[1]
    for k in range(4):
        outs[14][:, share * k : share * k + share] = turned[8 + k : 9 + k, :]
    for copy in writes + small_out:
        copy.wait()


def hand_out(large, totals):
    share = totals[0].shape[0]
    line = jax.ShapeDtypeStruct((1, share), F32)
    dma = pltpu.SemaphoreType.DMA
    pieces = 4
    return pl.pallas_call(
        functools.partial(hand_out_kernel, pieces),
        out_shape=[jax.ShapeDtypeStruct(a.shape, a.dtype) for a in large]
        + [jax.ShapeDtypeStruct(t.shape, F32) for t in totals[:6]]
        + [line] * 8
        + [jax.ShapeDtypeStruct((1, 4 * share), F32)],
        in_specs=[HBM_SPEC] * 9,
        out_specs=[HBM_SPEC] * 8 + [VMEM_SPEC] * 9,
        scratch_shapes=[pltpu.VMEM(a.shape, a.dtype) for a in large]
        + [pltpu.VMEM(t.shape, F32) for t in totals]
        + [dma((2, pieces)), dma((2, pieces)), dma((7,)), dma((6,))],
        compiler_params=pltpu.CompilerParams(vmem_limit_bytes=60 << 20),
        name="hand_out",
    )(*large, *totals)


def per_device_fused(n, frames, lengths, vectors, up_bias, weights, grad_out):
    width = frames.shape[2]
    x = frames[0]
    got = gather_attend(n, lengths, x, tuple(w.T for w in weights), vectors + (up_bias,))
    table, bup, qq, kk, vv, raised, part, nb, mixed, middle = got[6:]
    sums = both_back(
        n,
        lengths,
        middle,
        grad_out[0],
        mixed,
        got[3:6],
        x,
        nb,
        (qq, kk, vv),
        raised,
        part,
        got[:3],
        table,
        bup,
    )
    layer_out, grad_x, *outs = hand_out(sums[:2], sums[2:])
    gq, gk, gv, go, gu, gd = (g.T for g in outs[:6])
    line = [v.reshape(-1) for v in outs[6:14]]
    return (
        layer_out[None],
        grad_x[None],
        line[0],
        line[1],
        gq,
        line[2],
        gk,
        gv,
        line[3],
        go,
        line[4],
        line[5],
        line[6],
        gu,
        outs[14].reshape(-1),
        gd,
        line[7],
    )


def per_device(
    n,
    frames,
    lengths,
    attn_gain,
    attn_shift,
    query_weight,
    query_bias,
    key_weight,
    value_weight,
    value_bias,
    out_weight,
    out_bias,
    mlp_gain,
    mlp_shift,
    up_weight,
    up_bias,
    down_weight,
    down_bias,
    grad_out,
):
    slots, frame_count, width = frames.shape
    assert slots == 1
    share = width // n
    vectors = (
        attn_gain,
        attn_shift,
        query_bias,
        value_bias,
        out_bias,
        mlp_gain,
        mlp_shift,
        down_bias,
    )
    far, near = levels_of(n)
    if share % 16 == 0 and far == HEADS // 2:
        return per_device_fused(
            n,
            frames,
            lengths,
            vectors,
            up_bias,
            (query_weight, key_weight, value_weight, out_weight, up_weight, down_weight),
            grad_out,
        )
    packed = jnp.concatenate(
        [jnp.stack(vectors, axis=1), up_bias.reshape(share, 4), jnp.zeros((share, 116), BF)], axis=1
    )
    shards = (
        query_weight.T,
        key_weight.T,
        value_weight.T,
        out_weight.T,
        up_weight.T,
        down_weight.T,
        packed,
    )
    full = gather_all(n, shards)
    wq, wk, wv, wo, wup, wdn, vec = (
        f.reshape(n * f.shape[3], f.shape[4]) for f in full
    )
    bup = vec[:, 8:12].reshape(1, 4 * width)
    x = frames[0]
    nb, qaug, kk, vv, mixed, middle, kaug = attend(lengths, x, wq, wk, wv, wo, vec)
    layer_out, gmid, dmixed, dwo, dwup, dwdn, sums_two, sum_up = feed(
        lengths, middle, grad_out[0], mixed, wup, wdn, wo, vec, bup
    )
    grad_x, dwq, dwk, dwv, sums_one = attend_back(
        x, gmid, nb, qaug, kk, vv, mixed, dmixed, kaug, wq, wk, wv, vec
    )
    columns = jnp.concatenate(
        [
            sums_one[:4].T,
            sums_two[:4].T,
            sum_up[0].reshape(width, 4),
            jnp.zeros((width, 116), F32),
        ],
        axis=1,
    ).astype(BF)

    def split(g):
        return g.reshape(far, near, 2, g.shape[0] // n, g.shape[1])

    gq, gk, gv, go, gu, gd, gc = scatter_all(
        n, tuple(split(g) for g in (dwq, dwk, dwv, dwo, dwup, dwdn, columns))
    )
    return (
        layer_out[None],
        grad_x[None],
        gc[:, 0],
        gc[:, 1],
        gq.T,
        gc[:, 2],
        gk.T,
        gv.T,
        gc[:, 3],
        go.T,
        gc[:, 4],
        gc[:, 5],
        gc[:, 6],
        gu.T,
        gc[:, 8:12].reshape(4 * share),
        gd.T,
        gc[:, 7],
    )


def solution(mesh):
    row, col, vector = P("dp", None, None), P(None, "dp"), P("dp")
    return jax.shard_map(
        functools.partial(per_device, mesh.shape["dp"]),
        mesh=mesh,
        in_specs=(
            row,
            P("dp", None),
            vector,
            vector,
            col,
            vector,
            col,
            col,
            vector,
            col,
            vector,
            vector,
            vector,
            col,
            vector,
            col,
            vector,
            row,
        ),
        out_specs=(
            row,
            row,
            vector,
            vector,
            col,
            vector,
            col,
            col,
            vector,
            col,
            vector,
            vector,
            vector,
            col,
            vector,
            col,
            vector,
        ),
        check_vma=False,
    )
```

```python
import functools
import math

import jax
import jax.numpy as jnp
from jax import lax
from jax.experimental import pallas as pl
from jax.experimental.pallas import tpu as pltpu
from jax.sharding import PartitionSpec as P

HEADS = 8
EPS = 1e-05
MESH = pl.DeviceIdType.MESH
F32 = jnp.float32
BF = jnp.bfloat16
VMEM_SPEC = pl.BlockSpec(memory_space=pltpu.VMEM)
SMEM_SPEC = pl.BlockSpec(memory_space=pltpu.SMEM)
HBM_SPEC = pl.BlockSpec(memory_space=pl.ANY)
EXCLUDED = -1e30
VMEM_LIMIT = 62 << 20


def dot_nn(a, b):
    return lax.dot_general(a, b, (((1,), (0,)), ((), ())), preferred_element_type=F32)


def dot_nt(a, b):
    return lax.dot_general(a, b, (((1,), (1,)), ((), ())), preferred_element_type=F32)


def dot_tn(a, b):
    return lax.dot_general(a, b, (((0,), (0,)), ((), ())), preferred_element_type=F32)


def levels_of(n):
    rest = n // 2
    bits = rest.bit_length() - 1
    near = 2 ** ((bits + 1) // 2)
    return rest // near, near


def rows(start, size):
    return pl.ds(pl.multiple_of(start, size), size)


def normal_stats(block):
    mean = jnp.mean(block, axis=-1, keepdims=True)
    centered = block - mean
    inv = lax.rsqrt(jnp.mean(centered * centered, axis=-1, keepdims=True) + EPS)
    return centered * inv, inv


def announce(n, me, far, near):
    barrier = pltpu.get_barrier_semaphore()
    core = lax.rem(me, 2)
    mid = lax.rem(me // 2, near)
    top = me // (2 * near)
    peers = [(lax.rem(top + k, far) * near + mid) * 2 + core for k in range(1, far)]
    peers += [(top * near + lax.rem(mid + k, near)) * 2 + core for k in range(1, near)]
    peers += [(top * near + mid) * 2 + 1 - core]
    for peer in peers:
        pl.semaphore_signal(barrier, inc=1, device_id=(peer,), device_id_type=MESH)
    return top, mid, core


def await_peers(far, near):
    pl.semaphore_wait(pltpu.get_barrier_semaphore(), far + near - 1)


def everyone_barrier(n, me, far, near):
    place = announce(n, me, far, near)
    await_peers(far, near)
    return place


def gather_kernel(n, count, *refs):
    shards, outs = refs[:count], refs[count : 2 * count]
    own_sem, far_s, far_r, near_s, near_r, core_s, core_r = refs[2 * count :]
    far, near = levels_of(n)
    me = lax.axis_index("dp")
    top, mid, core = everyone_barrier(n, me, far, near)

    def index(t, m, c):
        return (t * near + m) * 2 + c

    far_copies, near_copies = {}, {}
    for a in range(count):
        for k in range(1, far):
            copy = pltpu.make_async_remote_copy(
                src_ref=shards[a],
                dst_ref=outs[a].at[top, mid, core],
                send_sem=far_s.at[a, k - 1],
                recv_sem=far_r.at[a, k - 1],
                device_id=(index(lax.rem(top + k, far), mid, core),),
                device_id_type=MESH,
            )
            copy.start()
            far_copies[a, k] = copy
        pltpu.make_async_copy(shards[a], outs[a].at[top, mid, core], own_sem.at[a]).start()
    for a in range(count):
        pltpu.make_async_copy(shards[a], outs[a].at[top, mid, core], own_sem.at[a]).wait()
        for k in range(1, far):
            far_copies[a, k].wait_recv()
        for k in range(1, near):
            copy = pltpu.make_async_remote_copy(
                src_ref=outs[a].at[:, mid, core],
                dst_ref=outs[a].at[:, mid, core],
                send_sem=near_s.at[a, k - 1],
                recv_sem=near_r.at[a, k - 1],
                device_id=(index(top, lax.rem(mid + k, near), core),),
                device_id_type=MESH,
            )
            copy.start()
            near_copies[a, k] = copy
    core_copies = []
    for a in range(count):
        for k in range(1, near):
            near_copies[a, k].wait_recv()
        copy = pltpu.make_async_remote_copy(
            src_ref=outs[a].at[:, :, core],
            dst_ref=outs[a].at[:, :, core],
            send_sem=core_s.at[a],
            recv_sem=core_r.at[a],
            device_id=(index(top, mid, 1 - core),),
            device_id_type=MESH,
        )
        copy.start()
        core_copies.append(copy)
    for a in range(count):
        core_copies[a].wait_recv()
    for a in range(count):
        for k in range(1, far):
            far_copies[a, k].wait_send()
        for k in range(1, near):
            near_copies[a, k].wait_send()
        core_copies[a].wait_send()


def gather_all(n, shards):
    far, near = levels_of(n)
    count = len(shards)
    return pl.pallas_call(
        functools.partial(gather_kernel, n, count),
        out_shape=[jax.ShapeDtypeStruct((far, near, 2) + s.shape, s.dtype) for s in shards],
        in_specs=[VMEM_SPEC] * count,
        out_specs=[HBM_SPEC] * count,
        scratch_shapes=[
            pltpu.SemaphoreType.DMA((count,)),
            pltpu.SemaphoreType.DMA((count, far - 1)),
            pltpu.SemaphoreType.DMA((count, far - 1)),
            pltpu.SemaphoreType.DMA((count, near - 1)),
            pltpu.SemaphoreType.DMA((count, near - 1)),
            pltpu.SemaphoreType.DMA((count,)),
            pltpu.SemaphoreType.DMA((count,)),
        ],
        compiler_params=pltpu.CompilerParams(
            collective_id=0, has_side_effects=True, vmem_limit_bytes=32 << 20
        ),
        name="gather_params",
    )(*shards)


def scatter_kernel(n, count, *refs):
    parts, outs = refs[:count], refs[count : 2 * count]
    pos = 2 * count
    core_in, core_sum = refs[pos : pos + count], refs[pos + count : pos + 2 * count]
    pos += 2 * count
    near_in, near_sum = refs[pos : pos + count], refs[pos + count : pos + 2 * count]
    pos += 2 * count
    far_in = refs[pos : pos + count]
    core_s, core_r, near_s, near_r, far_s, far_r = refs[pos + count :]
    far, near = levels_of(n)
    me = lax.axis_index("dp")
    top, mid, core = everyone_barrier(n, me, far, near)

    def index(t, m, c):
        return (t * near + m) * 2 + c

    core_copies, near_copies, far_copies = [], {}, {}
    for a in range(count):
        copy = pltpu.make_async_remote_copy(
            src_ref=parts[a].at[:, :, 1 - core],
            dst_ref=core_in[a],
            send_sem=core_s.at[a],
            recv_sem=core_r.at[a],
            device_id=(index(top, mid, 1 - core),),
            device_id_type=MESH,
        )
        copy.start()
        core_copies.append(copy)
    for a in range(count):
        core_copies[a].wait_recv()

        def add_core(i, carry, a=a):
            f, m = i // near, lax.rem(i, near)
            core_sum[a][m, f] = (
                parts[a][f, m, core].astype(F32) + core_in[a][f, m].astype(F32)
            ).astype(BF)
            return carry

        lax.fori_loop(0, far * near, add_core, 0)
        for k in range(1, near):
            peer = lax.rem(mid + k, near)
            copy = pltpu.make_async_remote_copy(
                src_ref=core_sum[a].at[peer],
                dst_ref=near_in[a].at[k - 1],
                send_sem=near_s.at[a, k - 1],
                recv_sem=near_r.at[a, k - 1],
                device_id=(index(top, peer, core),),
                device_id_type=MESH,
            )
            copy.start()
            near_copies[a, k] = copy
    for a in range(count):
        for k in range(1, near):
            near_copies[a, k].wait_recv()

        def add_near(f, carry, a=a):
            total = core_sum[a][mid, f].astype(F32)
            for k in range(near - 1):
                total = total + near_in[a][k, f].astype(F32)
            near_sum[a][f] = total.astype(BF)
            return carry

        lax.fori_loop(0, far, add_near, 0)
        for k in range(1, far):
            peer = lax.rem(top + k, far)
            copy = pltpu.make_async_remote_copy(
                src_ref=near_sum[a].at[peer],
                dst_ref=far_in[a].at[k - 1],
                send_sem=far_s.at[a, k - 1],
                recv_sem=far_r.at[a, k - 1],
                device_id=(index(peer, mid, core),),
                device_id_type=MESH,
            )
            copy.start()
            far_copies[a, k] = copy
    for a in range(count):
        for k in range(1, far):
            far_copies[a, k].wait_recv()
        total = near_sum[a][top].astype(F32)
        for k in range(far - 1):
            total = total + far_in[a][k].astype(F32)
        outs[a][...] = total
    for a in range(count):
        core_copies[a].wait_send()
        for k in range(1, near):
            near_copies[a, k].wait_send()
        for k in range(1, far):
            far_copies[a, k].wait_send()


def scatter_all(n, parts):
    far, near = levels_of(n)
    count = len(parts)
    blocks = [p.shape[3:] for p in parts]
    return pl.pallas_call(
        functools.partial(scatter_kernel, n, count),
        out_shape=[jax.ShapeDtypeStruct(b, F32) for b in blocks],
        in_specs=[VMEM_SPEC] * count,
        out_specs=[VMEM_SPEC] * count,
        scratch_shapes=[pltpu.VMEM((far, near) + b, BF) for b in blocks]
        + [pltpu.VMEM((near, far) + b, BF) for b in blocks]
        + [pltpu.VMEM((near - 1, far) + b, BF) for b in blocks]
        + [pltpu.VMEM((far,) + b, BF) for b in blocks]
        + [pltpu.VMEM((far - 1,) + b, BF) for b in blocks]
        + [
            pltpu.SemaphoreType.DMA((count,)),
            pltpu.SemaphoreType.DMA((count,)),
            pltpu.SemaphoreType.DMA((count, near - 1)),
            pltpu.SemaphoreType.DMA((count, near - 1)),
            pltpu.SemaphoreType.DMA((count, far - 1)),
            pltpu.SemaphoreType.DMA((count, far - 1)),
        ],
        compiler_params=pltpu.CompilerParams(
            collective_id=1, has_side_effects=True, vmem_limit_bytes=VMEM_LIMIT
        ),
        name="scatter_grads",
    )(*parts)


def segment_lanes(lengths, position, lane):
    leading = lengths[0, 0]
    finish = leading + lengths[0, 1]
    segment = jnp.where(position < leading, 0, jnp.where(position < finish, 1, 2))
    return lax.rem(lane, 64) == segment


def three_pieces(column):
    high = column.astype(BF)
    rest = column - high.astype(F32)
    middle = rest.astype(BF)
    return high, middle, (rest - middle.astype(F32)).astype(BF)


def own_lanes(lane, half):
    return (lane < 64) if half == 0 else (lane >= 64)


def attend_kernel(
    lengths, x, wq, wk, wv, wo, vec, nb, qaug, kk, vv, mixed, middle, kaug, qbuf, *, tb, lb
):
    frame_count = x.shape[0]
    lane = lax.broadcasted_iota(jnp.int32, (1, 128), 1)
    table = vec[...].astype(F32).T
    gain, shift, bq, bv, bo = (table[i : i + 1] for i in range(5))

    def project(i, carry):
        r = rows(i * lb, lb)
        xhat, _ = normal_stats(x[r, :].astype(F32))
        normed = (xhat * gain + shift).astype(BF)
        nb[r, :] = normed
        qbuf[r, :] = ((dot_nt(normed, wq[...]) + bq).astype(BF).astype(F32) * 0.125).astype(BF)
        kk[r, :] = dot_nt(normed, wk[...]).astype(BF)
        vv[r, :] = (dot_nt(normed, wv[...]) + bv).astype(BF)
        position = lax.broadcasted_iota(jnp.int32, (lb, 128), 0) + i * lb
        lanes = lax.broadcasted_iota(jnp.int32, (lb, 128), 1)
        same = segment_lanes(lengths, position, lanes)
        slot = lax.rem(lanes, 64)
        kaug[r, :] = jnp.where(
            slot < 3, jnp.where(same, 0.0, EXCLUDED), jnp.where(slot < 6, 1.0, 0.0)
        ).astype(BF)
        return carry

    lax.fori_loop(0, frame_count // lb, project, 0)

    def pair_step(p, carry):
        cols = rows(p * 128, 128)
        for half in range(2):
            own = own_lanes(lane, half)
            base = 64 - 64 * half
            key = jnp.where(own, kk[:, cols], kaug[...])
            value = jnp.where(own, vv[:, cols], jnp.ones((1, 128), BF))
            head = pl.multiple_of((2 * p + half) * 128, 128)

            def block(i, inner, half=half, own=own, base=base, key=key, value=value, head=head):
                r = rows(i * tb, tb)
                position = lax.broadcasted_iota(jnp.int32, (tb, 128), 0) + i * tb
                lanes = lax.broadcasted_iota(jnp.int32, (tb, 128), 1)
                mark = jnp.where(segment_lanes(lengths, position, lanes), 1.0, 0.0).astype(BF)
                query = jnp.where(own, qbuf[r, cols], mark)
                scores = dot_nt(query, key)
                top = jnp.max(scores, axis=1, keepdims=True)
                raised = jnp.exp(scores - top).astype(BF)
                got = dot_nn(raised, value)
                total = got[:, base : base + 1]
                got = (got * (1.0 / total)).astype(BF)
                if half == 0:
                    mixed[r, cols] = got
                else:
                    mixed[r, cols] = jnp.where(own, got, mixed[r, cols])
                high, mid, low = three_pieces(-(top + jnp.log(total)))
                query = jnp.where(lane == base + 3, high, query)
                query = jnp.where(lane == base + 4, mid, query)
                qaug[r, pl.ds(head, 128)] = jnp.where(lane == base + 5, low, query)
                return inner

            lax.fori_loop(0, frame_count // tb, block, 0, unroll=True)
        return carry

    lax.fori_loop(0, HEADS // 2, pair_step, 0)

    def finish(i, carry):
        r = rows(i * lb, lb)
        middle[r, :] = x[r, :].astype(F32) + (dot_nt(mixed[r, :], wo[...]) + bo)
        return carry

    lax.fori_loop(0, frame_count // lb, finish, 0)


def attend(lengths, x, wq, wk, wv, wo, vec):
    frame_count, width = x.shape
    low = jax.ShapeDtypeStruct((frame_count, width), BF)
    return pl.pallas_call(
        functools.partial(attend_kernel, tb=512, lb=512),
        out_shape=[
            low,
            jax.ShapeDtypeStruct((frame_count, HEADS * 128), BF),
            low,
            low,
            low,
            jax.ShapeDtypeStruct((frame_count, width), F32),
            jax.ShapeDtypeStruct((frame_count, 128), BF),
        ],
        in_specs=[SMEM_SPEC] + [VMEM_SPEC] * 6,
        out_specs=[VMEM_SPEC] * 7,
        scratch_shapes=[pltpu.VMEM((frame_count, width), BF)],
        compiler_params=pltpu.CompilerParams(vmem_limit_bytes=VMEM_LIMIT),
        name="attend_forward",
    )(lengths, x, wq, wk, wv, wo, vec)


def feed_kernel(
    lengths,
    middle,
    gout,
    mixed,
    wup,
    wdn,
    wo,
    vec,
    bup,
    layer_out,
    gmid,
    dmixed,
    dwo,
    dwup,
    dwdn,
    sums,
    sum_up,
    nb,
    act,
    gup,
    glow,
    gbl,
    *,
    tb,
):
    frame_count = middle.shape[0]
    finish = lengths[0, 0] + lengths[0, 1]
    table = vec[...].astype(F32).T
    gain, shift, bdn = (table[i : i + 1] for i in range(5, 8))
    sums[...] = jnp.zeros_like(sums)
    sum_up[...] = jnp.zeros_like(sum_up)

    def block(i, carry):
        r = rows(i * tb, tb)
        valid = lax.broadcasted_iota(jnp.int32, (tb, 1), 0) + i * tb < finish
        mid = middle[r, :]
        xhat, inv = normal_stats(mid)
        normed = (xhat * gain + shift).astype(BF)
        nb[r, :] = normed
        up = dot_nt(normed, wup[...]) + bup[...].astype(F32)
        cdf = 0.5 * (1.0 + lax.erf(up * (1.0 / math.sqrt(2.0))))
        low = (up * cdf).astype(BF)
        act[r, :] = low
        down = dot_nt(low, wdn[...]) + bdn
        layer_out[r, :] = jnp.where(valid, mid + down, 0.0).astype(BF)
        grow = jnp.where(valid, gout[r, :].astype(F32), 0.0)
        gl = grow.astype(BF)
        glow[r, :] = gl
        slope = cdf + up * jnp.exp(-0.5 * up * up) * (1.0 / math.sqrt(2.0 * math.pi))
        gu = (dot_nn(gl, wdn[...]) * slope).astype(BF)
        gup[r, :] = gu
        gn = dot_nn(gu, wup[...])
        scaled = gn * gain
        gm = grow + inv * (
            scaled
            - jnp.mean(scaled, axis=-1, keepdims=True)
            - xhat * jnp.mean(scaled * xhat, axis=-1, keepdims=True)
        )
        gmid[r, :] = gm
        gb = gm.astype(BF)
        gbl[r, :] = gb
        dmixed[r, :] = dot_nn(gb, wo[...]).astype(BF)
        sums[0:1, :] += jnp.sum(gb.astype(F32), axis=0, keepdims=True)
        sums[1:2, :] += jnp.sum(gn * xhat, axis=0, keepdims=True)
        sums[2:3, :] += jnp.sum(gn, axis=0, keepdims=True)
        sums[3:4, :] += jnp.sum(grow, axis=0, keepdims=True)
        sum_up[0:1, :] += jnp.sum(gu.astype(F32), axis=0, keepdims=True)
        return carry

    lax.fori_loop(0, frame_count // tb, block, 0)
    dwo[...] = dot_tn(gbl[...], mixed[...]).astype(BF)

    def weights(i, carry):
        c = rows(i * 512, 512)
        dwup[c, :] = dot_tn(gup[:, c], nb[...]).astype(BF)
        dwdn[:, c] = dot_tn(glow[...], act[:, c]).astype(BF)
        return carry

    lax.fori_loop(0, wup.shape[0] // 512, weights, 0)


def feed(lengths, middle, gout, mixed, wup, wdn, wo, vec, bup):
    frame_count, width = middle.shape
    hidden = wup.shape[0]
    low = jax.ShapeDtypeStruct((frame_count, width), BF)
    return pl.pallas_call(
        functools.partial(feed_kernel, tb=256),
        out_shape=[
            low,
            jax.ShapeDtypeStruct((frame_count, width), F32),
            low,
            jax.ShapeDtypeStruct((width, width), BF),
            jax.ShapeDtypeStruct((hidden, width), BF),
            jax.ShapeDtypeStruct((width, hidden), BF),
            jax.ShapeDtypeStruct((8, width), F32),
            jax.ShapeDtypeStruct((8, hidden), F32),
        ],
        in_specs=[SMEM_SPEC] + [VMEM_SPEC] * 8,
        out_specs=[VMEM_SPEC] * 8,
        scratch_shapes=[
            pltpu.VMEM((frame_count, width), BF),
            pltpu.VMEM((frame_count, hidden), BF),
            pltpu.VMEM((frame_count, hidden), BF),
            pltpu.VMEM((frame_count, width), BF),
            pltpu.VMEM((frame_count, width), BF),
        ],
        compiler_params=pltpu.CompilerParams(vmem_limit_bytes=VMEM_LIMIT),
        name="feed_forward_both",
    )(lengths, middle, gout, mixed, wup, wdn, wo, vec, bup)


def attend_back_kernel(
    x,
    gmid,
    nb,
    qaug,
    kk,
    vv,
    mixed,
    dmixed,
    kaug,
    wq,
    wk,
    wv,
    vec,
    grad_x,
    dwq,
    dwk,
    dwv,
    sums,
    dq,
    dqb,
    dkt,
    dvt,
    *,
    ub,
    lb,
):
    frame_count = x.shape[0]
    lane = lax.broadcasted_iota(jnp.int32, (1, 128), 1)
    gain = vec[...].astype(F32).T[0:1]

    def pair_step(p, carry):
        cols = rows(p * 128, 128)
        grad_pair = dmixed[:, cols]
        product = grad_pair.astype(F32) * mixed[:, cols].astype(F32)
        for half in range(2):
            own = own_lanes(lane, half)
            base = 64 - 64 * half
            delta = jnp.sum(jnp.where(own, product, 0.0), axis=1, keepdims=True)
            high, mid, low = three_pieces(-delta)
            grad = jnp.where(own, grad_pair, jnp.zeros((1, 128), BF))
            grad = jnp.where(lane == base + 3, high, grad)
            grad = jnp.where(lane == base + 4, mid, grad)
            grad = jnp.where(lane == base + 5, low, grad)
            query = qaug[:, pl.ds(pl.multiple_of((2 * p + half) * 128, 128), 128)]
            here = pl.ds(pl.multiple_of(p * 128 + 64 * half, 64), 64)
            part = slice(64 * half, 64 * half + 64)
            ones = jnp.where(
                (lane >= base + 3) & (lane < base + 6), jnp.ones((1, 128), F32), 0.0
            ).astype(BF)

            def block(i, inner):
                r = rows(i * ub, ub)
                key = jnp.where(own, kk[r, cols], kaug[r, :])
                value = jnp.where(own, vv[r, cols], ones)
                probs = jnp.exp(dot_nt(query, key))
                low_probs = probs.astype(BF)
                gs = (probs * dot_nt(grad, value)).astype(BF)
                dvt[here, r] = dot_tn(grad, low_probs)[part].astype(BF)
                dkt[here, r] = dot_tn(query, gs)[part].astype(BF)
                step = dot_nn(gs, kk[r, cols])
                if i == 0:
                    dq[...] = step
                else:
                    dq[...] += step
                return inner

            for i in range(frame_count // ub):
                block(i, 0)
            done = (dq[...] * 0.125).astype(BF)
            if half == 0:
                dqb[:, cols] = done
            else:
                dqb[:, cols] = jnp.where(own, done, dqb[:, cols])
        return carry

    lax.fori_loop(0, HEADS // 2, pair_step, 0)
    sums[...] = jnp.zeros_like(sums)

    def finish(i, carry):
        r = rows(i * lb, lb)
        gn = dot_nn(dqb[r, :], wq[...]) + dot_tn(dkt[:, r], wk[...]) + dot_tn(dvt[:, r], wv[...])
        xhat, inv = normal_stats(x[r, :].astype(F32))
        scaled = gn * gain
        grad_x[r, :] = (
            gmid[r, :]
            + inv
            * (
                scaled
                - jnp.mean(scaled, axis=-1, keepdims=True)
                - xhat * jnp.mean(scaled * xhat, axis=-1, keepdims=True)
            )
        ).astype(BF)
        sums[0:1, :] += jnp.sum(gn * xhat, axis=0, keepdims=True)
        sums[1:2, :] += jnp.sum(gn, axis=0, keepdims=True)
        sums[2:3, :] += jnp.sum(dqb[r, :].astype(F32), axis=0, keepdims=True)
        return carry

    lax.fori_loop(0, frame_count // lb, finish, 0)
    sums[3:4, :] = dot_nt(jnp.ones((8, frame_count), BF), dvt[...])[0:1]
    dwq[...] = dot_tn(dqb[...], nb[...]).astype(BF)
    dwk[...] = dot_nn(dkt[...], nb[...]).astype(BF)
    dwv[...] = dot_nn(dvt[...], nb[...]).astype(BF)


def attend_back(x, gmid, nb, qaug, kk, vv, mixed, dmixed, kaug, wq, wk, wv, vec):
    frame_count, width = x.shape
    square = jax.ShapeDtypeStruct((width, width), BF)
    return pl.pallas_call(
        functools.partial(attend_back_kernel, ub=512, lb=512),
        out_shape=[
            jax.ShapeDtypeStruct((frame_count, width), BF),
            square,
            square,
            square,
            jax.ShapeDtypeStruct((8, width), F32),
        ],
        in_specs=[VMEM_SPEC] * 13,
        out_specs=[VMEM_SPEC] * 5,
        scratch_shapes=[
            pltpu.VMEM((frame_count, 128), F32),
            pltpu.VMEM((frame_count, width), BF),
            pltpu.VMEM((width, frame_count), BF),
            pltpu.VMEM((width, frame_count), BF),
        ],
        compiler_params=pltpu.CompilerParams(vmem_limit_bytes=VMEM_LIMIT),
        name="attend_backward",
    )(x, gmid, nb, qaug, kk, vv, mixed, dmixed, kaug, wq, wk, wv, vec)


def bits_differ(a, b, size):
    total, bit = 0, 1
    while bit < size:
        total = total + bit * lax.rem(a // bit + b // bit, 2)
        bit *= 2
    return total


def remote(src, dst, send, recv, device):
    return pltpu.make_async_remote_copy(
        src_ref=src,
        dst_ref=dst,
        send_sem=send,
        recv_sem=recv,
        device_id=(device,),
        device_id_type=MESH,
    )


def spread_rows(blocks, share, width):
    count, height, lanes = blocks.shape
    source = lax.broadcasted_iota(jnp.int32, (lanes, width), 0)
    target = lax.broadcasted_iota(jnp.int32, (lanes, width), 1)
    pick = jnp.where(source == lax.rem(target, share), 1.0, 0.0).astype(BF)
    spread = dot_nn(blocks.reshape(count * height, lanes).astype(BF), pick)
    owner = lax.broadcasted_iota(jnp.int32, (count, height, width), 0)
    place = lax.broadcasted_iota(jnp.int32, (count, height, width), 2)
    spread = spread.reshape(count, height, width)
    return jnp.sum(jnp.where(owner == place // share, spread, 0.0), axis=0)


SECOND_DUTIES = ((0, 0, 3), (1, 0, 1), (3, 1, 2), (5, 1, 3), (6, 1, 1))


def gather_attend_kernel(n, tb, lb, *refs):
    (lengths, x, sq, sk, sv, so, su, sd) = refs[:8]
    vectors, refs = refs[8:17], refs[17:]
    (wq_h, wk_h, wv_h, wo_h, wup, wdn, table, bup, qq_h, kk_h, vv_h, raised_h, part_h) = refs[:13]
    (nb_h, mixed_h, middle_h) = refs[13:16]
    (xhat, nb, mixed, middle, kaug, qbuf, kbuf, vbuf, stage, part, svec, vec) = refs[16:28]
    (own_sem, near_s, near_r, core_s, core_r, far_s, far_r, fwd_s, fwd_r) = refs[28:37]
    (bown_sem, bfar_s, bfar_r, bnear_s, bnear_r, bcore_s, bcore_r, out_sem, end_sem) = refs[37:46]
    stage_sem, whole_sem, middle_sem, wq, wk, wv, wo = refs[46:]
    far, near = levels_of(n)
    share = 512 // n
    frame_count, width = x.shape
    pairs = HEADS // 2
    me = lax.axis_index("dp")
    top, mid, core = announce(n, me, far, near)
    lane = lax.broadcasted_iota(jnp.int32, (1, 128), 1)
    svec[...] = jnp.zeros_like(svec)
    for v, vector in enumerate(vectors):
        length = vector.shape[0]
        svec[v : v + 1, :length] = vector[...].reshape(1, length)

    def index(t, m, c):
        return (t * near + m) * 2 + c

    sibling = index(top, mid, 1 - core)
    first = list(zip((sq, sk, sv), (wq, wk, wv)))
    second = list(zip((svec, so, su, sd), (vec, wo, wup, wdn)))

    def near_copy(a, k):
        peer = index(top, lax.rem(mid + k, near), core)
        src, dst = first[a]
        return remote(src, dst.at[top, mid, core], near_s.at[a, k - 1], near_r.at[a, k - 1], peer)

    def core_copy(a):
        ref = first[a][1].at[top, :, core]
        return remote(ref, ref, core_s.at[a], core_r.at[a], sibling)

    def far_copy(a, k):
        ref = first[a][1].at[top, :, core]
        peer = index(bits_differ(top, k, far), mid, core)
        return remote(ref, ref, far_s.at[a, k - 1], far_r.at[a, k - 1], peer)

    def fwd_copy(a, k):
        ref = first[a][1].at[bits_differ(top, k, far), :, core]
        return remote(ref, ref, fwd_s.at[a, k - 1], fwd_r.at[a, k - 1], sibling)

    def bfar_copy(a, k):
        src, dst = second[a]
        peer = index(bits_differ(top, k, far), mid, core)
        return remote(src, dst.at[top, mid, core], bfar_s.at[a, k - 1], bfar_r.at[a, k - 1], peer)

    def bnear_copy(a, k):
        ref = second[a][1].at[:, mid, core]
        peer = index(top, lax.rem(mid + k, near), core)
        return remote(ref, ref, bnear_s.at[a, k - 1], bnear_r.at[a, k - 1], peer)

    def bcore_copy(a):
        ref = second[a][1].at[:, :, core]
        return remote(ref, ref, bcore_s.at[a], bcore_r.at[a], sibling)

    def own_copy(a):
        src, dst = first[a]
        return pltpu.make_async_copy(src, dst.at[top, mid, core], own_sem.at[a])

    def bown_copy(a):
        src, dst = second[a]
        return pltpu.make_async_copy(src, dst.at[top, mid, core], bown_sem.at[a])

    def stats(i, carry):
        r = rows(i * lb, lb)
        xhat[r, :] = normal_stats(x[r, :].astype(F32))[0]
        part[r, :] = jnp.zeros((lb, 128), F32)
        position = lax.broadcasted_iota(jnp.int32, (lb, 128), 0) + i * lb
        lanes = lax.broadcasted_iota(jnp.int32, (lb, 128), 1)
        same = segment_lanes(lengths, position, lanes)
        slot = lax.rem(lanes, 64)
        kaug[r, :] = jnp.where(
            slot < 3, jnp.where(same, 0.0, EXCLUDED), jnp.where(slot < 6, 1.0, 0.0)
        ).astype(BF)
        return carry

    lax.fori_loop(0, frame_count // lb, stats, 0)
    await_peers(far, near)
    for k in range(1, far):
        bfar_copy(0, k).start()
    bown_copy(0).start()
    for a in range(3):
        for k in range(1, near):
            near_copy(a, k).start()
        own_copy(a).start()
    for a in (2, 3, 1):
        for k in range(1, far):
            bfar_copy(a, k).start()
        bown_copy(a).start()

    bown_copy(0).wait()
    for k in range(1, far):
        bfar_copy(0, k).wait_recv()
    for k in range(1, near):
        bnear_copy(0, k).start()
    for a in range(3):
        own_copy(a).wait()
        for k in range(1, near):
            near_copy(a, k).wait_recv()
        core_copy(a).start()
    for k in range(1, near):
        bnear_copy(0, k).wait_recv()
    bcore_copy(0).start()
    for k in range(1, far):
        for a in range(3):
            far_copy(a, k).start()
    bcore_copy(0).wait_recv()
    blocks = vec[...].reshape(n, 16, 128)
    table[...] = spread_rows(blocks, share, width)
    gain, shift = table[0:1, :], table[1:2, :]

    def norm(i, carry):
        r = rows(i * lb, lb)
        nb[r, :] = (xhat[r, :] * gain + shift).astype(BF)
        return carry

    lax.fori_loop(0, frame_count // lb, norm, 0)
    nb_copy = pltpu.make_async_copy(nb, nb_h, end_sem.at[0])
    nb_copy.start()
    for a in range(3):
        core_copy(a).wait_recv()

    def second_near(a):
        bown_copy(a).wait()
        for k in range(1, far):
            bfar_copy(a, k).wait_recv()
        for k in range(1, near):
            bnear_copy(a, k).start()

    def second_core(a):
        for k in range(1, near):
            bnear_copy(a, k).wait_recv()
        bcore_copy(a).start()

    second_near(2)

    def out_copies(p, slot):
        cols = rows(p * 128, 128)
        return [
            pltpu.make_async_copy(buf.at[slot], out.at[:, cols], out_sem.at[slot, a])
            for a, (buf, out) in enumerate(((qbuf, qq_h), (kbuf, kk_h), (vbuf, vv_h)))
        ]

    def stage_copies(p, half):
        return [
            pltpu.make_async_copy(
                stage.at[half, j, :, pl.ds(b * tb, tb)],
                raised_h.at[2 * p + half, b, pl.ds(j * tb, tb)],
                stage_sem.at[half, j, b],
            )
            for j in range(frame_count // tb)
            for b in range(frame_count // tb)
        ]

    def pair_step(i, carry):
        p = bits_differ(top, i, far)
        slot = lax.rem(i, 2)
        cols = rows(p * 128, 128)

        @pl.when(i > 0)
        def _():
            for a in range(3):
                fwd_copy(a, i).wait_recv()

        @pl.when(i > 1)
        def _():
            for copy in out_copies(bits_differ(top, i - 2, far), slot):
                copy.wait()

        weights = jnp.concatenate(
            [w[p].reshape(128, width) for w in (wq, wk, wv)], axis=0
        )
        bq, bv = table[2:3, cols], table[3:4, cols]

        def project(j, inner):
            r = rows(j * lb, lb)
            got = dot_nt(nb[r, :], weights)
            qbuf[slot, r, :] = ((got[:, :128] + bq).astype(BF).astype(F32) * 0.125).astype(BF)
            kbuf[slot, r, :] = got[:, 128:256].astype(BF)
            vbuf[slot, r, :] = (got[:, 256:] + bv).astype(BF)
            return inner

        lax.fori_loop(0, frame_count // lb, project, 0)
        for half in range(2):
            own = own_lanes(lane, half)
            base = 64 - 64 * half
            key = jnp.where(own, kbuf[slot], kaug[...])
            value = jnp.where(own, vbuf[slot], jnp.ones((1, 128), BF))

            @pl.when(i > 0)
            def _():
                for copy in stage_copies(bits_differ(top, i - 1, far), half):
                    copy.wait()

            def block(j):
                r = pl.ds(j * tb, tb)
                position = lax.broadcasted_iota(jnp.int32, (tb, 128), 0) + j * tb
                lanes = lax.broadcasted_iota(jnp.int32, (tb, 128), 1)
                mark = jnp.where(segment_lanes(lengths, position, lanes), 1.0, 0.0).astype(BF)
                query = jnp.where(own, qbuf[slot, r, :], mark)
                scores = dot_nt(query, key)
                peak = jnp.max(scores, axis=1, keepdims=True)
                raised = jnp.exp(scores - peak).astype(BF)
                stage[half, j] = raised
                got = dot_nn(raised, value)
                inverse = 1.0 / got[:, base : base + 1]
                part[r, :] = jnp.where(lane == 2 * p + half, inverse, part[r, :])
                got = (got * inverse).astype(BF)
                if half == 0:
                    mixed[r, cols] = got
                else:
                    mixed[r, cols] = jnp.where(own, got, mixed[r, cols])
            for j in range(frame_count // tb):
                block(j)
            for copy in stage_copies(p, half):
                copy.start()
            if half == 0:

                @pl.when(i < far - 1)
                def _():
                    for a in range(3):
                        far_copy(a, i + 1).wait_recv()
                        fwd_copy(a, i + 1).start()

            for step, duty, a in SECOND_DUTIES:
                if step % 2 == half:
                    act = second_near if duty == 0 else second_core
                    pl.when(i == step // 2)(functools.partial(act, a))

        for copy in out_copies(p, slot):
            copy.start()
        return carry

    lax.fori_loop(0, pairs, pair_step, 0)
    mixed_copy = pltpu.make_async_copy(mixed, mixed_h, end_sem.at[1])
    mixed_copy.start()
    part_copy = pltpu.make_async_copy(part, part_h, end_sem.at[3])
    part_copy.start()
    bcore_copy(1).wait_recv()
    whole_copies = [
        pltpu.make_async_copy(src, dst, whole_sem.at[a])
        for a, (src, dst) in enumerate(((wq, wq_h), (wk, wk_h), (wv, wv_h), (wo, wo_h)))
    ]
    for copy in whole_copies:
        copy.start()

    def middle_copy(i):
        r = rows(i * lb, lb)
        return pltpu.make_async_copy(middle.at[r], middle_h.at[r], middle_sem.at[i])

    out_weight = wo[...].reshape(width, width)
    bo = table[4:5, :]
    bup[...] = spread_rows(vec[...].reshape(n, 16, 128)[:, 8:16], 4 * share, 4 * width)

    def finish(i, carry):
        r = rows(i * lb, lb)
        middle[r, :] = x[r, :].astype(F32) + (dot_nt(mixed[r, :], out_weight) + bo)
        middle_copy(i).start()
        return carry

    lax.fori_loop(0, frame_count // lb, finish, 0)
    for i in (pairs - 2, pairs - 1):
        for copy in out_copies(bits_differ(top, i, far), i % 2):
            copy.wait()
    for half in range(2):
        for copy in stage_copies(bits_differ(top, pairs - 1, far), half):
            copy.wait()
    part_copy.wait()
    nb_copy.wait()
    mixed_copy.wait()
    for a in range(3):
        for k in range(1, near):
            near_copy(a, k).wait_send()
        core_copy(a).wait_send()
        for k in range(1, far):
            far_copy(a, k).wait_send()
            fwd_copy(a, k).wait_send()
    bcore_copy(2).wait_recv()
    bcore_copy(3).wait_recv()
    for a in range(4):
        for k in range(1, far):
            bfar_copy(a, k).wait_send()
        for k in range(1, near):
            bnear_copy(a, k).wait_send()
        bcore_copy(a).wait_send()
    for copy in whole_copies:
        copy.wait()
    for i in range(frame_count // lb):
        middle_copy(i).wait()


def gather_attend(n, lengths, x, shards, vectors):
    far, near = levels_of(n)
    frame_count, width = x.shape
    lead = (far, near, 2)
    share = width // n
    square = jax.ShapeDtypeStruct(lead + (share, width), BF)
    low = jax.ShapeDtypeStruct((frame_count, width), BF)
    dma = pltpu.SemaphoreType.DMA
    tb = 512
    return pl.pallas_call(
        functools.partial(gather_attend_kernel, n, tb, 512),
        out_shape=[
            square,
            square,
            square,
            square,
            jax.ShapeDtypeStruct(lead + (4 * share, width), BF),
            jax.ShapeDtypeStruct(lead + (share, 4 * width), BF),
            jax.ShapeDtypeStruct((16, width), F32),
            jax.ShapeDtypeStruct((8, 4 * width), F32),
            low,
            low,
            low,
            jax.ShapeDtypeStruct((HEADS, frame_count // tb, frame_count, tb), BF),
            jax.ShapeDtypeStruct((frame_count, 128), F32),
            low,
            low,
            jax.ShapeDtypeStruct((frame_count, width), F32),
        ],
        in_specs=[SMEM_SPEC, VMEM_SPEC] + [HBM_SPEC] * 6 + [VMEM_SPEC] * 9,
        out_specs=[HBM_SPEC] * 6 + [VMEM_SPEC] * 2 + [HBM_SPEC] * 8,
        scratch_shapes=[
            pltpu.VMEM((frame_count, width), F32),
            pltpu.VMEM((frame_count, width), BF),
            pltpu.VMEM((frame_count, width), BF),
            pltpu.VMEM((frame_count, width), F32),
            pltpu.VMEM((frame_count, 128), BF),
            pltpu.VMEM((2, frame_count, 128), BF),
            pltpu.VMEM((2, frame_count, 128), BF),
            pltpu.VMEM((2, frame_count, 128), BF),
            pltpu.VMEM((2, frame_count // tb, tb, frame_count), BF),
            pltpu.VMEM((frame_count, 128), F32),
            pltpu.VMEM((16, 128), BF),
            pltpu.VMEM(lead + (16, 128), BF),
            dma((3,)),
            dma((3, near - 1)),
            dma((3, near - 1)),
            dma((3,)),
            dma((3,)),
            dma((3, far - 1)),
            dma((3, far - 1)),
            dma((3, far - 1)),
            dma((3, far - 1)),
            dma((4,)),
            dma((4, far - 1)),
            dma((4, far - 1)),
            dma((4, near - 1)),
            dma((4, near - 1)),
            dma((4,)),
            dma((4,)),
            dma((2, 3)),
            dma((4,)),
            dma((2, frame_count // tb, frame_count // tb)),
            dma((4,)),
            dma((frame_count // tb,)),
        ]
        + [pltpu.VMEM(square.shape, BF)] * 4,
        compiler_params=pltpu.CompilerParams(
            collective_id=2, has_side_effects=True, vmem_limit_bytes=VMEM_LIMIT
        ),
        name="gather_attend",
    )(lengths, x, *shards, *vectors)


def both_back_kernel(n, tb, ub, lb, *refs):
    (lengths, middle_h, gout_h, mixed_h, wo_h, wup_h, wdn_h, x_h, nb_h) = refs[:9]
    (qq_h, kk_h, vv_h, raised_h, wq_h, wk_h, wv_h, part, table, bup) = refs[9:19]
    (layer_h, grad_h, gq, gk, gv, go, gu, gd, gc) = refs[19:28]
    (wide, nb, x, grad, gmid, mixed, heads, layer, wo, wup, wdn, held) = refs[28:40]
    dmixed, refs = refs[40], refs[:40] + refs[41:]
    (qbuf, kbuf, vbuf, dqt, turned, sums, sum_up, biases) = refs[40:48]
    refs = refs[:48] + (None,) + refs[48:]
    (parts, core_in, core_sum, near_in, near_sum, far_in) = refs[49:55]
    (core_in2, near_in2, near_sum2, far_in2) = (refs[55 + 3 * j : 58 + 3 * j] for j in range(4))
    (cparts, ccore_in, ccore_sum, cnear_in, cnear_sum, cfar_in) = refs[67:73]
    (row_sem, weight_sem, in_sem, end_sem, raised_sem, held_sem) = refs[73:79]
    refs = refs[:78] + refs[79:]
    (core_s, core_r, near_s, near_r, far_s, far_r) = refs[78:84]
    (core2_s, core2_r, near2_s, near2_r, far2_s, far2_r) = refs[84:90]
    (ccore_s, ccore_r, cnear_s, cnear_r, cfar_s, cfar_r) = refs[90:]
    normed, glow, gbl = nb, x, grad
    far, near = levels_of(n)
    frame_count, width = gmid.shape
    hidden = 4 * width
    share = width // n
    pairs = HEADS // 2
    last = pairs - 1
    me = lax.axis_index("dp")
    top, mid, core = announce(n, me, far, near)
    lane = lax.broadcasted_iota(jnp.int32, (1, 128), 1)
    finish_row = lengths[0, 0] + lengths[0, 1]

    def index(t, m, c):
        return (t * near + m) * 2 + c

    sibling = index(top, mid, 1 - core)
    big = (wo, wup, wdn)

    def row_copies(i):
        r = rows(i * tb, tb)
        return [
            pltpu.make_async_copy(middle_h.at[r], gmid.at[r], row_sem.at[i, 0]),
            pltpu.make_async_copy(gout_h.at[r], glow.at[r], row_sem.at[i, 1]),
            pltpu.make_async_copy(mixed_h.at[r], mixed.at[r], row_sem.at[i, 3]),
        ]

    def layer_copy(i):
        r = rows(i * tb, tb)
        return pltpu.make_async_copy(layer.at[r], layer_h.at[r], row_sem.at[i, 2])

    weight_copies = [
        pltpu.make_async_copy(src, dst, weight_sem.at[a])
        for a, (src, dst) in enumerate(
            ((wup_h, wup), (wdn_h, wdn), (wo_h, wo))
        )
    ]
    held_copies = [
        pltpu.make_async_copy(w, held.at[:, a], held_sem.at[a])
        for a, w in enumerate((wq_h, wk_h, wv_h))
    ]
    nb_copy = pltpu.make_async_copy(nb_h, nb, end_sem.at[2])
    for copy in row_copies(0) + weight_copies:
        copy.start()
    for i in range(1, frame_count // tb):
        for copy in row_copies(i):
            copy.start()
    for copy in held_copies:
        copy.start()

    def core2_copy(a):
        return remote(
            big[a].at[:, :, 1 - core], core_in2[a], core2_s.at[a], core2_r.at[a], sibling
        )

    def near2_copy(a, k):
        peer = lax.rem(mid + k, near)
        return remote(
            big[a].at[:, peer, core],
            near_in2[a].at[k - 1],
            near2_s.at[a, k - 1],
            near2_r.at[a, k - 1],
            index(top, peer, core),
        )

    def far2_copy(a, k):
        peer = bits_differ(top, k, far)
        return remote(
            near_sum2[a].at[peer],
            far_in2[a].at[k - 1],
            far2_s.at[a, k - 1],
            far2_r.at[a, k - 1],
            index(peer, mid, core),
        )

    def second_near(a):
        core2_copy(a).wait_recv()

        def add(f, inner):
            big[a][f, :, core] = (
                big[a][f, :, core].astype(F32) + core_in2[a][f].astype(F32)
            ).astype(BF)
            return inner

        lax.fori_loop(0, far, add, 0)
        for k in range(1, near):
            near2_copy(a, k).start()

    def second_far(a):
        for k in range(1, near):
            near2_copy(a, k).wait_recv()

        def add(f, inner):
            total = big[a][f, mid, core].astype(F32)
            for k in range(near - 1):
                total = total + near_in2[a][k, f].astype(F32)
            near_sum2[a][f] = total.astype(BF)
            return inner

        lax.fori_loop(0, far, add, 0)
        for k in range(1, far):
            far2_copy(a, k).start()

    def core_copy(j):
        return remote(
            parts.at[j, :, :, 1 - core], core_in.at[j], core_s.at[j], core_r.at[j], sibling
        )

    def near_copy(j, k):
        peer = lax.rem(mid + k, near)
        return remote(
            core_sum.at[j, peer],
            near_in.at[j, k - 1],
            near_s.at[j, k - 1],
            near_r.at[j, k - 1],
            index(top, peer, core),
        )

    def far_copy(j):
        peer = index(bits_differ(top, last - j, far), mid, core)
        return remote(near_sum.at[j], far_in.at[j], far_s.at[j], far_r.at[j], peer)

    def add_core(j):
        for m in range(near):
            core_sum[j, m] = (
                parts[j, :, m, core].astype(F32) + core_in[j, :, m].astype(F32)
            ).astype(BF)

    def add_near(j):
        total = core_sum[j, mid].astype(F32)
        for k in range(near - 1):
            total = total + near_in[j, k].astype(F32)
        return total

    def pair_near(j):
        core_copy(j).wait_recv()
        add_core(j)
        for k in range(1, near):
            near_copy(j, k).start()

    def pair_far(j):
        for k in range(1, near):
            near_copy(j, k).wait_recv()
        near_sum[j] = add_near(j).astype(BF)
        far_copy(j).start()

    def in_copies(p, slot):
        cols = rows(p * 128, 128)
        return [
            pltpu.make_async_copy(src.at[:, cols], buf.at[slot], in_sem.at[slot, a])
            for a, (src, buf) in enumerate(((qq_h, qbuf), (kk_h, kbuf), (vv_h, vbuf)))
        ]

    def raised_copies(p, half):
        return [
            pltpu.make_async_copy(
                raised_h.at[2 * p + half, j], wide.at[3 * half + j], raised_sem.at[half, j]
            )
            for j in range(frame_count // ub)
        ]

    gain2, shift2, bdn = (table[i : i + 1, :] for i in range(5, 8))
    sums[...] = jnp.zeros_like(sums)
    sum_up[...] = jnp.zeros_like(sum_up)
    for copy in weight_copies:
        copy.wait()

    def build_heads(i):
        r = rows(i * tb, tb)
        for p in range(pairs):
            cols = slice(128 * p, 128 * p + 128)
            inverse = jnp.where(
                lane < 64, part[r, 2 * p : 2 * p + 1], part[r, 2 * p + 1 : 2 * p + 2]
            )
            scaled = (dmixed[:, cols].astype(F32) * inverse).astype(BF).astype(F32)
            product = scaled * mixed[r, cols].astype(F32)
            for half in range(2):
                own = own_lanes(lane, half)
                base = 64 - 64 * half
                delta = jnp.sum(jnp.where(own, -product, 0.0), axis=1, keepdims=True)
                rest = delta - delta.astype(BF).astype(F32)
                head = jnp.where(own, scaled, 0.0)
                head = jnp.where(lane == base + 3, delta, head)
                head = jnp.where(lane == base + 4, rest, head)
                at = 256 * p + 128 * half
                heads[r, at : at + 128] = head.astype(BF)

    def block(i, carry):
        r = rows(i * tb, tb)
        for copy in row_copies(i):
            copy.wait()
        build_heads(jnp.maximum(i - 1, 0))
        up_rows, down_rows = wup[...].reshape(hidden, width), wdn[...].reshape(width, hidden)
        valid = lax.broadcasted_iota(jnp.int32, (tb, 1), 0) + i * tb < finish_row
        row = gmid[r, :]
        xhat, inv = normal_stats(row)
        normed_rows = (xhat * gain2 + shift2).astype(BF)
        normed[r, :] = normed_rows
        up = dot_nt(normed_rows, up_rows) + bup[0:1, :]
        cdf = 0.5 * (1.0 + lax.erf(up * (1.0 / math.sqrt(2.0))))
        low = (up * cdf).astype(BF)
        for c in range(4):
            wide[c, r, :] = low[:, 512 * c : 512 * c + 512]
        down = dot_nt(low, down_rows) + bdn
        layer[r, :] = jnp.where(valid, row + down, 0.0).astype(BF)
        layer_copy(i).start()
        grow = jnp.where(valid, glow[r, :].astype(F32), 0.0)
        gl = grow.astype(BF)
        glow[r, :] = gl
        slope = cdf + up * jnp.exp(-0.5 * up * up) * (1.0 / math.sqrt(2.0 * math.pi))
        gu = (dot_nn(gl, down_rows) * slope).astype(BF)
        for c in range(4):
            wide[4 + c, r, :] = gu[:, 512 * c : 512 * c + 512]
        gn = dot_nn(gu, up_rows)
        scaled = gn * gain2
        gm = grow + inv * (
            scaled
            - jnp.mean(scaled, axis=-1, keepdims=True)
            - xhat * jnp.mean(scaled * xhat, axis=-1, keepdims=True)
        )
        gmid[r, :] = gm
        gb = gm.astype(BF)
        gbl[r, :] = gb
        dmixed[...] = dot_nn(gb, wo[...].reshape(width, width)).astype(BF)
        sums[4:5, :] += jnp.sum(gb.astype(F32), axis=0, keepdims=True)
        sums[5:6, :] += jnp.sum(gn * xhat, axis=0, keepdims=True)
        sums[6:7, :] += jnp.sum(gn, axis=0, keepdims=True)
        sums[7:8, :] += jnp.sum(grow, axis=0, keepdims=True)
        sum_up[0:1, :] += jnp.sum(gu.astype(F32), axis=0, keepdims=True)
        return carry

    dmixed[...] = jnp.zeros_like(dmixed)
    lax.fori_loop(0, frame_count // tb, block, 0)
    build_heads(frame_count // tb - 1)
    wo[...] = dot_tn(gbl[...], mixed[...]).astype(BF).reshape(wo.shape)
    await_peers(far, near)
    core2_copy(0).start()

    def down_part(c, carry):
        got = dot_tn(glow[...], wide[c]).astype(BF)
        wdn[:, :, :, :, rows(c * 512, 512)] = got.reshape(far, near, 2, share, 512)
        return carry

    lax.fori_loop(0, 4, down_part, 0)
    core2_copy(2).start()
    x_copy = pltpu.make_async_copy(x_h, x, end_sem.at[0])
    x_copy.start()
    for copy in raised_copies(bits_differ(top, last, far), 0):
        copy.start()
    for copy in in_copies(bits_differ(top, last, far), 0):
        copy.start()
    second_near(0)

    def up_part(c, carry):
        wup[c] = dot_tn(wide[4 + c], normed[...]).astype(BF).reshape(near, 2, 4 * share, width)
        return carry

    lax.fori_loop(0, 4, up_part, 0)
    core2_copy(1).start()
    nb_copy.start()
    for copy in raised_copies(bits_differ(top, last, far), 1):
        copy.start()
    plain = sums[...].T
    pieces = sum_up[...].T.reshape(n, 4, share, 8)
    found = jnp.zeros((width, 128), F32)
    for v in range(4, 8):
        found = jnp.where(lane == v, plain[:, v : v + 1], found)
    for k in range(4):
        found = jnp.where(lane == 8 + k, pieces[:, k].reshape(width, 8)[:, 0:1], found)
    biases[...] = found
    second_near(2)
    for copy in held_copies:
        copy.wait()
    nb_copy.wait()

    def pair_step(i, carry):
        p = bits_differ(top, last - i, far)
        slot = lax.rem(i, 2)
        cols = rows(p * 128, 128)
        for copy in in_copies(p, slot):
            copy.wait()

        @pl.when(i < last)
        def _():
            for copy in in_copies(bits_differ(top, last - i - 1, far), 1 - slot):
                copy.start()

        turned_query = qbuf[slot].T
        turned_key = kbuf[slot].T
        for half in range(2):
            own = own_lanes(lane, half)
            base = 64 - 64 * half
            for copy in raised_copies(p, half):
                copy.wait()
            grad_head = heads[:, rows((2 * p + half) * 128, 128)]
            turned_grad = grad_head.T
            part_rows = slice(64 * half, 64 * half + 64)
            ones = jnp.where(
                (lane >= base + 3) & (lane < base + 5), jnp.ones((1, 128), F32), 0.0
            ).astype(BF)
            for j in range(frame_count // ub):
                r = pl.ds(j * ub, ub)
                value = jnp.where(own, vbuf[slot, r, :], ones)
                weights = wide[3 * half + j]
                gs = (weights.astype(F32) * dot_nt(grad_head, value)).astype(BF)
                turned[p, 2, part_rows, r] = dot_nn(turned_grad, weights)[part_rows].astype(BF)
                turned[p, 1, part_rows, r] = dot_nn(turned_query, gs)[part_rows].astype(BF)
                step = dot_nn(turned_key[:, j * ub : j * ub + ub], gs.T)[part_rows]
                if j == 0:
                    dqt[...] = step
                else:
                    dqt[...] += step
            turned[p, 0, part_rows, :] = (dqt[...] * 0.125).astype(BF)

            @pl.when(i < last)
            def _():
                for copy in raised_copies(bits_differ(top, last - i - 1, far), half):
                    copy.start()

            if half == 0:
                pl.when(i == 0)(functools.partial(second_near, 1))
                pl.when(i > 0)(functools.partial(pair_near, i - 1))
                pl.when(i == last)(functools.partial(pair_far, 0))
            else:
                for step_index, a in ((0, 0), (1, 2), (2, 1)):
                    pl.when(i == step_index)(functools.partial(second_far, a))
                pl.when(i == last)(functools.partial(pair_far, 1))

        pair_rows = rows(p * 128, 128)
        shape = (near, 2, share, width)
        found = dot_nn(turned[p].reshape(3 * 128, frame_count), nb[...])
        found = [found[128 * a : 128 * a + 128] for a in range(3)]
        for a in range(3):
            parts[i, a] = found[a].astype(BF).reshape(shape)
        core_copy(i).start()
        column = [
            jnp.sum(turned[p, a].astype(F32), axis=1, keepdims=True) for a in range(3)
        ]
        own_weights = [held[p, a].reshape(128, width).astype(F32) for a in range(3)]
        with_rows = sum(g * w for g, w in zip(found, own_weights))
        alone = sum(c * w for c, w in zip(column, own_weights))
        sums[0:1, :] += jnp.sum(with_rows, axis=0, keepdims=True)
        sums[1:2, :] += jnp.sum(alone, axis=0, keepdims=True)
        biases[pair_rows, :] = jnp.where(
            lane == 2, column[0], jnp.where(lane == 3, column[2], biases[pair_rows, :])
        )
        return carry

    sums[...] = jnp.zeros_like(sums)
    lax.fori_loop(0, pairs, pair_step, 0)

    gain, shift = table[0:1, :], table[1:2, :]
    sums[0:1, :] = (sums[0:1, :] - shift * sums[1:2, :]) / gain
    plain = sums[...].T
    found = jnp.where(lane == 0, plain[:, 0:1], biases[...])
    found = jnp.where(lane == 1, plain[:, 1:2], found)
    cparts[...] = found.astype(BF).reshape(far, near, 2, share, 128)
    ccore = remote(cparts.at[:, :, 1 - core], ccore_in, ccore_s, ccore_r, sibling)
    ccore.start()
    pair_near(last)
    pair_far(last - 1)
    cnear, cfar = [], []
    for k in range(1, near):
        peer = lax.rem(mid + k, near)
        cnear.append(
            remote(
                ccore_sum.at[peer],
                cnear_in.at[k - 1],
                cnear_s.at[k - 1],
                cnear_r.at[k - 1],
                index(top, peer, core),
            )
        )
    for k in range(1, far):
        peer = bits_differ(top, k, far)
        cfar.append(
            remote(
                cnear_sum.at[peer],
                cfar_in.at[k - 1],
                cfar_s.at[k - 1],
                cfar_r.at[k - 1],
                index(peer, mid, core),
            )
        )
    x_copy.wait()

    def finish(i, carry):
        r = rows(i * lb, lb)
        gn = dot_tn(
            turned[:, :, :, r].reshape(3 * width, lb), held[...].reshape(3 * width, width)
        )
        xhat, inv = normal_stats(x[r, :].astype(F32))
        scaled = gn * gain
        grad[r, :] = (
            gmid[r, :]
            + inv
            * (
                scaled
                - jnp.mean(scaled, axis=-1, keepdims=True)
                - xhat * jnp.mean(scaled * xhat, axis=-1, keepdims=True)
            )
        ).astype(BF)

        @pl.when(i == 0)
        def _():
            ccore.wait_recv()
            for m in range(near):
                ccore_sum[m] = (
                    cparts[:, m, core].astype(F32) + ccore_in[:, m].astype(F32)
                ).astype(BF)
            for copy in cnear:
                copy.start()

        @pl.when(i == 1)
        def _():
            for copy in cnear:
                copy.wait_recv()
            total = ccore_sum[mid].astype(F32)
            for k in range(near - 1):
                total = total + cnear_in[k].astype(F32)
            cnear_sum[...] = total.astype(BF)
            for copy in cfar:
                copy.start()

        return carry

    lax.fori_loop(0, frame_count // lb, finish, 0)
    grad_copy = pltpu.make_async_copy(grad, grad_h, end_sem.at[1])
    grad_copy.start()
    for k in range(1, near):
        near_copy(last, k).wait_recv()
    total = add_near(last)
    for j in range(last):
        far_copy(j).wait_recv()
        total = total + far_in[j].astype(F32)
    gq[...] = total[0]
    gk[...] = total[1]
    gv[...] = total[2]
    for a, out in enumerate((go, gu, gd)):
        for k in range(1, far):
            far2_copy(a, k).wait_recv()
        total = near_sum2[a][top].astype(F32)
        for k in range(far - 1):
            total = total + far_in2[a][k].astype(F32)
        out[...] = total
    for copy in cfar:
        copy.wait_recv()
    total = cnear_sum[top].astype(F32)
    for k in range(far - 1):
        total = total + cfar_in[k].astype(F32)
    gc[...] = total
    for a in range(3):
        core2_copy(a).wait_send()
        for k in range(1, near):
            near2_copy(a, k).wait_send()
        for k in range(1, far):
            far2_copy(a, k).wait_send()
    for j in range(pairs):
        core_copy(j).wait_send()
        for k in range(1, near):
            near_copy(j, k).wait_send()
        if j < last:
            far_copy(j).wait_send()
    ccore.wait_send()
    for copy in cnear + cfar:
        copy.wait_send()
    for i in range(frame_count // tb):
        layer_copy(i).wait()
    grad_copy.wait()


def both_back(n, lengths, middle, gout, mixed, big, x, nb, qkv, raised, part, weights, table, bup):
    far, near = levels_of(n)
    frame_count, width = x.shape
    share = width // n
    pairs = HEADS // 2
    blocks = [p.shape[3:] for p in big]
    row_block = jax.ShapeDtypeStruct((share, width), F32)
    low = jax.ShapeDtypeStruct((frame_count, width), BF)
    low_rows = pltpu.VMEM((frame_count, width), BF)
    pair_rows = pltpu.VMEM((2, frame_count, 128), BF)
    dma = pltpu.SemaphoreType.DMA
    tb, ub = 384, raised.shape[3]
    return pl.pallas_call(
        functools.partial(both_back_kernel, n, tb, ub, 512),
        out_shape=[low, low, row_block, row_block, row_block]
        + [jax.ShapeDtypeStruct(b, F32) for b in blocks]
        + [jax.ShapeDtypeStruct((share, 128), F32)],
        in_specs=[SMEM_SPEC] + [HBM_SPEC] * 15 + [VMEM_SPEC] * 3,
        out_specs=[HBM_SPEC] * 2 + [VMEM_SPEC] * 7,
        scratch_shapes=[
            pltpu.VMEM((8, frame_count, 512), BF),
            low_rows,
            low_rows,
            low_rows,
            pltpu.VMEM((frame_count, width), F32),
            low_rows,
            pltpu.VMEM((frame_count, HEADS * 128), BF),
            low_rows,
        ]
        + [pltpu.VMEM(p.shape, BF) for p in big]
        + [
            pltpu.VMEM((pairs, 3) + weights[0].shape[1:], BF),
            pltpu.VMEM((tb, width), BF),
            pair_rows,
            pair_rows,
            pair_rows,
            pltpu.VMEM((64, frame_count), F32),
            pltpu.VMEM((pairs, 3, 128, frame_count), BF),
            pltpu.VMEM((8, width), F32),
            pltpu.VMEM((8, 4 * width), F32),
            pltpu.VMEM((width, 128), F32),
            pltpu.VMEM((pairs, 3, near, 2, share, width), BF),
            pltpu.VMEM((pairs, 3, near, share, width), BF),
            pltpu.VMEM((pairs, near, 3, share, width), BF),
            pltpu.VMEM((pairs, near - 1, 3, share, width), BF),
            pltpu.VMEM((pairs, 3, share, width), BF),
            pltpu.VMEM((pairs - 1, 3, share, width), BF),
        ]
        + [pltpu.VMEM((far, near) + b, BF) for b in blocks]
        + [pltpu.VMEM((near - 1, far) + b, BF) for b in blocks]
        + [pltpu.VMEM((far,) + b, BF) for b in blocks]
        + [pltpu.VMEM((far - 1,) + b, BF) for b in blocks]
        + [
            pltpu.VMEM((far, near, 2, share, 128), BF),
            pltpu.VMEM((far, near, share, 128), BF),
            pltpu.VMEM((near, far, share, 128), BF),
            pltpu.VMEM((near - 1, far, share, 128), BF),
            pltpu.VMEM((far, share, 128), BF),
            pltpu.VMEM((far - 1, share, 128), BF),
            dma((frame_count // tb, 4)),
            dma((3,)),
            dma((2, 3)),
            dma((3,)),
            dma((2, frame_count // ub)),
            dma((3,)),
            dma((pairs,)),
            dma((pairs,)),
            dma((pairs, near - 1)),
            dma((pairs, near - 1)),
            dma((pairs,)),
            dma((pairs,)),
            dma((3,)),
            dma((3,)),
            dma((3, near - 1)),
            dma((3, near - 1)),
            dma((3, far - 1)),
            dma((3, far - 1)),
            dma,
            dma,
            dma((near - 1,)),
            dma((near - 1,)),
            dma((far - 1,)),
            dma((far - 1,)),
        ],
        compiler_params=pltpu.CompilerParams(
            collective_id=3, has_side_effects=True, vmem_limit_bytes=67043328
        ),
        name="both_back",
    )(lengths, middle, gout, mixed, *big, x, nb, *qkv, raised, *weights, part, table, bup)


def hand_out_kernel(pieces, *refs):
    rows_in, ins, rows_out, outs = refs[:2], refs[2:9], refs[9:11], refs[11:26]
    rows_held, held, lanes = refs[26:28], refs[28:34], refs[34]
    read_sem, write_sem, in_sem, out_sem = refs[35:]
    size = rows_held[0].shape[0] // pieces
    reads, writes = [], []
    for j in range(pieces):
        for b in range(2):
            r = pl.ds(j * size, size)
            reads.append(
                pltpu.make_async_copy(rows_in[b].at[r], rows_held[b].at[r], read_sem.at[b, j])
            )
            writes.append(
                pltpu.make_async_copy(rows_held[b].at[r], rows_out[b].at[r], write_sem.at[b, j])
            )
    small_in = [pltpu.make_async_copy(ins[a], held[a], in_sem.at[a]) for a in range(6)]
    small_in.append(pltpu.make_async_copy(ins[6], lanes, in_sem.at[6]))
    small_out = [pltpu.make_async_copy(held[a], outs[a], out_sem.at[a]) for a in range(6)]
    for copy in small_in + reads:
        copy.start()
    for read, write in zip(reads, writes):
        read.wait()
        write.start()
    for a in range(6):
        small_in[a].wait()
        small_out[a].start()
    small_in[6].wait()
    turned = lanes[...].T
    for v in range(8):
        outs[6 + v][...] = turned[v : v + 1, :]
    share = turned.shape[1]
    for k in range(4):
        outs[14][:, share * k : share * k + share] = turned[8 + k : 9 + k, :]
    for copy in writes + small_out:
        copy.wait()


def hand_out(large, totals):
    share = totals[0].shape[0]
    line = jax.ShapeDtypeStruct((1, share), F32)
    dma = pltpu.SemaphoreType.DMA
    pieces = 4
    return pl.pallas_call(
        functools.partial(hand_out_kernel, pieces),
        out_shape=[jax.ShapeDtypeStruct(a.shape, a.dtype) for a in large]
        + [jax.ShapeDtypeStruct(t.shape, F32) for t in totals[:6]]
        + [line] * 8
        + [jax.ShapeDtypeStruct((1, 4 * share), F32)],
        in_specs=[HBM_SPEC] * 9,
        out_specs=[HBM_SPEC] * 8 + [VMEM_SPEC] * 9,
        scratch_shapes=[pltpu.VMEM(a.shape, a.dtype) for a in large]
        + [pltpu.VMEM(t.shape, F32) for t in totals]
        + [dma((2, pieces)), dma((2, pieces)), dma((7,)), dma((6,))],
        compiler_params=pltpu.CompilerParams(vmem_limit_bytes=60 << 20),
        name="hand_out",
    )(*large, *totals)


def per_device_fused(n, frames, lengths, vectors, up_bias, weights, grad_out):
    width = frames.shape[2]
    x = frames[0]
    got = gather_attend(n, lengths, x, tuple(w.T for w in weights), vectors + (up_bias,))
    table, bup, qq, kk, vv, raised, part, nb, mixed, middle = got[6:]
    sums = both_back(
        n,
        lengths,
        middle,
        grad_out[0],
        mixed,
        got[3:6],
        x,
        nb,
        (qq, kk, vv),
        raised,
        part,
        got[:3],
        table,
        bup,
    )
    layer_out, grad_x, *outs = hand_out(sums[:2], sums[2:])
    gq, gk, gv, go, gu, gd = (g.T for g in outs[:6])
    line = [v.reshape(-1) for v in outs[6:14]]
    return (
        layer_out[None],
        grad_x[None],
        line[0],
        line[1],
        gq,
        line[2],
        gk,
        gv,
        line[3],
        go,
        line[4],
        line[5],
        line[6],
        gu,
        outs[14].reshape(-1),
        gd,
        line[7],
    )


def per_device(
    n,
    frames,
    lengths,
    attn_gain,
    attn_shift,
    query_weight,
    query_bias,
    key_weight,
    value_weight,
    value_bias,
    out_weight,
    out_bias,
    mlp_gain,
    mlp_shift,
    up_weight,
    up_bias,
    down_weight,
    down_bias,
    grad_out,
):
    slots, frame_count, width = frames.shape
    assert slots == 1
    share = width // n
    vectors = (
        attn_gain,
        attn_shift,
        query_bias,
        value_bias,
        out_bias,
        mlp_gain,
        mlp_shift,
        down_bias,
    )
    far, near = levels_of(n)
    if share % 16 == 0 and far == HEADS // 2:
        return per_device_fused(
            n,
            frames,
            lengths,
            vectors,
            up_bias,
            (query_weight, key_weight, value_weight, out_weight, up_weight, down_weight),
            grad_out,
        )
    packed = jnp.concatenate(
        [jnp.stack(vectors, axis=1), up_bias.reshape(share, 4), jnp.zeros((share, 116), BF)], axis=1
    )
    shards = (
        query_weight.T,
        key_weight.T,
        value_weight.T,
        out_weight.T,
        up_weight.T,
        down_weight.T,
        packed,
    )
    full = gather_all(n, shards)
    wq, wk, wv, wo, wup, wdn, vec = (
        f.reshape(n * f.shape[3], f.shape[4]) for f in full
    )
    bup = vec[:, 8:12].reshape(1, 4 * width)
    x = frames[0]
    nb, qaug, kk, vv, mixed, middle, kaug = attend(lengths, x, wq, wk, wv, wo, vec)
    layer_out, gmid, dmixed, dwo, dwup, dwdn, sums_two, sum_up = feed(
        lengths, middle, grad_out[0], mixed, wup, wdn, wo, vec, bup
    )
    grad_x, dwq, dwk, dwv, sums_one = attend_back(
        x, gmid, nb, qaug, kk, vv, mixed, dmixed, kaug, wq, wk, wv, vec
    )
    columns = jnp.concatenate(
        [
            sums_one[:4].T,
            sums_two[:4].T,
            sum_up[0].reshape(width, 4),
            jnp.zeros((width, 116), F32),
        ],
        axis=1,
    ).astype(BF)

    def split(g):
        return g.reshape(far, near, 2, g.shape[0] // n, g.shape[1])

    gq, gk, gv, go, gu, gd, gc = scatter_all(
        n, tuple(split(g) for g in (dwq, dwk, dwv, dwo, dwup, dwdn, columns))
    )
    return (
        layer_out[None],
        grad_x[None],
        gc[:, 0],
        gc[:, 1],
        gq.T,
        gc[:, 2],
        gk.T,
        gv.T,
        gc[:, 3],
        go.T,
        gc[:, 4],
        gc[:, 5],
        gc[:, 6],
        gu.T,
        gc[:, 8:12].reshape(4 * share),
        gd.T,
        gc[:, 7],
    )


def solution(mesh):
    row, col, vector = P("dp", None, None), P(None, "dp"), P("dp")
    return jax.shard_map(
        functools.partial(per_device, mesh.shape["dp"]),
        mesh=mesh,
        in_specs=(
            row,
            P("dp", None),
            vector,
            vector,
            col,
            vector,
            col,
            col,
            vector,
            col,
            vector,
            vector,
            vector,
            col,
            vector,
            col,
            vector,
            row,
        ),
        out_specs=(
            row,
            row,
            vector,
            vector,
            col,
            vector,
            col,
            col,
            vector,
            col,
            vector,
            vector,
            vector,
            col,
            vector,
            col,
            vector,
        ),
        check_vma=False,
    )
```
